32 devices in a mesh: event: 2 (over y), mesh: 16 (over z, x, core).
Axes of the slice: x: 2, y: 2, z: 4, core: 2. Of those that a mesh axis runs over, the one named last changes fastest.
Arguments:
- forward_before: float32 [2, 3, 128, 8, 128], P('event', None, 'mesh'), may hold values from -3 to 3
- forward_now: float32 [2, 3, 128, 8, 128], P('event', None, 'mesh'), may hold values from -3 to 3
- adjoint_after: float32 [2, 3, 128, 8, 128], P('event', None, 'mesh'), may hold values from -3 to 3
- adjoint_now: float32 [2, 3, 128, 8, 128], P('event', None, 'mesh'), may hold values from -3 to 3
- mass_density: float32 [125, 2048], P(None, 'mesh'), may hold values from 0.8 to 1.5
- lame_lambda: float32 [125, 2048], P(None, 'mesh'), may hold values from 0.3 to 1
- lame_mu: float32 [125, 2048], P(None, 'mesh'), may hold values from 0.3 to 1
- source_element: int32 [2], P('event'), may hold values from 0 to 2047
- source_offset: int32 [2, 3], P('event'), may hold values from 0 to 4
- source_force: float32 [2, 3, 3], P('event'), may hold values from -120 to 120
- receiver_element: int32 [2, 32], P('event'), may hold values from 0 to 2047
- receiver_offset: int32 [2, 32, 3], P('event'), may hold values from 0 to 4
- receiver_data: float32 [2, 3, 32, 3], P('event'), may hold values from -3 to 3
Outputs:
- forward_final: float32 [2, 3, 128, 8, 128], P('event', None, 'mesh')
- adjoint_final: float32 [2, 3, 128, 8, 128], P('event', None, 'mesh')
- kernels: float32 [2, 125, 2048], P(None, None, ('mesh', 'event'))
The draws below stay inside these ranges and needn't reach their ends.
Inputs may be any that keep to these rules, and one draw needn't show every extreme that they name: `source_element`: element e lies at depth layer e // 64, row (e // 32) % 2, column e % 32. `source_offset`: offsets along depth, row, column; a point on the fixed bottom plane takes no force. `receiver_element`: element e lies at depth layer e // 64, row (e // 32) % 2, column e % 32; receivers may share points. `receiver_offset`: offsets along depth, row, column; a receiver on the fixed bottom plane records zero and takes no force.
All inputs are finite; a program needn't handle non-finite values.
Results may differ from the reference program's by a relative error of at most 0.0003.
Values sent between devices are 32-bit elements; how exact they have to be, the bound alone decides.
A program may use at most 192 MiB of HBM per device.

```python
import math
import jax
import jax.numpy as jnp
import numpy as np
from jax import lax

EX = 32
EY = 2
EZ = 2
STEPS = 3
NREC = 32
NX = 128
NY = 8
NZ = 128
NEL = 2048
N_EVENT = 2
N_MESH = 16


def set_ends(values, rng, least, top_value):
    dims = values.shape
    spot = [jax.random.randint(jax.random.fold_in(rng, axis), (), 0, dims[axis]) for axis in range(len(dims))]
    values = values.at[tuple(spot)].set(least)
    longest = dims.index(max(dims))
    spot[longest] = (spot[longest] + 1) % dims[longest]
    return values.at[tuple(spot)].set(top_value)


def levels(rng, dims, cuts, least, top_value):
    loudness, own = 1.0, jax.random.fold_in(rng, 6)
    for position, blocks in cuts:
        draws = jnp.exp(jax.random.uniform(jax.random.fold_in(own, position), (blocks,), jnp.float32, least / len(cuts), top_value / len(cuts)))
        loudness = loudness * jnp.repeat(draws, dims[position] // blocks).reshape([-1 if axis == position else 1 for axis in range(len(dims))])
    return loudness


def normal_values(stream_key, shape, scale, bound, shards=(), held_as=jnp.bfloat16):
    loudness = levels(stream_key, shape, shards, -0.22, 0.18) if shards else 1.0
    result = jax.random.normal(stream_key, shape, jnp.float32) * scale * loudness
    return jnp.minimum(jnp.maximum(result, -bound), bound).astype(held_as)


def setup_inputs(seed: int = 0) -> dict:
    arg_keys = jax.random.split(jax.random.key(seed), 14)
    return {
        "forward_before": normal_values(arg_keys[0], (N_EVENT, 3, NZ, NY, NX), 0.5, 3.0, ((0, 2), (2, 16)), jnp.float32),
        "forward_now": normal_values(arg_keys[1], (N_EVENT, 3, NZ, NY, NX), 0.5, 3.0, ((0, 2), (2, 16)), jnp.float32),
        "adjoint_after": normal_values(arg_keys[2], (N_EVENT, 3, NZ, NY, NX), 0.5, 3.0, ((0, 2), (2, 16)), jnp.float32),
        "adjoint_now": normal_values(arg_keys[3], (N_EVENT, 3, NZ, NY, NX), 0.5, 3.0, ((0, 2), (2, 16)), jnp.float32),
        "mass_density": jnp.clip(jnp.exp(math.log(1.5) - 0.62860864 * jax.random.uniform(arg_keys[4], (125, NEL), jnp.float32) ** levels(arg_keys[4], (125, NEL), ((1, 16),), -0.2, 0.2)), 0.8, 1.5),
        "lame_lambda": jnp.clip(jnp.exp(math.log(1.0) - 1.2039728 * jax.random.uniform(arg_keys[5], (125, NEL), jnp.float32) ** levels(arg_keys[5], (125, NEL), ((1, 16),), -0.2, 0.2)), 0.3, 1.0),
        "lame_mu": jnp.clip(jnp.exp(math.log(1.0) - 1.2039728 * jax.random.uniform(arg_keys[6], (125, NEL), jnp.float32) ** levels(arg_keys[6], (125, NEL), ((1, 16),), -0.2, 0.2)), 0.3, 1.0),
        "source_element": jax.random.randint(arg_keys[7], (N_EVENT,), 0, NEL).astype(jnp.int32),
        "source_offset": set_ends(jax.random.randint(arg_keys[8], (N_EVENT, 3), 0, 5), jax.random.fold_in(arg_keys[8], 1), 0, 4).astype(jnp.int32),
        "source_force": normal_values(arg_keys[9], (N_EVENT, STEPS, 3), 20.0, 120.0, ((0, 2),), jnp.float32),
        "receiver_element": set_ends(jax.random.randint(arg_keys[10], (N_EVENT, NREC), 0, NEL), jax.random.fold_in(arg_keys[10], 1), 0, NEL - 1).astype(jnp.int32),
        "receiver_offset": set_ends(jax.random.randint(arg_keys[11], (N_EVENT, NREC, 3), 0, 5), jax.random.fold_in(arg_keys[11], 1), 0, 4).astype(jnp.int32),
        "receiver_data": normal_values(arg_keys[12], (N_EVENT, STEPS, NREC, 3), 0.5, 3.0, ((0, 2),), jnp.float32),
    }


time_step = 0.04
adjoint_gain = 25.0

def numpy_tables():
    gll_points = np.array([-1.0, -math.sqrt(3.0 / 7.0), 0.0, math.sqrt(3.0 / 7.0), 1.0])
    legendre = (35.0 * gll_points ** 4 - 30.0 * gll_points ** 2 + 3.0) / 8.0
    deriv_table = np.zeros((5, 5))
    for row_q in range(5):
        for col_k in range(5):
            if row_q != col_k:
                deriv_table[row_q, col_k] = legendre[row_q] / (legendre[col_k] * (gll_points[row_q] - gll_points[col_k]))
    deriv_table[0, 0] = -5.0
    deriv_table[4, 4] = 5.0
    gll_weights = np.array([0.1, 49.0 / 90.0, 32.0 / 45.0, 49.0 / 90.0, 0.1])
    cube_weights = gll_weights[:, None, None] * gll_weights[None, :, None] * gll_weights[None, None, :]
    return (deriv_table, cube_weights)

def gll_tables():
    deriv_table, cube_weights = numpy_tables()
    return (jnp.asarray(deriv_table, jnp.float32), jnp.asarray(cube_weights.reshape(5, 5, 5, 1), jnp.float32))

def five_point(values, axis_pos, flipped):
    deriv_np = numpy_tables()[0]
    slices = [lax.index_in_dim(values, k_pos, axis_pos, keepdims=True) for k_pos in range(5)]
    outputs = []
    for p_pos in range(5):
        total = None
        for k_pos in range(5):
            coef = float(deriv_np[k_pos, p_pos] if flipped else deriv_np[p_pos, k_pos])
            if coef == 0.0:
                continue
            term = coef * slices[k_pos]
            total = term if total is None else total + term
        outputs.append(total)
    return jnp.concatenate(outputs, axis=axis_pos)

def unfold_cycle(wave_field, axis_pos):
    shape_in = wave_field.shape
    blocks = shape_in[axis_pos] // 4
    blocked = wave_field.reshape(shape_in[:axis_pos] + (blocks, 4) + shape_in[axis_pos + 1:])
    following = jnp.roll(lax.slice_in_dim(blocked, 0, 1, axis=axis_pos + 1), -1, axis=axis_pos)
    return jnp.concatenate([blocked, following], axis=axis_pos + 1)

def fold_cycle(blocked, axis_pos):
    leading = lax.slice_in_dim(blocked, 0, 1, axis=axis_pos + 1) + jnp.roll(lax.slice_in_dim(blocked, 4, 5, axis=axis_pos + 1), 1, axis=axis_pos)
    merged = jnp.concatenate([leading, lax.slice_in_dim(blocked, 1, 4, axis=axis_pos + 1)], axis=axis_pos + 1)
    shape_mid = merged.shape
    return merged.reshape(shape_mid[:axis_pos] + (shape_mid[axis_pos] * 4,) + shape_mid[axis_pos + 2:])

def unfold_depth(wave_field):
    blocks = (wave_field.shape[1] - 1) // 4
    lower_part = wave_field[:, :4 * blocks].reshape((wave_field.shape[0], blocks, 4) + wave_field.shape[2:])
    upper_part = wave_field[:, 4::4][:, :, None]
    return jnp.concatenate([lower_part, upper_part], axis=2)

def fold_depth(blocked):
    upper_part = blocked[:, :, 4]
    carried = jnp.concatenate([jnp.zeros_like(upper_part[:, :1]), upper_part[:, :-1]], axis=1)
    leading = blocked[:, :, 0] + carried
    merged = jnp.concatenate([leading[:, :, None], blocked[:, :, 1:4]], axis=2)
    plane_vals = merged.reshape((blocked.shape[0], blocked.shape[1] * 4) + blocked.shape[3:])
    return jnp.concatenate([plane_vals, upper_part[:, -1:]], axis=1)

def to_local(extended):
    spread = unfold_depth(unfold_cycle(unfold_cycle(extended, 3), 2))
    channels = spread.shape[0]
    element_total = spread.shape[1] * spread.shape[3] * spread.shape[5]
    return spread.transpose(0, 2, 4, 6, 1, 3, 5).reshape(channels, 5, 5, 5, element_total)

def from_local(local_vals, depth_count, rows_y, cols_x):
    channels = local_vals.shape[0]
    blocked = local_vals.reshape(channels, 5, 5, 5, depth_count, rows_y, cols_x).transpose(0, 4, 1, 5, 2, 6, 3)
    return fold_cycle(fold_cycle(fold_depth(blocked), 2), 3)

def gradients(local_vals, deriv_table):
    along_z = five_point(local_vals, 1, False)
    along_y = five_point(local_vals, 2, False)
    along_x = five_point(local_vals, 3, False)
    return (along_x, along_y, along_z)

def stress_columns(grad_table, lam_local, mu_local):
    diverg = grad_table[0][0] + grad_table[1][1] + grad_table[2][2]
    columns = []
    for dir_j in range(3):
        components = []
        for comp_i in range(3):
            entry_value = mu_local * (grad_table[dir_j][comp_i] + grad_table[comp_i][dir_j])
            if comp_i == dir_j:
                entry_value = entry_value + lam_local * diverg
            components.append(entry_value)
        columns.append(jnp.stack(components))
    return columns

def internal_force(columns, deriv_table, cube_weights):
    force_x = five_point(columns[0] * cube_weights, 3, True)
    force_y = five_point(columns[1] * cube_weights, 2, True)
    force_z = five_point(columns[2] * cube_weights, 1, True)
    return force_x + force_y + force_z

def kernel_terms(grads_adj, grads_fwd, lam_local, mu_local):
    div_adj = grads_adj[0][0] + grads_adj[1][1] + grads_adj[2][2]
    div_fwd = grads_fwd[0][0] + grads_fwd[1][1] + grads_fwd[2][2]
    contraction = jnp.zeros_like(div_adj)
    for dir_j in range(3):
        for comp_i in range(3):
            strain_adj = 0.5 * (grads_adj[dir_j][comp_i] + grads_adj[comp_i][dir_j])
            strain_fwd = 0.5 * (grads_fwd[dir_j][comp_i] + grads_fwd[comp_i][dir_j])
            contraction = contraction + strain_adj * strain_fwd
    lam_term = -lam_local * div_adj * div_fwd
    mu_term = -2.0 * mu_local * contraction
    return jnp.stack([lam_term, mu_term]).reshape(2, 125, div_adj.shape[-1])

def point_index(element, offset, plane_start, planes, elems_y, elems_x):
    row_span = 4 * elems_y
    col_span = 4 * elems_x
    z_local = 4 * (element // (elems_y * elems_x)) + offset[..., 0] - plane_start
    y_pos = (4 * (element // elems_x % elems_y) + offset[..., 1]) % row_span
    x_pos = (4 * (element % elems_x) + offset[..., 2]) % col_span
    valid = (z_local >= 0) & (z_local < planes)
    flat_pos = (z_local * row_span + y_pos) * col_span + x_pos
    return jnp.where(valid, flat_pos, planes * row_span * col_span).astype(jnp.int32)

def evolve(previous, current, after, present, src_point, src_force, rec_points, rec_data, inverse_mass, lam_local, mu_local, extend_fn, assemble_fn, reduce_fn):
    deriv_table, cube_weights = gll_tables()
    point_total = current[0].size
    step_total = src_force.shape[0]

    def advance(ext_field, older_field, load_field):
        local_vals = to_local(ext_field)
        grad_parts = gradients(local_vals, deriv_table)
        force = assemble_fn(internal_force(stress_columns(grad_parts, lam_local, mu_local), deriv_table, cube_weights))
        wave_field = ext_field[:, :-1]
        return (2.0 * wave_field - older_field + time_step ** 2 * inverse_mass * (load_field - force), grad_parts)
    ext_now = extend_fn(current)
    stored = []
    residuals = []
    for moment in range(step_total):
        load_field = jnp.zeros((3, point_total), current.dtype).at[:, src_point].add(src_force[moment], mode='drop').reshape(current.shape)
        following, unused_grads = advance(ext_now, previous, load_field)
        record = jnp.take(following.reshape(3, point_total), rec_points, axis=1, mode='fill', fill_value=0.0)
        residuals.append(record.T - rec_data[moment])
        previous, current = (current, following)
        ext_now = extend_fn(current)
        stored.append(ext_now)
    kernel = None
    ext_adj = extend_fn(present)
    older_field = after
    for moment in reversed(range(step_total)):
        load_field = jnp.zeros((3, point_total), present.dtype).at[:, rec_points].add(adjoint_gain * residuals[moment].T, mode='drop').reshape(present.shape)
        following, grads_adj = advance(ext_adj, older_field, load_field)
        grads_fwd = gradients(to_local(stored[moment]), deriv_table)
        kernel_term = reduce_fn(time_step * kernel_terms(grads_adj, grads_fwd, lam_local, mu_local))
        kernel = kernel_term if kernel is None else kernel + kernel_term
        older_field = present
        present = following
        if moment > 0:
            ext_adj = extend_fn(present)
    return (current, present, kernel)

def reference(forward_before, forward_now, adjoint_after, adjoint_now, mass_density, lame_lambda, lame_mu, source_element, source_offset, source_force, receiver_element, receiver_offset, receiver_data):
    deriv_table, cube_weights = gll_tables()
    planes = 4 * EZ * N_MESH
    elem_count = EX * EY * EZ * N_MESH
    lam_local = lame_lambda.reshape(5, 5, 5, elem_count)
    mu_local = lame_mu.reshape(5, 5, 5, elem_count)

    def extend(wave_field):
        return jnp.concatenate([wave_field, jnp.zeros_like(wave_field[:, :1])], axis=1)

    def assemble(local_vals):
        return from_local(local_vals, planes // 4, EY, EX)[:, :-1]

    def keep_term(kernel_term):
        return kernel_term
    inverse_mass = 1.0 / assemble((cube_weights * mass_density.reshape(5, 5, 5, elem_count))[None])

    def one_event(kernel_sum, event_inputs):
        before_one, now_one, after_one, adj_one, src_elem_one, src_off_one, force_one, rec_elem_one, rec_off_one, data_one = event_inputs
        src_point = point_index(src_elem_one, src_off_one, 0, planes, EY, EX)
        rec_points = point_index(rec_elem_one, rec_off_one, 0, planes, EY, EX)
        final_forward, final_adjoint, kernel = evolve(before_one, now_one, after_one, adj_one, src_point, force_one, rec_points, data_one, inverse_mass, lam_local, mu_local, extend, assemble, keep_term)
        return (kernel_sum + kernel, (final_forward, final_adjoint))
    start_sum = jnp.zeros((2, 125, elem_count), jnp.float32)
    kernel_sum, finals = lax.scan(one_event, start_sum, (forward_before, forward_now, adjoint_after, adjoint_now, source_element, source_offset, source_force, receiver_element, receiver_offset, receiver_data))
    return (finals[0], finals[1], kernel_sum)
```

```python
import functools
import math

import jax
import jax.numpy as jnp
import numpy as np
from jax import lax
from jax.experimental import pallas as pl
from jax.experimental.pallas import tpu as pltpu
from jax.sharding import PartitionSpec as P

time_step = 0.04
adjoint_gain = 25.0
LANES = 128


def numpy_tables():
    gll_points = np.array([-1.0, -math.sqrt(3.0 / 7.0), 0.0, math.sqrt(3.0 / 7.0), 1.0])
    legendre = (35.0 * gll_points**4 - 30.0 * gll_points**2 + 3.0) / 8.0
    deriv_table = np.zeros((5, 5))
    for row_q in range(5):
        for col_k in range(5):
            if row_q != col_k:
                deriv_table[row_q, col_k] = legendre[row_q] / (
                    legendre[col_k] * (gll_points[row_q] - gll_points[col_k])
                )
    deriv_table[0, 0] = -5.0
    deriv_table[4, 4] = 5.0
    gll_weights = np.array([0.1, 49.0 / 90.0, 32.0 / 45.0, 49.0 / 90.0, 0.1])
    return (deriv_table, gll_weights)


DERIV, WEIGHTS = numpy_tables()


def constants():
    spread = np.zeros((4, LANES, 4, 4, 32), np.float32)
    for j in range(4):
        for ex in range(32):
            for c in range(4):
                spread[j, 4 * ex + c, c, j, ex] = 1.0
    spread = spread.reshape(512, 512)
    rows = np.zeros((5, 5, 8, 125), np.float32)
    cube = np.zeros((5, 5, 8, LANES), np.float32)
    for a in range(5):
        for b in range(5):
            for c in range(5):
                rows[a, c, b, (a * 5 + b) * 5 + c] = 1.0
                cube[a, c, b, :] = WEIGHTS[a] * WEIGHTS[b] * WEIGHTS[c]
    rows = rows.reshape(200, 125)
    dy = np.zeros((2, 5, 8, LANES), np.float32)
    for k in range(5):
        for b in range(5):
            dy[0, k, b, :] = DERIV[b, k]
            dy[1, k, b, :] = DERIV[k, b]
    bf = jnp.bfloat16
    return (
        jnp.asarray(spread, bf),
        jnp.asarray(np.ascontiguousarray(spread.T), bf),
        jnp.asarray(rows, bf),
        jnp.asarray(cube),
        jnp.asarray(dy),
    )


def split3(value):
    high = value.astype(jnp.bfloat16)
    rest = value - high.astype(jnp.float32)
    middle = rest.astype(jnp.bfloat16)
    low = (rest - middle.astype(jnp.float32)).astype(jnp.bfloat16)
    return (high, middle, low)


def dot(left, right):
    return jnp.dot(left, right, preferred_element_type=jnp.float32)


def move_right(values, table):
    parts = split3(values)
    count = values.shape[0]
    stacked = jnp.concatenate(parts, axis=0)
    moved = dot(stacked, table)
    return moved[0:count] + moved[count : 2 * count] + moved[2 * count : 3 * count]


def move_left(table, values):
    high, middle, low = split3(values)
    return dot(table, high) + dot(table, middle) + dot(table, low)


def move_left_t(table, values):
    contract = (((0,), (0,)), ((), ()))
    return sum(
        lax.dot_general(table, part, contract, preferred_element_type=jnp.float32)
        for part in split3(values)
    )


def roll_lane(value, shift):
    return pltpu.roll(value, shift % LANES, value.ndim - 1)


def lane_iota(ndim):
    return lax.broadcasted_iota(jnp.int32, (1,) * (ndim - 1) + (LANES,), ndim - 1)


def sub_iota(ndim):
    return lax.broadcasted_iota(jnp.int32, (1,) * (ndim - 2) + (8, LANES), ndim - 2)


def pick(mask, first, second):
    return jnp.where(jnp.broadcast_to(mask, first.shape), first, second)


def from_left(value):
    at_edge = lane_iota(value.ndim) % 32 == 0
    return pick(at_edge, roll_lane(value, -31), roll_lane(value, 1))


def from_right(value):
    at_edge = lane_iota(value.ndim) % 32 == 31
    return pick(at_edge, roll_lane(value, 31), roll_lane(value, -1))


def roll_sub(value):
    return pltpu.roll(value, 4, value.ndim - 2)


def assemble_xy(value):
    first = value[:, 0:1] + from_left(value[:, 4:5])
    value = jnp.concatenate([first, value[:, 1:4], from_right(first)], axis=1)
    swapped = roll_sub(value)
    other = pick(
        lane_iota(4) % 64 < 32, roll_lane(swapped, -32), roll_lane(swapped, 32)
    )
    return value + pick(sub_iota(4) % 4 == 0, other, jnp.zeros_like(other))


EDGE = float(DERIV[0, 0])
HALF = 64


def mix(coefs, planes):
    total = None
    for coef, plane in zip(coefs, planes):
        if coef != 0.0:
            term = float(coef) * plane
            total = term if total is None else total + term
    return total


def along_x(value, flipped=False):
    table = DERIV.T if flipped else DERIV
    rows = [value[k] for k in range(5)]
    return jnp.stack([mix(table[c], rows) for c in range(5)], axis=0)


def mirror(value):
    return jnp.concatenate([value[0:2], -value[2:3]], axis=0)


def low_lanes(ndim):
    return lane_iota(ndim) < HALF


def swap_half(value):
    return roll_lane(value, HALF)


def unpack(from_above, from_below):
    low = low_lanes(from_above.ndim)
    return (
        pick(low, from_above, swap_half(from_below)),
        pick(low, swap_half(from_above), from_below),
    )


def pack(first, second):
    low = low_lanes(first.ndim)
    return (
        pick(low, first, swap_half(second)),
        pick(low, swap_half(first), second),
    )


def kernel(
    n_mesh,
    n_event,
    steps,
    now_hbm,
    before_hbm,
    adj_hbm,
    after_hbm,
    rho_hbm,
    lam_hbm,
    mu_hbm,
    rec_elem_hbm,
    rec_off_hbm,
    data_hbm,
    spread_hbm,
    gather_hbm,
    rows_hbm,
    cube_hbm,
    dy_hbm,
    elem_ref,
    off_ref,
    force_ref,
    final_f_ref,
    final_a_ref,
    out_ref,
    now_ref,
    before_ref,
    adj_ref,
    after_ref,
    rho_ref,
    lam_ref,
    mu_ref,
    rec_elem_ref,
    rec_off_ref,
    data_ref,
    spread_ref,
    gather_ref,
    rows_ref,
    cube_ref,
    dy_ref,
    s_in,
    fields,
    stress,
    force,
    load_ref,
    strains,
    astrains,
    ksum,
    clam,
    cmu,
    minv,
    ghost_mat,
    work,
    halo_s,
    halo_r,
    mat_us,
    mat_ur,
    mat_ds,
    mat_dr,
    up_s,
    up_r,
    down_s,
    down_r,
    ev_s,
    ev_r,
    s_up,
    r_up,
    s_down,
    r_down,
    s_ev,
    r_ev,
):
    me = lax.axis_index("mesh")
    event = lax.axis_index("event")
    has_up = me > 0
    has_down = me < n_mesh - 1

    barrier = pltpu.get_barrier_semaphore()

    @pl.when(has_up)
    def _():
        pl.semaphore_signal(barrier, inc=1, device_id={"mesh": me - 1})

    @pl.when(has_down)
    def _():
        pl.semaphore_signal(barrier, inc=1, device_id={"mesh": me + 1})

    for hop in range(1, n_event):
        pl.semaphore_signal(
            barrier, inc=1, device_id={"event": lax.rem(event + hop, n_event)}
        )

    loads = []
    pairs = (
        (rows_hbm, rows_ref),
        (lam_hbm, lam_ref),
        (mu_hbm, mu_ref),
        (rho_hbm, rho_ref),
        (cube_hbm, cube_ref),
        (now_hbm, now_ref),
        (before_hbm, before_ref),
        (adj_hbm, adj_ref),
        (after_hbm, after_ref),
        (spread_hbm, spread_ref),
        (dy_hbm, dy_ref),
        (rec_elem_hbm, rec_elem_ref),
        (rec_off_hbm, rec_off_ref),
        (data_hbm, data_ref),
        (gather_hbm, gather_ref),
    )
    for place, (source, target) in enumerate(pairs):
        load_copy = pltpu.make_async_copy(source, target, s_in.at[place])
        load_copy.start()
        loads.append(load_copy)

    def up_copy(source, target, slot):
        return pltpu.make_async_remote_copy(
            src_ref=source, dst_ref=target, send_sem=s_up.at[slot],
            recv_sem=r_up.at[slot], device_id={"mesh": me - 1},
        )

    def down_copy(source, target, slot):
        return pltpu.make_async_remote_copy(
            src_ref=source, dst_ref=target, send_sem=s_down.at[slot],
            recv_sem=r_down.at[slot], device_id={"mesh": me + 1},
        )

    n_face = 6
    mat_slot = n_face
    halo_slot = n_face + 1

    def start_both(up, down):
        @pl.when(has_up)
        def _():
            up.start()

        @pl.when(has_down)
        def _():
            down.start()

    def wait_both(up, down):
        @pl.when(has_down)
        def _():
            up.wait_recv()

        @pl.when(has_up)
        def _():
            down.wait_recv()

    @pl.when(jnp.logical_not(has_down))
    def _():
        halo_r[...] = jnp.zeros_like(halo_r)
        up_r[...] = jnp.zeros_like(up_r)
        mat_ur[...] = jnp.zeros_like(mat_ur)

    @pl.when(jnp.logical_not(has_up))
    def _():
        down_r[...] = jnp.zeros_like(down_r)
        mat_dr[...] = jnp.zeros_like(mat_dr)

    low4 = low_lanes(4)

    for place in range(5):
        loads[place].wait()
    materials = jnp.concatenate([lam_ref[...], mu_ref[...], rho_ref[...]], axis=1)
    moved = move_left(rows_ref[...], materials)
    cube = cube_ref[...]

    def modulus(which):
        value = moved[:, which * LANES : (which + 1) * LANES].reshape(5, 5, 8, LANES)
        turned = jnp.stack([value[4 - a] for a in range(5)], axis=0)
        return pick(low4, value, turned) * cube

    lam_value = modulus(0)
    mu_value = modulus(1)
    clam[...] = lam_value
    cmu[...] = mu_value
    mass = modulus(2)
    mass = [assemble_xy(mass[a : a + 1])[0] for a in range(5)]
    mass[4] = mass[4] + swap_half(mass[4])

    squares = [float(DERIV[q, 0]) ** 2 for q in range(5)]
    diag_mu = mix(squares[1:], [mu_value[q] for q in range(1, 5)])
    diag_lam = mix(squares[1:], [lam_value[q] for q in range(1, 5)])
    diag_lam = diag_lam + (diag_mu + diag_mu)
    listed = [mass[0][c] for c in range(4)]
    for value in (lam_value[0], mu_value[0], diag_mu, diag_lam):
        listed += [value[c] for c in range(5)]
    for pair in range(12):
        up, down = pack(listed[2 * pair], listed[2 * pair + 1])
        mat_us[pair] = up
        mat_ds[pair] = down

    inputs = (now_ref, before_ref, adj_ref, after_ref)
    for place in range(5, 9):
        loads[place].wait()
    for index, ref in enumerate(inputs):
        halo_s[index] = ref[0, :, 0]

    pl.semaphore_wait(
        barrier,
        jnp.where(has_up, 1, 0) + jnp.where(has_down, 1, 0) + (n_event - 1),
    )

    @pl.when(has_up)
    def _():
        up_copy(halo_s, halo_r, halo_slot).start()

    start_both(up_copy(mat_us, mat_ur, mat_slot), down_copy(mat_ds, mat_dr, mat_slot))

    for place in range(9, 14):
        loads[place].wait()

    def bring_in(index):
        ref = inputs[index]
        upper = ref[0, :, 0:5]
        lower = mirror(
            jnp.stack(
                [jnp.zeros((3, 8, LANES), jnp.float32)]
                + [ref[0, :, 8 - a] for a in range(1, 5)],
                axis=1,
            )
        )
        parts = []
        for layer in (upper, lower):
            for shifted in (layer, roll_sub(layer)):
                parts.append(shifted.reshape(120, LANES))
        moved = move_right(jnp.concatenate(parts, axis=1), spread_ref[...])
        for c in range(4):
            fields[index, :, :, c] = moved[:, c * LANES : (c + 1) * LANES].reshape(
                3, 5, 8, LANES
            )
        fields[index, :, :, 4] = from_right(
            moved[:, 0:LANES].reshape(3, 5, 8, LANES)
        )

    def bring_halos():
        @pl.when(has_down)
        def _():
            up_copy(halo_s, halo_r, halo_slot).wait_recv()

        planes = jnp.stack([halo_r[:, 0], halo_r[:, 1], -halo_r[:, 2]], axis=1)
        parts = [
            planes.reshape(96, LANES),
            roll_sub(planes).reshape(96, LANES),
        ]
        moved = move_right(
            jnp.concatenate(parts, axis=1), spread_ref[2 * LANES : 4 * LANES]
        )
        for c in range(5):
            part = moved[:, (c % 4) * LANES : (c % 4 + 1) * LANES]
            part = part.reshape(4, 3, 8, LANES)
            if c == 4:
                part = from_right(part)
            fields[:, :, 0, c] = fields[:, :, 0, c] + part

    def along_y(value, flipped=False):
        total = None
        for k in range(5):
            row = jnp.broadcast_to(value[..., k : k + 1, :], value.shape)
            term = dy_ref[1 if flipped else 0, k] * row
            total = term if total is None else total + term
        return total

    def send(slot, value):
        for pair in range(2):
            up, down = pack(value[:, 2 * pair], value[:, 2 * pair + 1])
            up_s[slot, :, pair] = up
            down_s[slot, :, pair] = down
        start_both(
            up_copy(up_s.at[slot], up_r.at[slot], slot),
            down_copy(down_s.at[slot], down_r.at[slot], slot),
        )

    def receive(slot):
        wait_both(
            up_copy(up_s.at[slot], up_r.at[slot], slot),
            down_copy(down_s.at[slot], down_r.at[slot], slot),
        )
        sides = []
        for pair in range(2):
            sides += unpack(down_r[slot, :, pair], up_r[slot, :, pair])
        sides.append(from_right(sides[0]))
        return mirror(jnp.stack(sides, axis=1))

    def along_z(index, comp, a, first=0):
        return mix(
            DERIV[a, first:], [fields[index, comp, k] for k in range(first, 5)]
        )

    def strain_at(index, a):
        u = [fields[index, comp, a] for comp in range(3)]
        gz = [along_z(index, comp, a) for comp in range(3)]
        return (
            along_x(u[0]),
            along_y(u[1]),
            gz[2],
            along_y(u[0]) + along_x(u[1]),
            gz[0] + along_x(u[2]),
            gz[1] + along_y(u[2]),
        )

    def inside_face_force(index):
        total = [None, None, None]
        for q in range(1, 5):
            u = [fields[index, comp, q] for comp in range(3)]
            gz = [along_z(index, comp, q, 1) for comp in range(3)]
            mu_q = cmu[q]
            div = along_x(u[0]) + along_y(u[1]) + gz[2]
            parts = (
                mu_q * (gz[0] + along_x(u[2])),
                mu_q * (gz[1] + along_y(u[2])),
                clam[q] * div + (mu_q + mu_q) * gz[2],
            )
            for comp in range(3):
                term = float(DERIV[q, 0]) * parts[comp]
                total[comp] = term if total[comp] is None else total[comp] + term
        gz = [along_z(index, comp, 0, 1) for comp in range(3)]
        mu_0 = cmu[0]
        side = clam[0] * gz[2]
        xz = mu_0 * gz[0]
        yz = mu_0 * gz[1]
        zz = side + (mu_0 + mu_0) * gz[2]
        work[0] = side
        work[1] = yz
        return assemble_xy(
            jnp.stack(
                [
                    total[0] + along_x(side, True) + EDGE * xz,
                    total[1] + along_y(work[0], True) + EDGE * yz,
                    total[2]
                    + along_x(xz, True)
                    + along_y(work[1], True)
                    + EDGE * zz,
                ],
                axis=0,
            )
        )

    def ghost_face_force(index):
        u = [fields[index, comp, 0] for comp in range(3)]
        gz = [-EDGE * value for value in u]
        lam_g, mu_g = ghost_mat[0], ghost_mat[1]
        xx = along_x(u[0])
        yy = along_y(u[1])
        zz = gz[2]
        side = lam_g * (xx + yy + zz)
        mu_two = mu_g + mu_g
        xx = side + mu_two * xx
        yy = side + mu_two * yy
        zz = side + mu_two * zz
        xy = mu_g * (along_y(u[0]) + along_x(u[1]))
        xz = mu_g * (gz[0] + along_x(u[2]))
        yz = mu_g * (gz[1] + along_y(u[2]))
        work[0] = xy
        work[1] = yy
        work[2] = yz
        return (
            along_x(xx, True)
            + along_y(work[0], True)
            - EDGE * xz
            + ghost_mat[2] * u[0],
            along_x(xy, True)
            + along_y(work[1], True)
            - EDGE * yz
            + ghost_mat[2] * u[1],
            along_x(xz, True)
            + along_y(work[2], True)
            - EDGE * zz
            + ghost_mat[3] * u[2],
        )

    def make_stress(index, keep_strain):
        for a in range(5):
            strain = strain_at(index, a)
            lam_div = clam[a] * (strain[0] + strain[1] + strain[2])
            mu_a = cmu[a]
            mu_two = mu_a + mu_a
            for i in range(3):
                stress[i, a] = lam_div + mu_two * strain[i]
                stress[3 + i, a] = mu_a * strain[3 + i]
            if keep_strain is not None:
                for i in range(6):
                    keep_strain[a, i] = strain[i]

    pairs_of = ((0, 3, 4), (3, 1, 5), (4, 5, 2))

    def plane_force(a, load, extra=None):
        values = []
        for comp in range(3):
            ix, iy, iz = pairs_of[comp]
            total = along_x(stress[ix, a], True) + along_y(stress[iy, a], True)
            total = total + mix(DERIV[:, a], [stress[iz, q] for q in range(5)])
            if extra is not None:
                total = total + extra[comp]
            if load is not None:
                total = total - load(comp, a)
            values.append(total)
        value = assemble_xy(jnp.stack(values, axis=0))
        return value + mirror(swap_half(value)) if a == 4 else value

    def advance(index, older, a, value):
        fields[older, :, a] = (
            2.0 * fields[index, :, a] - fields[older, :, a]
        ) - minv[a] * value

    def inside_planes(index, older, load):
        for a in range(1, 5):
            advance(index, older, a, plane_force(a, load))

    def closed_step(index, older, slot, load):
        inside_planes(index, older, load)
        value = plane_force(0, load, ghost_face_force(index))
        advance(index, older, 0, value + receive(slot))

    def open_step(index, older, slot, load):
        force[...] = plane_force(0, None)
        send(slot, force[...])
        inside_planes(index, older, load)
        send(slot + 1, inside_face_force(older))

    def close_face(index, older, slot, load):
        value = force[...]
        if load is not None:
            value = value - assemble_xy(
                jnp.stack([load(comp, 0) for comp in range(3)], axis=0)
            )
        advance(index, older, 0, value + receive(slot))

    bring_in(0)
    send(0, inside_face_force(0))
    bring_in(2)
    send(1, inside_face_force(2))
    bring_in(1)
    bring_in(3)

    nrec = rec_elem_ref.shape[1]
    local = rec_elem_ref[...] - LANES * me
    depth = rec_off_ref[0]
    in_slab = (local >= 0) & (local < LANES)
    over = (local >= -HALF) & (local < 0) & (depth == 4)
    under = (local >= LANES) & (local < LANES + HALF) & (depth == 0)
    rec_at = jnp.where(
        in_slab,
        local,
        jnp.where(over, local + HALF, jnp.where(under, local - HALF, -1)),
    )
    depth = jnp.where(
        in_slab, jnp.where(local < HALF, depth, 4 - depth), jnp.zeros_like(depth)
    )
    lane_t = lax.broadcasted_iota(jnp.int32, (LANES, nrec), 0) == rec_at
    lane_t = jnp.where(lane_t, 1.0, 0.0).astype(jnp.bfloat16)
    eye = jnp.where(
        lax.broadcasted_iota(jnp.int32, (nrec, nrec), 0)
        == lax.broadcasted_iota(jnp.int32, (nrec, nrec), 1),
        1.0,
        0.0,
    ).astype(jnp.bfloat16)
    turned = (((1,), (1,)), ((), ()))

    def turn(part):
        return lax.dot_general(eye, part, turned, preferred_element_type=jnp.float32)

    rec_lane = turn(lane_t)
    rec_lanes = (rec_lane, rec_lane, pick(low_lanes(2), rec_lane, -rec_lane))
    row = depth * 40 + rec_off_ref[2] * 8 + rec_off_ref[1]
    rows_lanes = lax.broadcasted_iota(jnp.int32, (200, nrec), 0) == row
    rows_lanes = jnp.where(rows_lanes, 1.0, 0.0).astype(jnp.bfloat16)
    rec_rows = turn(rows_lanes).astype(jnp.bfloat16)
    observed = jnp.concatenate(
        [data_ref[n, comp] for n in range(steps) for comp in range(3)], axis=0
    )
    observed = sum(turn(part) for part in split3(observed))

    src_local = elem_ref[0] - LANES * me
    src_depth = off_ref[0, 0]
    src_in = (src_local >= 0) & (src_local < LANES)
    src_over = (src_local >= -HALF) & (src_local < 0) & (src_depth == 4)
    src_under = (src_local >= LANES) & (src_local < LANES + HALF) & (src_depth == 0)
    src_lane = jnp.where(
        src_in,
        src_local,
        jnp.where(
            src_over, src_local + HALF, jnp.where(src_under, src_local - HALF, -1)
        ),
    )
    src_depth = jnp.where(
        src_in, jnp.where(src_local < HALF, src_depth, 4 - src_depth), 0
    )
    src_row = src_depth * 40 + off_ref[0, 2] * 8 + off_ref[0, 1]

    def source_load(moment):
        def load(comp, a):
            shape = (5, 8, LANES)
            here = (
                lax.broadcasted_iota(jnp.int32, shape, 0) * 8
                + lax.broadcasted_iota(jnp.int32, shape, 1)
                + a * 40
            ) == src_row
            lanes = lax.broadcasted_iota(jnp.int32, shape, 2)
            value = force_ref[moment, 0, comp]
            if comp == 2:
                value = jnp.where(src_lane < HALF, value, -value)
            return jnp.where(here & (lanes == src_lane), value, 0.0)

        return load

    def record(index, moment):
        values = jnp.concatenate(
            [fields[index, comp].reshape(200, LANES) for comp in range(3)], axis=1
        )
        at_rows = move_left(rec_rows, values)
        found = []
        for comp in range(3):
            seen = at_rows[:, comp * LANES : (comp + 1) * LANES] * rec_lanes[comp]
            found.append(
                jnp.sum(seen, axis=1, keepdims=True)
                - observed[:, 3 * moment + comp : 3 * moment + comp + 1]
            )
        return found

    def inject(residual):
        scaled = jnp.concatenate(
            [adjoint_gain * residual[comp] * rec_lanes[comp] for comp in range(3)],
            axis=1,
        )
        injected = sum(dot(rows_lanes, part) for part in split3(scaled))
        for comp in range(3):
            load_ref[comp] = injected[:, comp * LANES : (comp + 1) * LANES].reshape(
                5, 5, 8, LANES
            )

    def held_load(comp, a):
        return load_ref[comp, a]

    bring_halos()
    make_stress(0, None)

    wait_both(up_copy(mat_us, mat_ur, mat_slot), down_copy(mat_ds, mat_dr, mat_slot))
    listed = []
    for pair in range(12):
        listed += unpack(mat_dr[pair], mat_ur[pair])
    face_mass = listed[0:4]
    face_mass = jnp.stack(face_mass + [from_right(face_mass[0])], axis=0)
    mass[0] = mass[0] + face_mass
    for which in range(4):
        for c in range(5):
            ghost_mat[which, c] = listed[4 + 5 * which + c]
    for a in range(5):
        keep = sub_iota(3) < 5
        if a == 0:
            keep = keep & (low_lanes(3) | has_down)
        keep = jnp.broadcast_to(keep, mass[a].shape)
        safe = jnp.where(keep, mass[a], 1.0)
        minv[a] = jnp.where(keep, time_step**2 / safe, 0.0)

    closed_step(0, 1, 0, source_load(0))

    make_stress(1, strains.at[0])
    open_step(1, 0, 2, source_load(1))

    residuals = [record(1, 0)]
    make_stress(2, astrains.at[2])
    closed_step(2, 3, 1, None)

    close_face(1, 0, 2, source_load(1))

    make_stress(0, strains.at[1])
    closed_step(0, 1, 3, source_load(2))
    residuals.append(record(0, 1))
    residuals.append(record(1, 2))

    inject(residuals[2])
    for a in range(5):
        value = assemble_xy(load_ref[:, a])
        if a == 4:
            value = value + mirror(swap_half(value))
        fields[3, :, a] = fields[3, :, a] + minv[a] * value

    make_stress(3, astrains.at[1])
    inject(residuals[1])
    open_step(3, 2, 4, held_load)

    def put_out(index, ref):
        sides = []
        for c in range(4):
            upper = fields[index, :, 0:4, c]
            lower = mirror(
                jnp.stack([fields[index, :, 4 - i, c] for i in range(4)], axis=1)
            )
            sides.append(pick(low4, upper, lower).reshape(96, LANES))
        moved = move_right(jnp.concatenate(sides, axis=1), gather_ref[...])
        for ez in range(2):
            first = moved[:, 2 * ez * LANES : (2 * ez + 1) * LANES]
            second = moved[:, (2 * ez + 1) * LANES : (2 * ez + 2) * LANES]
            first = first.reshape(3, 4, 8, LANES)
            second = roll_sub(second.reshape(3, 4, 8, LANES))
            ref[0, :, 4 * ez : 4 * ez + 4] = pick(sub_iota(4) < 4, first, second)

    def add_kernels(adjoint, other_at, first):
        for a in range(5):
            strain = [adjoint[a, i] for i in range(6)]
            other = other_at(a)
            div_a = strain[0] + strain[1] + strain[2]
            div_f = other[0] + other[1] + other[2]
            diag = strain[0] * other[0] + strain[1] * other[1] + strain[2] * other[2]
            shear = strain[3] * other[3] + strain[4] * other[4] + strain[5] * other[5]
            lam_part = div_a * div_f
            mu_part = diag + 0.5 * shear
            if not first:
                lam_part = ksum[0, a] + lam_part
                mu_part = ksum[1, a] + mu_part
            ksum[0, a] = lam_part
            ksum[1, a] = mu_part

    def kept(which):
        return lambda a: [strains[which, a, i] for i in range(6)]

    add_kernels(astrains.at[2], lambda a: strain_at(1, a), True)
    add_kernels(astrains.at[1], kept(1), False)
    loads[14].wait()
    put_out(1, final_f_ref)

    close_face(3, 2, 4, held_load)

    width = LANES // n_event

    def event_copy(hop):
        target = lax.rem(event + hop, n_event)
        return pltpu.make_async_remote_copy(
            src_ref=ev_s.at[:, pl.ds(pl.multiple_of(width * target, width), width)],
            dst_ref=ev_r.at[hop - 1],
            send_sem=s_ev.at[hop - 1],
            recv_sem=r_ev.at[hop - 1],
            device_id={"event": target},
        )

    def send_kernels():
        scales = (-time_step, -2.0 * time_step)
        for which, modulus_ref in enumerate((lam_ref, mu_ref)):
            value = ksum[which]
            turned_back = jnp.stack([value[4 - a] for a in range(5)], axis=0)
            value = pick(low4, value, turned_back).reshape(200, LANES)
            natural = move_left_t(rows_ref[...], value)
            ev_s[which] = jnp.transpose(natural * (scales[which] * modulus_ref[...]))
        for hop in range(1, n_event):
            event_copy(hop).start()

    make_stress(2, astrains.at[0])
    add_kernels(astrains.at[0], kept(0), False)
    send_kernels()
    inject(residuals[0])
    closed_step(2, 3, 5, held_load)
    put_out(3, final_a_ref)

    mine = pl.ds(pl.multiple_of(width * event, width), width)
    total = ev_s[:, mine]
    for hop in range(1, n_event):
        event_copy(hop).wait_recv()
        total = total + ev_r[hop - 1]
    out_ref[...] = total

    @pl.when(has_up)
    def _():
        up_copy(halo_s, halo_r, halo_slot).wait_send()
        up_copy(mat_us, mat_ur, mat_slot).wait_send()
        for slot in range(n_face):
            up_copy(up_s.at[slot], up_r.at[slot], slot).wait_send()

    @pl.when(has_down)
    def _():
        down_copy(mat_ds, mat_dr, mat_slot).wait_send()
        for slot in range(n_face):
            down_copy(down_s.at[slot], down_r.at[slot], slot).wait_send()

    for hop in range(1, n_event):
        event_copy(hop).wait_send()


def on_device(
    n_mesh,
    n_event,
    forward_before,
    forward_now,
    adjoint_after,
    adjoint_now,
    mass_density,
    lame_lambda,
    lame_mu,
    source_element,
    source_offset,
    source_force,
    receiver_element,
    receiver_offset,
    receiver_data,
):
    assert forward_now.shape[1:] == (3, 8, 8, 128)
    assert lame_mu.shape == (125, 128)
    steps = source_force.shape[1]
    assert steps == 3
    field = forward_now.shape
    vmem = pl.BlockSpec(memory_space=pltpu.VMEM)
    hbm = pl.BlockSpec(memory_space=pltpu.HBM)
    smem = pl.BlockSpec(memory_space=pltpu.SMEM)
    f32 = jnp.float32
    elem = (5, 5, 8, LANES)
    faces = (6, 3, 2, 8, LANES)
    copied = (
        forward_now,
        forward_before,
        adjoint_now,
        adjoint_after,
        mass_density,
        lame_lambda,
        lame_mu,
        receiver_element,
        receiver_offset.transpose(2, 0, 1),
        receiver_data.transpose(1, 3, 0, 2),
    ) + constants()
    final_f, final_a, kernels = pl.pallas_call(
        functools.partial(kernel, n_mesh, n_event, steps),
        out_shape=(
            jax.ShapeDtypeStruct(field, f32),
            jax.ShapeDtypeStruct(field, f32),
            jax.ShapeDtypeStruct((2, LANES // n_event, 125), f32),
        ),
        in_specs=[hbm] * 15 + [smem] * 3,
        out_specs=(vmem, vmem, vmem),
        scratch_shapes=[pltpu.VMEM(value.shape, value.dtype) for value in copied]
        + [
            pltpu.SemaphoreType.DMA((len(copied),)),
            pltpu.VMEM((4, 3) + elem, f32),
            pltpu.VMEM((6,) + elem, f32),
            pltpu.VMEM((3,) + elem[1:], f32),
            pltpu.VMEM((3,) + elem, f32),
            pltpu.VMEM((2, 5, 6, 5, 8, LANES), f32),
            pltpu.VMEM((3, 5, 6, 5, 8, LANES), f32),
            pltpu.VMEM((2,) + elem, f32),
            pltpu.VMEM(elem, f32),
            pltpu.VMEM(elem, f32),
            pltpu.VMEM(elem, f32),
            pltpu.VMEM((4,) + elem[1:], f32),
            pltpu.VMEM((3,) + elem[1:], f32),
            pltpu.VMEM((4, 3, 8, LANES), f32),
            pltpu.VMEM((4, 3, 8, LANES), f32),
            pltpu.VMEM((12, 8, LANES), f32),
            pltpu.VMEM((12, 8, LANES), f32),
            pltpu.VMEM((12, 8, LANES), f32),
            pltpu.VMEM((12, 8, LANES), f32),
            pltpu.VMEM(faces, f32),
            pltpu.VMEM(faces, f32),
            pltpu.VMEM(faces, f32),
            pltpu.VMEM(faces, f32),
            pltpu.VMEM((2, LANES, 125), f32),
            pltpu.VMEM((max(1, n_event - 1), 2, LANES // n_event, 125), f32),
            pltpu.SemaphoreType.DMA((8,)),
            pltpu.SemaphoreType.DMA((8,)),
            pltpu.SemaphoreType.DMA((7,)),
            pltpu.SemaphoreType.DMA((7,)),
            pltpu.SemaphoreType.DMA((max(1, n_event - 1),)),
            pltpu.SemaphoreType.DMA((max(1, n_event - 1),)),
        ],
        compiler_params=pltpu.CompilerParams(
            collective_id=0, has_side_effects=True, vmem_limit_bytes=60 * 1024 * 1024
        ),
    )(
        *copied,
        source_element,
        source_offset,
        source_force.transpose(1, 0, 2),
    )
    return (final_f, final_a, kernels.transpose(0, 2, 1))


def solution(mesh):
    return jax.shard_map(
        functools.partial(on_device, mesh.shape["mesh"], mesh.shape["event"]),
        mesh=mesh,
        in_specs=(
            P("event", None, "mesh", None, None),
            P("event", None, "mesh", None, None),
            P("event", None, "mesh", None, None),
            P("event", None, "mesh", None, None),
            P(None, "mesh"),
            P(None, "mesh"),
            P(None, "mesh"),
            P("event"),
            P("event", None),
            P("event", None, None),
            P("event", None),
            P("event", None, None),
            P("event", None, None, None),
        ),
        out_specs=(
            P("event", None, "mesh", None, None),
            P("event", None, "mesh", None, None),
            P(None, None, ("mesh", "event")),
        ),
        check_vma=False,
    )
```

```python
import functools
import math

import jax
import jax.numpy as jnp
import numpy as np
from jax import lax
from jax.experimental import pallas as pl
from jax.experimental.pallas import tpu as pltpu
from jax.sharding import PartitionSpec as P

time_step = 0.04
adjoint_gain = 25.0
LANES = 128


def numpy_tables():
    gll_points = np.array([-1.0, -math.sqrt(3.0 / 7.0), 0.0, math.sqrt(3.0 / 7.0), 1.0])
    legendre = (35.0 * gll_points**4 - 30.0 * gll_points**2 + 3.0) / 8.0
    deriv_table = np.zeros((5, 5))
    for row_q in range(5):
        for col_k in range(5):
            if row_q != col_k:
                deriv_table[row_q, col_k] = legendre[row_q] / (
                    legendre[col_k] * (gll_points[row_q] - gll_points[col_k])
                )
    deriv_table[0, 0] = -5.0
    deriv_table[4, 4] = 5.0
    gll_weights = np.array([0.1, 49.0 / 90.0, 32.0 / 45.0, 49.0 / 90.0, 0.1])
    return (deriv_table, gll_weights)


DERIV, WEIGHTS = numpy_tables()


def constants():
    spread = np.zeros((4, LANES, 4, 4, 32), np.float32)
    for j in range(4):
        for ex in range(32):
            for c in range(4):
                spread[j, 4 * ex + c, c, j, ex] = 1.0
    spread = spread.reshape(512, 512)
    rows = np.zeros((5, 5, 8, 125), np.float32)
    cube = np.zeros((5, 5, 8, LANES), np.float32)
    for a in range(5):
        for b in range(5):
            for c in range(5):
                rows[a, c, b, (a * 5 + b) * 5 + c] = 1.0
                cube[a, c, b, :] = WEIGHTS[a] * WEIGHTS[b] * WEIGHTS[c]
    rows = rows.reshape(200, 125)
    dy = np.zeros((2, 5, 8, LANES), np.float32)
    for k in range(5):
        for b in range(5):
            dy[0, k, b, :] = DERIV[b, k]
            dy[1, k, b, :] = DERIV[k, b]
    bf = jnp.bfloat16
    return (
        jnp.asarray(spread, bf),
        jnp.asarray(np.ascontiguousarray(spread.T), bf),
        jnp.asarray(rows, bf),
        jnp.asarray(cube),
        jnp.asarray(dy),
    )


def split3(value):
    high = value.astype(jnp.bfloat16)
    rest = value - high.astype(jnp.float32)
    middle = rest.astype(jnp.bfloat16)
    low = (rest - middle.astype(jnp.float32)).astype(jnp.bfloat16)
    return (high, middle, low)


def dot(left, right):
    return jnp.dot(left, right, preferred_element_type=jnp.float32)


def move_right(values, table):
    parts = split3(values)
    count = values.shape[0]
    stacked = jnp.concatenate(parts, axis=0)
    moved = dot(stacked, table)
    return moved[0:count] + moved[count : 2 * count] + moved[2 * count : 3 * count]


def move_left(table, values):
    high, middle, low = split3(values)
    return dot(table, high) + dot(table, middle) + dot(table, low)


def move_left_t(table, values):
    contract = (((0,), (0,)), ((), ()))
    return sum(
        lax.dot_general(table, part, contract, preferred_element_type=jnp.float32)
        for part in split3(values)
    )


def roll_lane(value, shift):
    return pltpu.roll(value, shift % LANES, value.ndim - 1)


def lane_iota(ndim):
    return lax.broadcasted_iota(jnp.int32, (1,) * (ndim - 1) + (LANES,), ndim - 1)


def sub_iota(ndim):
    return lax.broadcasted_iota(jnp.int32, (1,) * (ndim - 2) + (8, LANES), ndim - 2)


def pick(mask, first, second):
    return jnp.where(jnp.broadcast_to(mask, first.shape), first, second)


def from_left(value):
    at_edge = lane_iota(value.ndim) % 32 == 0
    return pick(at_edge, roll_lane(value, -31), roll_lane(value, 1))


def from_right(value):
    at_edge = lane_iota(value.ndim) % 32 == 31
    return pick(at_edge, roll_lane(value, 31), roll_lane(value, -1))


def roll_sub(value):
    return pltpu.roll(value, 4, value.ndim - 2)


def assemble_xy(value):
    first = value[:, 0:1] + from_left(value[:, 4:5])
    value = jnp.concatenate([first, value[:, 1:4], from_right(first)], axis=1)
    swapped = roll_sub(value)
    other = pick(
        lane_iota(4) % 64 < 32, roll_lane(swapped, -32), roll_lane(swapped, 32)
    )
    return value + pick(sub_iota(4) % 4 == 0, other, jnp.zeros_like(other))


EDGE = float(DERIV[0, 0])
HALF = 64


def mix(coefs, planes):
    total = None
    for coef, plane in zip(coefs, planes):
        if coef != 0.0:
            term = float(coef) * plane
            total = term if total is None else total + term
    return total


def along_x(value, flipped=False):
    table = DERIV.T if flipped else DERIV
    rows = [value[k] for k in range(5)]
    return jnp.stack([mix(table[c], rows) for c in range(5)], axis=0)


def mirror(value):
    return jnp.concatenate([value[0:2], -value[2:3]], axis=0)


def low_lanes(ndim):
    return lane_iota(ndim) < HALF


def swap_half(value):
    return roll_lane(value, HALF)


def unpack(from_above, from_below):
    low = low_lanes(from_above.ndim)
    return (
        pick(low, from_above, swap_half(from_below)),
        pick(low, swap_half(from_above), from_below),
    )


def pack(first, second):
    low = low_lanes(first.ndim)
    return (
        pick(low, first, swap_half(second)),
        pick(low, swap_half(first), second),
    )


def kernel(
    n_mesh,
    n_event,
    steps,
    now_hbm,
    before_hbm,
    adj_hbm,
    after_hbm,
    rho_hbm,
    lam_hbm,
    mu_hbm,
    rec_elem_hbm,
    rec_off_hbm,
    data_hbm,
    spread_hbm,
    gather_hbm,
    rows_hbm,
    cube_hbm,
    dy_hbm,
    off_hbm,
    force_hbm,
    elem_ref,
    final_f_ref,
    final_a_ref,
    out_ref,
    now_ref,
    before_ref,
    adj_ref,
    after_ref,
    rho_ref,
    lam_ref,
    mu_ref,
    rec_elem_ref,
    rec_off_ref,
    data_ref,
    spread_ref,
    gather_ref,
    rows_ref,
    cube_ref,
    dy_ref,
    off_ref,
    force_ref,
    s_in,
    fields,
    stress,
    force,
    load_ref,
    strains,
    astrains,
    ksum,
    clam,
    cmu,
    minv,
    ghost_mat,
    work,
    halo_s,
    halo_r,
    mat_us,
    mat_ur,
    mat_ds,
    mat_dr,
    up_s,
    up_r,
    down_s,
    down_r,
    ev_s,
    ev_r,
    s_up,
    r_up,
    s_down,
    r_down,
    s_ev,
    r_ev,
):
    me = lax.axis_index("mesh")
    event = lax.axis_index("event")
    has_up = me > 0
    has_down = me < n_mesh - 1

    barrier = pltpu.get_barrier_semaphore()

    @pl.when(has_up)
    def _():
        pl.semaphore_signal(barrier, inc=1, device_id={"mesh": me - 1})

    @pl.when(has_down)
    def _():
        pl.semaphore_signal(barrier, inc=1, device_id={"mesh": me + 1})

    for hop in range(1, n_event):
        pl.semaphore_signal(
            barrier, inc=1, device_id={"event": lax.rem(event + hop, n_event)}
        )

    loads = []
    pairs = (
        (rows_hbm, rows_ref),
        (lam_hbm, lam_ref),
        (mu_hbm, mu_ref),
        (rho_hbm, rho_ref),
        (cube_hbm, cube_ref),
        (now_hbm, now_ref),
        (before_hbm, before_ref),
        (adj_hbm, adj_ref),
        (after_hbm, after_ref),
        (spread_hbm, spread_ref),
        (dy_hbm, dy_ref),
        (rec_elem_hbm, rec_elem_ref),
        (rec_off_hbm, rec_off_ref),
        (data_hbm, data_ref),
        (gather_hbm, gather_ref),
        (off_hbm, off_ref),
        (force_hbm, force_ref),
    )
    for place, (source, target) in enumerate(pairs):
        load_copy = pltpu.make_async_copy(source, target, s_in.at[place])
        load_copy.start()
        loads.append(load_copy)

    def up_copy(source, target, slot):
        return pltpu.make_async_remote_copy(
            src_ref=source, dst_ref=target, send_sem=s_up.at[slot],
            recv_sem=r_up.at[slot], device_id={"mesh": me - 1},
        )

    def down_copy(source, target, slot):
        return pltpu.make_async_remote_copy(
            src_ref=source, dst_ref=target, send_sem=s_down.at[slot],
            recv_sem=r_down.at[slot], device_id={"mesh": me + 1},
        )

    n_face = 6
    mat_slot = n_face
    halo_slot = n_face + 1

    def start_both(up, down):
        @pl.when(has_up)
        def _():
            up.start()

        @pl.when(has_down)
        def _():
            down.start()

    def wait_both(up, down):
        @pl.when(has_down)
        def _():
            up.wait_recv()

        @pl.when(has_up)
        def _():
            down.wait_recv()

    @pl.when(jnp.logical_not(has_down))
    def _():
        halo_r[...] = jnp.zeros_like(halo_r)
        up_r[...] = jnp.zeros_like(up_r)
        mat_ur[...] = jnp.zeros_like(mat_ur)

    @pl.when(jnp.logical_not(has_up))
    def _():
        down_r[...] = jnp.zeros_like(down_r)
        mat_dr[...] = jnp.zeros_like(mat_dr)

    low4 = low_lanes(4)

    for place in range(5):
        loads[place].wait()
    materials = jnp.concatenate([lam_ref[...], mu_ref[...], rho_ref[...]], axis=1)
    moved = move_left(rows_ref[...], materials)
    cube = cube_ref[...]

    def modulus(which):
        value = moved[:, which * LANES : (which + 1) * LANES].reshape(5, 5, 8, LANES)
        turned = jnp.stack([value[4 - a] for a in range(5)], axis=0)
        return pick(low4, value, turned) * cube

    lam_value = modulus(0)
    mu_value = modulus(1)
    clam[...] = lam_value
    cmu[...] = mu_value
    mass = modulus(2)
    mass = [assemble_xy(mass[a : a + 1])[0] for a in range(5)]
    mass[4] = mass[4] + swap_half(mass[4])

    squares = [float(DERIV[q, 0]) ** 2 for q in range(5)]
    diag_mu = mix(squares[1:], [mu_value[q] for q in range(1, 5)])
    diag_lam = mix(squares[1:], [lam_value[q] for q in range(1, 5)])
    diag_lam = diag_lam + (diag_mu + diag_mu)
    listed = [mass[0][c] for c in range(4)]
    for value in (lam_value[0], mu_value[0], diag_mu, diag_lam):
        listed += [value[c] for c in range(5)]
    for pair in range(12):
        up, down = pack(listed[2 * pair], listed[2 * pair + 1])
        mat_us[pair] = up
        mat_ds[pair] = down

    inputs = (now_ref, before_ref, adj_ref, after_ref)
    for place in range(5, 9):
        loads[place].wait()
    for index, ref in enumerate(inputs):
        halo_s[index] = ref[0, :, 0]

    pl.semaphore_wait(
        barrier,
        jnp.where(has_up, 1, 0) + jnp.where(has_down, 1, 0) + (n_event - 1),
    )

    @pl.when(has_up)
    def _():
        up_copy(halo_s, halo_r, halo_slot).start()

    start_both(up_copy(mat_us, mat_ur, mat_slot), down_copy(mat_ds, mat_dr, mat_slot))

    for place in range(9, 14):
        loads[place].wait()

    def bring_in(index):
        ref = inputs[index]
        upper = ref[0, :, 0:5]
        lower = mirror(
            jnp.stack(
                [jnp.zeros((3, 8, LANES), jnp.float32)]
                + [ref[0, :, 8 - a] for a in range(1, 5)],
                axis=1,
            )
        )
        parts = []
        for layer in (upper, lower):
            for shifted in (layer, roll_sub(layer)):
                parts.append(shifted.reshape(120, LANES))
        moved = move_right(jnp.concatenate(parts, axis=1), spread_ref[...])
        for c in range(4):
            fields[index, :, :, c] = moved[:, c * LANES : (c + 1) * LANES].reshape(
                3, 5, 8, LANES
            )
        fields[index, :, :, 4] = from_right(
            moved[:, 0:LANES].reshape(3, 5, 8, LANES)
        )

    def bring_halos():
        @pl.when(has_down)
        def _():
            up_copy(halo_s, halo_r, halo_slot).wait_recv()

        planes = jnp.stack([halo_r[:, 0], halo_r[:, 1], -halo_r[:, 2]], axis=1)
        parts = [
            planes.reshape(96, LANES),
            roll_sub(planes).reshape(96, LANES),
        ]
        moved = move_right(
            jnp.concatenate(parts, axis=1), spread_ref[2 * LANES : 4 * LANES]
        )
        for c in range(5):
            part = moved[:, (c % 4) * LANES : (c % 4 + 1) * LANES]
            part = part.reshape(4, 3, 8, LANES)
            if c == 4:
                part = from_right(part)
            fields[:, :, 0, c] = fields[:, :, 0, c] + part

    def along_y(value, flipped=False):
        total = None
        for k in range(5):
            row = jnp.broadcast_to(value[..., k : k + 1, :], value.shape)
            term = dy_ref[1 if flipped else 0, k] * row
            total = term if total is None else total + term
        return total

    def send(slot, value):
        for pair in range(2):
            up, down = pack(value[:, 2 * pair], value[:, 2 * pair + 1])
            up_s[slot, :, pair] = up
            down_s[slot, :, pair] = down
        start_both(
            up_copy(up_s.at[slot], up_r.at[slot], slot),
            down_copy(down_s.at[slot], down_r.at[slot], slot),
        )

    def receive(slot):
        wait_both(
            up_copy(up_s.at[slot], up_r.at[slot], slot),
            down_copy(down_s.at[slot], down_r.at[slot], slot),
        )
        sides = []
        for pair in range(2):
            sides += unpack(down_r[slot, :, pair], up_r[slot, :, pair])
        sides.append(from_right(sides[0]))
        return mirror(jnp.stack(sides, axis=1))

    def along_z(index, comp, a, first=0):
        return mix(
            DERIV[a, first:], [fields[index, comp, k] for k in range(first, 5)]
        )

    def strain_at(index, a):
        u = [fields[index, comp, a] for comp in range(3)]
        gz = [along_z(index, comp, a) for comp in range(3)]
        return (
            along_x(u[0]),
            along_y(u[1]),
            gz[2],
            along_y(u[0]) + along_x(u[1]),
            gz[0] + along_x(u[2]),
            gz[1] + along_y(u[2]),
        )

    def inside_face_force(index):
        total = [None, None, None]
        for q in range(1, 5):
            u = [fields[index, comp, q] for comp in range(3)]
            gz = [along_z(index, comp, q, 1) for comp in range(3)]
            mu_q = cmu[q]
            div = along_x(u[0]) + along_y(u[1]) + gz[2]
            parts = (
                mu_q * (gz[0] + along_x(u[2])),
                mu_q * (gz[1] + along_y(u[2])),
                clam[q] * div + (mu_q + mu_q) * gz[2],
            )
            for comp in range(3):
                term = float(DERIV[q, 0]) * parts[comp]
                total[comp] = term if total[comp] is None else total[comp] + term
        gz = [along_z(index, comp, 0, 1) for comp in range(3)]
        mu_0 = cmu[0]
        side = clam[0] * gz[2]
        xz = mu_0 * gz[0]
        yz = mu_0 * gz[1]
        zz = side + (mu_0 + mu_0) * gz[2]
        work[0] = side
        work[1] = yz
        return assemble_xy(
            jnp.stack(
                [
                    total[0] + along_x(side, True) + EDGE * xz,
                    total[1] + along_y(work[0], True) + EDGE * yz,
                    total[2]
                    + along_x(xz, True)
                    + along_y(work[1], True)
                    + EDGE * zz,
                ],
                axis=0,
            )
        )

    def ghost_face_force(index):
        u = [fields[index, comp, 0] for comp in range(3)]
        gz = [-EDGE * value for value in u]
        lam_g, mu_g = ghost_mat[0], ghost_mat[1]
        xx = along_x(u[0])
        yy = along_y(u[1])
        zz = gz[2]
        side = lam_g * (xx + yy + zz)
        mu_two = mu_g + mu_g
        xx = side + mu_two * xx
        yy = side + mu_two * yy
        zz = side + mu_two * zz
        xy = mu_g * (along_y(u[0]) + along_x(u[1]))
        xz = mu_g * (gz[0] + along_x(u[2]))
        yz = mu_g * (gz[1] + along_y(u[2]))
        work[0] = xy
        work[1] = yy
        work[2] = yz
        return (
            along_x(xx, True)
            + along_y(work[0], True)
            - EDGE * xz
            + ghost_mat[2] * u[0],
            along_x(xy, True)
            + along_y(work[1], True)
            - EDGE * yz
            + ghost_mat[2] * u[1],
            along_x(xz, True)
            + along_y(work[2], True)
            - EDGE * zz
            + ghost_mat[3] * u[2],
        )

    def make_stress(index, keep_strain):
        for a in range(5):
            strain = strain_at(index, a)
            lam_div = clam[a] * (strain[0] + strain[1] + strain[2])
            mu_a = cmu[a]
            mu_two = mu_a + mu_a
            for i in range(3):
                stress[i, a] = lam_div + mu_two * strain[i]
                stress[3 + i, a] = mu_a * strain[3 + i]
            if keep_strain is not None:
                for i in range(6):
                    keep_strain[a, i] = strain[i]

    pairs_of = ((0, 3, 4), (3, 1, 5), (4, 5, 2))

    def plane_force(a, load, extra=None):
        values = []
        for comp in range(3):
            ix, iy, iz = pairs_of[comp]
            total = along_x(stress[ix, a], True) + along_y(stress[iy, a], True)
            total = total + mix(DERIV[:, a], [stress[iz, q] for q in range(5)])
            if extra is not None:
                total = total + extra[comp]
            if load is not None:
                total = total - load(comp, a)
            values.append(total)
        value = assemble_xy(jnp.stack(values, axis=0))
        return value + mirror(swap_half(value)) if a == 4 else value

    def advance(index, older, a, value):
        fields[older, :, a] = (
            2.0 * fields[index, :, a] - fields[older, :, a]
        ) - minv[a] * value

    def inside_planes(index, older, load):
        for a in range(1, 5):
            advance(index, older, a, plane_force(a, load))

    def closed_step(index, older, slot, load):
        inside_planes(index, older, load)
        value = plane_force(0, load, ghost_face_force(index))
        advance(index, older, 0, value + receive(slot))

    def open_step(index, older, slot, load):
        force[...] = plane_force(0, None)
        send(slot, force[...])
        inside_planes(index, older, load)
        send(slot + 1, inside_face_force(older))

    def close_face(index, older, slot, load):
        value = force[...]
        if load is not None:
            value = value - assemble_xy(
                jnp.stack([load(comp, 0) for comp in range(3)], axis=0)
            )
        advance(index, older, 0, value + receive(slot))

    bring_in(0)
    send(0, inside_face_force(0))
    bring_in(2)
    send(1, inside_face_force(2))
    bring_in(1)
    bring_in(3)

    nrec = rec_elem_ref.shape[1]
    local = rec_elem_ref[...] - LANES * me
    depth = rec_off_ref[0]
    in_slab = (local >= 0) & (local < LANES)
    over = (local >= -HALF) & (local < 0) & (depth == 4)
    under = (local >= LANES) & (local < LANES + HALF) & (depth == 0)
    rec_at = jnp.where(
        in_slab,
        local,
        jnp.where(over, local + HALF, jnp.where(under, local - HALF, -1)),
    )
    depth = jnp.where(
        in_slab, jnp.where(local < HALF, depth, 4 - depth), jnp.zeros_like(depth)
    )
    lane_t = lax.broadcasted_iota(jnp.int32, (LANES, nrec), 0) == rec_at
    lane_t = jnp.where(lane_t, 1.0, 0.0).astype(jnp.bfloat16)
    eye = jnp.where(
        lax.broadcasted_iota(jnp.int32, (nrec, nrec), 0)
        == lax.broadcasted_iota(jnp.int32, (nrec, nrec), 1),
        1.0,
        0.0,
    ).astype(jnp.bfloat16)
    turned = (((1,), (1,)), ((), ()))

    def turn(part):
        return lax.dot_general(eye, part, turned, preferred_element_type=jnp.float32)

    rec_lane = turn(lane_t)
    rec_lanes = (rec_lane, rec_lane, pick(low_lanes(2), rec_lane, -rec_lane))
    row = depth * 40 + rec_off_ref[2] * 8 + rec_off_ref[1]
    rows_lanes = lax.broadcasted_iota(jnp.int32, (200, nrec), 0) == row
    rows_lanes = jnp.where(rows_lanes, 1.0, 0.0).astype(jnp.bfloat16)
    rec_rows = turn(rows_lanes).astype(jnp.bfloat16)
    observed = jnp.concatenate(
        [data_ref[n, comp] for n in range(steps) for comp in range(3)], axis=0
    )
    observed = sum(turn(part) for part in split3(observed))

    for place in range(15, 17):
        loads[place].wait()
    src_local = elem_ref[0] - LANES * me
    src_depth = off_ref[0, 0]
    src_in = (src_local >= 0) & (src_local < LANES)
    src_over = (src_local >= -HALF) & (src_local < 0) & (src_depth == 4)
    src_under = (src_local >= LANES) & (src_local < LANES + HALF) & (src_depth == 0)
    src_lane = jnp.where(
        src_in,
        src_local,
        jnp.where(
            src_over, src_local + HALF, jnp.where(src_under, src_local - HALF, -1)
        ),
    )
    src_depth = jnp.where(
        src_in, jnp.where(src_local < HALF, src_depth, 4 - src_depth), 0
    )
    src_row = src_depth * 40 + off_ref[0, 2] * 8 + off_ref[0, 1]

    def source_load(moment):
        def load(comp, a):
            shape = (5, 8, LANES)
            here = (
                lax.broadcasted_iota(jnp.int32, shape, 0) * 8
                + lax.broadcasted_iota(jnp.int32, shape, 1)
                + a * 40
            ) == src_row
            lanes = lax.broadcasted_iota(jnp.int32, shape, 2)
            value = force_ref[moment, 0, comp]
            if comp == 2:
                value = jnp.where(src_lane < HALF, value, -value)
            return jnp.where(here & (lanes == src_lane), value, 0.0)

        return load

    def record(index, moment):
        values = jnp.concatenate(
            [fields[index, comp].reshape(200, LANES) for comp in range(3)], axis=1
        )
        at_rows = move_left(rec_rows, values)
        found = []
        for comp in range(3):
            seen = at_rows[:, comp * LANES : (comp + 1) * LANES] * rec_lanes[comp]
            found.append(
                jnp.sum(seen, axis=1, keepdims=True)
                - observed[:, 3 * moment + comp : 3 * moment + comp + 1]
            )
        return found

    def inject(residual):
        scaled = jnp.concatenate(
            [adjoint_gain * residual[comp] * rec_lanes[comp] for comp in range(3)],
            axis=1,
        )
        injected = sum(dot(rows_lanes, part) for part in split3(scaled))
        for comp in range(3):
            load_ref[comp] = injected[:, comp * LANES : (comp + 1) * LANES].reshape(
                5, 5, 8, LANES
            )

    def held_load(comp, a):
        return load_ref[comp, a]

    bring_halos()
    make_stress(0, None)

    wait_both(up_copy(mat_us, mat_ur, mat_slot), down_copy(mat_ds, mat_dr, mat_slot))
    listed = []
    for pair in range(12):
        listed += unpack(mat_dr[pair], mat_ur[pair])
    face_mass = listed[0:4]
    face_mass = jnp.stack(face_mass + [from_right(face_mass[0])], axis=0)
    mass[0] = mass[0] + face_mass
    for which in range(4):
        for c in range(5):
            ghost_mat[which, c] = listed[4 + 5 * which + c]
    for a in range(5):
        keep = sub_iota(3) < 5
        if a == 0:
            keep = keep & (low_lanes(3) | has_down)
        keep = jnp.broadcast_to(keep, mass[a].shape)
        safe = jnp.where(keep, mass[a], 1.0)
        minv[a] = jnp.where(keep, time_step**2 / safe, 0.0)

    closed_step(0, 1, 0, source_load(0))

    make_stress(1, strains.at[0])
    open_step(1, 0, 2, source_load(1))

    residuals = [record(1, 0)]
    make_stress(2, astrains.at[2])
    closed_step(2, 3, 1, None)

    close_face(1, 0, 2, source_load(1))

    make_stress(0, strains.at[1])
    closed_step(0, 1, 3, source_load(2))
    residuals.append(record(0, 1))
    residuals.append(record(1, 2))

    inject(residuals[2])
    for a in range(5):
        value = assemble_xy(load_ref[:, a])
        if a == 4:
            value = value + mirror(swap_half(value))
        fields[3, :, a] = fields[3, :, a] + minv[a] * value

    make_stress(3, astrains.at[1])
    inject(residuals[1])
    open_step(3, 2, 4, held_load)

    def put_out(index, ref):
        sides = []
        for c in range(4):
            upper = fields[index, :, 0:4, c]
            lower = mirror(
                jnp.stack([fields[index, :, 4 - i, c] for i in range(4)], axis=1)
            )
            sides.append(pick(low4, upper, lower).reshape(96, LANES))
        moved = move_right(jnp.concatenate(sides, axis=1), gather_ref[...])
        for ez in range(2):
            first = moved[:, 2 * ez * LANES : (2 * ez + 1) * LANES]
            second = moved[:, (2 * ez + 1) * LANES : (2 * ez + 2) * LANES]
            first = first.reshape(3, 4, 8, LANES)
            second = roll_sub(second.reshape(3, 4, 8, LANES))
            ref[0, :, 4 * ez : 4 * ez + 4] = pick(sub_iota(4) < 4, first, second)

    def add_kernels(adjoint, other_at, first):
        for a in range(5):
            strain = [adjoint[a, i] for i in range(6)]
            other = other_at(a)
            div_a = strain[0] + strain[1] + strain[2]
            div_f = other[0] + other[1] + other[2]
            diag = strain[0] * other[0] + strain[1] * other[1] + strain[2] * other[2]
            shear = strain[3] * other[3] + strain[4] * other[4] + strain[5] * other[5]
            lam_part = div_a * div_f
            mu_part = diag + 0.5 * shear
            if not first:
                lam_part = ksum[0, a] + lam_part
                mu_part = ksum[1, a] + mu_part
            ksum[0, a] = lam_part
            ksum[1, a] = mu_part

    def kept(which):
        return lambda a: [strains[which, a, i] for i in range(6)]

    add_kernels(astrains.at[2], lambda a: strain_at(1, a), True)
    add_kernels(astrains.at[1], kept(1), False)
    loads[14].wait()
    put_out(1, final_f_ref)

    close_face(3, 2, 4, held_load)

    width = LANES // n_event

    def event_copy(hop):
        target = lax.rem(event + hop, n_event)
        return pltpu.make_async_remote_copy(
            src_ref=ev_s.at[:, pl.ds(pl.multiple_of(width * target, width), width)],
            dst_ref=ev_r.at[hop - 1],
            send_sem=s_ev.at[hop - 1],
            recv_sem=r_ev.at[hop - 1],
            device_id={"event": target},
        )

    def send_kernels():
        scales = (-time_step, -2.0 * time_step)
        for which, modulus_ref in enumerate((lam_ref, mu_ref)):
            value = ksum[which]
            turned_back = jnp.stack([value[4 - a] for a in range(5)], axis=0)
            value = pick(low4, value, turned_back).reshape(200, LANES)
            natural = move_left_t(rows_ref[...], value)
            ev_s[which] = jnp.transpose(natural * (scales[which] * modulus_ref[...]))
        for hop in range(1, n_event):
            event_copy(hop).start()

    make_stress(2, astrains.at[0])
    add_kernels(astrains.at[0], kept(0), False)
    send_kernels()
    inject(residuals[0])
    closed_step(2, 3, 5, held_load)
    put_out(3, final_a_ref)

    mine = pl.ds(pl.multiple_of(width * event, width), width)
    total = ev_s[:, mine]
    for hop in range(1, n_event):
        event_copy(hop).wait_recv()
        total = total + ev_r[hop - 1]
    out_ref[...] = total

    @pl.when(has_up)
    def _():
        up_copy(halo_s, halo_r, halo_slot).wait_send()
        up_copy(mat_us, mat_ur, mat_slot).wait_send()
        for slot in range(n_face):
            up_copy(up_s.at[slot], up_r.at[slot], slot).wait_send()

    @pl.when(has_down)
    def _():
        down_copy(mat_ds, mat_dr, mat_slot).wait_send()
        for slot in range(n_face):
            down_copy(down_s.at[slot], down_r.at[slot], slot).wait_send()

    for hop in range(1, n_event):
        event_copy(hop).wait_send()


def write_out(first, second, third, first_out, second_out, third_out, sems):
    copies = [
        pltpu.make_async_copy(source, target, sems.at[place])
        for place, (source, target) in enumerate(
            ((first, first_out), (second, second_out), (third, third_out))
        )
    ]
    for copy in copies:
        copy.start()
    for copy in copies:
        copy.wait()


def on_device(
    n_mesh,
    n_event,
    forward_before,
    forward_now,
    adjoint_after,
    adjoint_now,
    mass_density,
    lame_lambda,
    lame_mu,
    source_element,
    source_offset,
    source_force,
    receiver_element,
    receiver_offset,
    receiver_data,
):
    assert forward_now.shape[1:] == (3, 8, 8, 128)
    assert lame_mu.shape == (125, 128)
    steps = source_force.shape[1]
    assert steps == 3
    field = forward_now.shape
    vmem = pl.BlockSpec(memory_space=pltpu.VMEM)
    hbm = pl.BlockSpec(memory_space=pltpu.HBM)
    f32 = jnp.float32
    elem = (5, 5, 8, LANES)
    faces = (6, 3, 2, 8, LANES)
    copied = (
        forward_now,
        forward_before,
        adjoint_now,
        adjoint_after,
        mass_density,
        lame_lambda,
        lame_mu,
        receiver_element,
        receiver_offset.transpose(2, 0, 1),
        receiver_data.transpose(1, 3, 0, 2),
    ) + constants()
    small = (source_offset, source_force.transpose(1, 0, 2))
    results = pl.pallas_call(
        functools.partial(kernel, n_mesh, n_event, steps),
        out_shape=(
            pltpu.VMEM(field, f32),
            pltpu.VMEM(field, f32),
            pltpu.VMEM((2, LANES // n_event, 125), f32),
        ),
        in_specs=[hbm] * 17 + [pl.BlockSpec(memory_space=pltpu.SMEM)],
        out_specs=(vmem, vmem, vmem),
        scratch_shapes=[pltpu.VMEM(value.shape, value.dtype) for value in copied]
        + [pltpu.SMEM(value.shape, value.dtype) for value in small]
        + [
            pltpu.SemaphoreType.DMA((len(copied) + len(small),)),
            pltpu.VMEM((4, 3) + elem, f32),
            pltpu.VMEM((6,) + elem, f32),
            pltpu.VMEM((3,) + elem[1:], f32),
            pltpu.VMEM((3,) + elem, f32),
            pltpu.VMEM((2, 5, 6, 5, 8, LANES), f32),
            pltpu.VMEM((3, 5, 6, 5, 8, LANES), f32),
            pltpu.VMEM((2,) + elem, f32),
            pltpu.VMEM(elem, f32),
            pltpu.VMEM(elem, f32),
            pltpu.VMEM(elem, f32),
            pltpu.VMEM((4,) + elem[1:], f32),
            pltpu.VMEM((3,) + elem[1:], f32),
            pltpu.VMEM((4, 3, 8, LANES), f32),
            pltpu.VMEM((4, 3, 8, LANES), f32),
            pltpu.VMEM((12, 8, LANES), f32),
            pltpu.VMEM((12, 8, LANES), f32),
            pltpu.VMEM((12, 8, LANES), f32),
            pltpu.VMEM((12, 8, LANES), f32),
            pltpu.VMEM(faces, f32),
            pltpu.VMEM(faces, f32),
            pltpu.VMEM(faces, f32),
            pltpu.VMEM(faces, f32),
            pltpu.VMEM((2, LANES, 125), f32),
            pltpu.VMEM((max(1, n_event - 1), 2, LANES // n_event, 125), f32),
            pltpu.SemaphoreType.DMA((8,)),
            pltpu.SemaphoreType.DMA((8,)),
            pltpu.SemaphoreType.DMA((7,)),
            pltpu.SemaphoreType.DMA((7,)),
            pltpu.SemaphoreType.DMA((max(1, n_event - 1),)),
            pltpu.SemaphoreType.DMA((max(1, n_event - 1),)),
        ],
        compiler_params=pltpu.CompilerParams(
            collective_id=0, has_side_effects=True, vmem_limit_bytes=32 * 1024 * 1024
        ),
    )(
        *(
            pltpu.with_memory_space_constraint(value, pltpu.HBM)
            for value in copied + small
        ),
        source_element,
    )
    final_f, final_a, kernels = pl.pallas_call(
        write_out,
        out_shape=tuple(
            jax.ShapeDtypeStruct(value.shape, value.dtype) for value in results
        ),
        in_specs=[vmem] * 3,
        out_specs=(hbm, hbm, hbm),
        scratch_shapes=[pltpu.SemaphoreType.DMA((3,))],
    )(*(pltpu.with_memory_space_constraint(value, pltpu.VMEM) for value in results))
    return (final_f, final_a, kernels.transpose(0, 2, 1))


def solution(mesh):
    return jax.shard_map(
        functools.partial(on_device, mesh.shape["mesh"], mesh.shape["event"]),
        mesh=mesh,
        in_specs=(
            P("event", None, "mesh", None, None),
            P("event", None, "mesh", None, None),
            P("event", None, "mesh", None, None),
            P("event", None, "mesh", None, None),
            P(None, "mesh"),
            P(None, "mesh"),
            P(None, "mesh"),
            P("event"),
            P("event", None),
            P("event", None, None),
            P("event", None),
            P("event", None, None),
            P("event", None, None, None),
        ),
        out_specs=(
            P("event", None, "mesh", None, None),
            P("event", None, "mesh", None, None),
            P(None, None, ("mesh", "event")),
        ),
        check_vma=False,
    )
```

```python
import functools
import math

import jax
import jax.numpy as jnp
import numpy as np
from jax import lax
from jax.experimental import pallas as pl
from jax.experimental.pallas import tpu as pltpu
from jax.sharding import PartitionSpec as P

time_step = 0.04
adjoint_gain = 25.0
LANES = 128


def numpy_tables():
    gll_points = np.array([-1.0, -math.sqrt(3.0 / 7.0), 0.0, math.sqrt(3.0 / 7.0), 1.0])
    legendre = (35.0 * gll_points**4 - 30.0 * gll_points**2 + 3.0) / 8.0
    deriv_table = np.zeros((5, 5))
    for row_q in range(5):
        for col_k in range(5):
            if row_q != col_k:
                deriv_table[row_q, col_k] = legendre[row_q] / (
                    legendre[col_k] * (gll_points[row_q] - gll_points[col_k])
                )
    deriv_table[0, 0] = -5.0
    deriv_table[4, 4] = 5.0
    gll_weights = np.array([0.1, 49.0 / 90.0, 32.0 / 45.0, 49.0 / 90.0, 0.1])
    return (deriv_table, gll_weights)


DERIV, WEIGHTS = numpy_tables()


def constants():
    spread = np.zeros((4, LANES, 4, 4, 32), np.float32)
    for j in range(4):
        for ex in range(32):
            for c in range(4):
                spread[j, 4 * ex + c, c, j, ex] = 1.0
    spread = spread.reshape(512, 512)
    rows = np.zeros((5, 5, 8, 125), np.float32)
    cube = np.zeros((5, 5, 8, LANES), np.float32)
    for a in range(5):
        for b in range(5):
            for c in range(5):
                rows[a, c, b, (a * 5 + b) * 5 + c] = 1.0
                cube[a, c, b, :] = WEIGHTS[a] * WEIGHTS[b] * WEIGHTS[c]
    rows = rows.reshape(200, 125)
    dy = np.zeros((2, 5, 8, LANES), np.float32)
    for k in range(5):
        for b in range(5):
            dy[0, k, b, :] = DERIV[b, k]
            dy[1, k, b, :] = DERIV[k, b]
    bf = jnp.bfloat16
    return (
        jnp.asarray(spread, bf),
        jnp.asarray(np.ascontiguousarray(spread.T), bf),
        jnp.asarray(rows, bf),
        jnp.asarray(cube),
        jnp.asarray(dy),
    )


def split3(value):
    high = value.astype(jnp.bfloat16)
    rest = value - high.astype(jnp.float32)
    middle = rest.astype(jnp.bfloat16)
    low = (rest - middle.astype(jnp.float32)).astype(jnp.bfloat16)
    return (high, middle, low)


def dot(left, right):
    return jnp.dot(left, right, preferred_element_type=jnp.float32)


def move_right(values, table):
    parts = split3(values)
    count = values.shape[0]
    stacked = jnp.concatenate(parts, axis=0)
    moved = dot(stacked, table)
    return moved[0:count] + moved[count : 2 * count] + moved[2 * count : 3 * count]


def move_left(table, values):
    high, middle, low = split3(values)
    return dot(table, high) + dot(table, middle) + dot(table, low)


def move_left_t(table, values):
    contract = (((0,), (0,)), ((), ()))
    return sum(
        lax.dot_general(table, part, contract, preferred_element_type=jnp.float32)
        for part in split3(values)
    )


def roll_lane(value, shift):
    return pltpu.roll(value, shift % LANES, value.ndim - 1)


def lane_iota(ndim):
    return lax.broadcasted_iota(jnp.int32, (1,) * (ndim - 1) + (LANES,), ndim - 1)


def sub_iota(ndim):
    return lax.broadcasted_iota(jnp.int32, (1,) * (ndim - 2) + (8, LANES), ndim - 2)


def pick(mask, first, second):
    return jnp.where(jnp.broadcast_to(mask, first.shape), first, second)


def from_left(value):
    at_edge = lane_iota(value.ndim) % 32 == 0
    return pick(at_edge, roll_lane(value, -31), roll_lane(value, 1))


def from_right(value):
    at_edge = lane_iota(value.ndim) % 32 == 31
    return pick(at_edge, roll_lane(value, 31), roll_lane(value, -1))


def roll_sub(value):
    return pltpu.roll(value, 4, value.ndim - 2)


def assemble_xy(value):
    first = value[:, 0:1] + from_left(value[:, 4:5])
    value = jnp.concatenate([first, value[:, 1:4], from_right(first)], axis=1)
    swapped = roll_sub(value)
    other = pick(
        lane_iota(4) % 64 < 32, roll_lane(swapped, -32), roll_lane(swapped, 32)
    )
    return value + pick(sub_iota(4) % 4 == 0, other, jnp.zeros_like(other))


EDGE = float(DERIV[0, 0])
HALF = 64


def mix(coefs, planes):
    total = None
    for coef, plane in zip(coefs, planes):
        if coef != 0.0:
            term = float(coef) * plane
            total = term if total is None else total + term
    return total


def along_x(value, flipped=False):
    table = DERIV.T if flipped else DERIV
    rows = [value[k] for k in range(5)]
    return jnp.stack([mix(table[c], rows) for c in range(5)], axis=0)


def mirror(value):
    return jnp.concatenate([value[0:2], -value[2:3]], axis=0)


def low_lanes(ndim):
    return lane_iota(ndim) < HALF


def swap_half(value):
    return roll_lane(value, HALF)


def unpack(from_above, from_below):
    low = low_lanes(from_above.ndim)
    return (
        pick(low, from_above, swap_half(from_below)),
        pick(low, swap_half(from_above), from_below),
    )


def pack(first, second):
    low = low_lanes(first.ndim)
    return (
        pick(low, first, swap_half(second)),
        pick(low, swap_half(first), second),
    )


def kernel(
    n_mesh,
    n_event,
    steps,
    now_hbm,
    before_hbm,
    adj_hbm,
    after_hbm,
    rho_hbm,
    lam_hbm,
    mu_hbm,
    rec_elem_hbm,
    rec_off_hbm,
    data_hbm,
    spread_hbm,
    gather_hbm,
    rows_hbm,
    cube_hbm,
    dy_hbm,
    off_hbm,
    force_hbm,
    elem_ref,
    final_f_ref,
    final_a_ref,
    out_ref,
    now_ref,
    before_ref,
    adj_ref,
    after_ref,
    rho_ref,
    lam_ref,
    mu_ref,
    rec_elem_ref,
    rec_off_ref,
    data_ref,
    spread_ref,
    gather_ref,
    rows_ref,
    cube_ref,
    dy_ref,
    off_ref,
    force_ref,
    s_in,
    fields,
    stress,
    stress_a,
    held,
    ghost,
    delta,
    count_map,
    data_map,
    source_map,
    first_load,
    strains,
    astrains,
    ksum,
    clam,
    cmu,
    minv,
    ghost_mat,
    work,
    halo_r,
    halo_e,
    mat_us,
    mat_ur,
    mat_ds,
    mat_dr,
    up_s,
    up_r,
    down_s,
    down_r,
    ev_s,
    ev_r,
    s_up,
    r_up,
    s_down,
    r_down,
    s_ev,
    r_ev,
):
    me = lax.axis_index("mesh")
    event = lax.axis_index("event")
    has_up = me > 0
    has_down = me < n_mesh - 1

    barrier = pltpu.get_barrier_semaphore()

    @pl.when(has_up)
    def _():
        pl.semaphore_signal(barrier, inc=1, device_id={"mesh": me - 1})

    @pl.when(has_down)
    def _():
        pl.semaphore_signal(barrier, inc=1, device_id={"mesh": me + 1})

    for hop in range(1, n_event):
        pl.semaphore_signal(
            barrier, inc=1, device_id={"event": lax.rem(event + hop, n_event)}
        )

    loads = []
    pairs = (
        (rows_hbm, rows_ref),
        (lam_hbm, lam_ref),
        (mu_hbm, mu_ref),
        (rho_hbm, rho_ref),
        (cube_hbm, cube_ref),
        (now_hbm, now_ref),
        (before_hbm, before_ref),
        (adj_hbm, adj_ref),
        (after_hbm, after_ref),
        (spread_hbm, spread_ref),
        (dy_hbm, dy_ref),
        (rec_elem_hbm, rec_elem_ref),
        (rec_off_hbm, rec_off_ref),
        (data_hbm, data_ref),
        (gather_hbm, gather_ref),
        (off_hbm, off_ref),
        (force_hbm, force_ref),
    )
    for place, (source, target) in enumerate(pairs):
        load_copy = pltpu.make_async_copy(source, target, s_in.at[place])
        load_copy.start()
        loads.append(load_copy)

    def up_copy(source, target, slot):
        return pltpu.make_async_remote_copy(
            src_ref=source, dst_ref=target, send_sem=s_up.at[slot],
            recv_sem=r_up.at[slot], device_id={"mesh": me - 1},
        )

    def down_copy(source, target, slot):
        return pltpu.make_async_remote_copy(
            src_ref=source, dst_ref=target, send_sem=s_down.at[slot],
            recv_sem=r_down.at[slot], device_id={"mesh": me + 1},
        )

    n_face = 6
    mat_slot = n_face
    halo_slot = n_face + 1

    def start_both(up, down):
        @pl.when(has_up)
        def _():
            up.start()

        @pl.when(has_down)
        def _():
            down.start()

    def wait_both(up, down):
        @pl.when(has_down)
        def _():
            up.wait_recv()

        @pl.when(has_up)
        def _():
            down.wait_recv()

    @pl.when(jnp.logical_not(has_down))
    def _():
        halo_r[...] = jnp.zeros_like(halo_r)
        up_r[...] = jnp.zeros_like(up_r)
        mat_ur[...] = jnp.zeros_like(mat_ur)

    @pl.when(jnp.logical_not(has_up))
    def _():
        down_r[...] = jnp.zeros_like(down_r)
        mat_dr[...] = jnp.zeros_like(mat_dr)

    pl.semaphore_wait(
        barrier,
        jnp.where(has_up, 1, 0) + jnp.where(has_down, 1, 0) + (n_event - 1),
    )
    tops = (now_hbm, before_hbm, adj_hbm, after_hbm)

    def halo_copy(index):
        return up_copy(
            tops[index].at[0, :, 0], halo_r.at[index], halo_slot + index
        )

    @pl.when(has_up)
    def _():
        for index in range(4):
            halo_copy(index).start()

    low4 = low_lanes(4)

    for place in range(5):
        loads[place].wait()
    materials = jnp.concatenate([lam_ref[...], mu_ref[...], rho_ref[...]], axis=1)
    moved = move_left(rows_ref[...], materials)
    cube = cube_ref[...]

    def modulus(which):
        value = moved[:, which * LANES : (which + 1) * LANES].reshape(5, 5, 8, LANES)
        turned = jnp.stack([value[4 - a] for a in range(5)], axis=0)
        return pick(low4, value, turned) * cube

    lam_value = modulus(0)
    mu_value = modulus(1)
    clam[...] = lam_value
    cmu[...] = mu_value
    mass = modulus(2)
    mass = [assemble_xy(mass[a : a + 1])[0] for a in range(5)]
    mass[4] = mass[4] + swap_half(mass[4])

    def set_minv(a, value):
        keep = sub_iota(3) < 5
        if a == 0:
            keep = keep & (low_lanes(3) | has_down)
        keep = jnp.broadcast_to(keep, value.shape)
        safe = jnp.where(keep, value, 1.0)
        minv[a] = jnp.where(keep, time_step**2 / safe, 0.0)

    for a in range(1, 5):
        set_minv(a, mass[a])

    squares = [float(DERIV[q, 0]) ** 2 for q in range(5)]
    diag_mu = mix(squares[1:], [mu_value[q] for q in range(1, 5)])
    diag_lam = mix(squares[1:], [lam_value[q] for q in range(1, 5)])
    diag_lam = diag_lam + (diag_mu + diag_mu)
    listed = [mass[0][c] for c in range(4)]
    for value in (lam_value[0], mu_value[0], diag_mu, diag_lam):
        listed += [value[c] for c in range(5)]
    for pair in range(12):
        up, down = pack(listed[2 * pair], listed[2 * pair + 1])
        mat_us[pair] = up
        mat_ds[pair] = down

    start_both(up_copy(mat_us, mat_ur, mat_slot), down_copy(mat_ds, mat_dr, mat_slot))

    for place in range(5, 11):
        loads[place].wait()
    inputs = (now_ref, before_ref, adj_ref, after_ref)

    def bring_in(index):
        ref = inputs[index]
        upper = ref[0, :, 0:5]
        lower = mirror(
            jnp.stack(
                [jnp.zeros((3, 8, LANES), jnp.float32)]
                + [ref[0, :, 8 - a] for a in range(1, 5)],
                axis=1,
            )
        )
        parts = []
        for layer in (upper, lower):
            for shifted in (layer, roll_sub(layer)):
                parts.append(shifted.reshape(120, LANES))
        moved = move_right(jnp.concatenate(parts, axis=1), spread_ref[...])
        for c in range(4):
            fields[index, :, :, c] = moved[:, c * LANES : (c + 1) * LANES].reshape(
                3, 5, 8, LANES
            )
        fields[index, :, :, 4] = from_right(
            moved[:, 0:LANES].reshape(3, 5, 8, LANES)
        )

    def bring_halos():
        @pl.when(has_down)
        def _():
            for index in range(4):
                halo_copy(index).wait_recv()

        planes = jnp.stack([halo_r[:, 0], halo_r[:, 1], -halo_r[:, 2]], axis=1)
        parts = [
            planes.reshape(96, LANES),
            roll_sub(planes).reshape(96, LANES),
        ]
        moved = move_right(
            jnp.concatenate(parts, axis=1), spread_ref[2 * LANES : 4 * LANES]
        )
        for c in range(5):
            part = moved[:, (c % 4) * LANES : (c % 4 + 1) * LANES]
            part = part.reshape(4, 3, 8, LANES)
            if c == 4:
                part = from_right(part)
            halo_e[:, :, c] = part
            fields[:, :, 0, c] = fields[:, :, 0, c] + part

    def along_y(value, flipped=False):
        total = None
        for k in range(5):
            row = jnp.broadcast_to(value[..., k : k + 1, :], value.shape)
            term = dy_ref[1 if flipped else 0, k] * row
            total = term if total is None else total + term
        return total

    def send(slot, value):
        for pair in range(2):
            up, down = pack(value[:, 2 * pair], value[:, 2 * pair + 1])
            up_s[slot, :, pair] = up
            down_s[slot, :, pair] = down
        start_both(
            up_copy(up_s.at[slot], up_r.at[slot], slot),
            down_copy(down_s.at[slot], down_r.at[slot], slot),
        )

    def receive(slot):
        wait_both(
            up_copy(up_s.at[slot], up_r.at[slot], slot),
            down_copy(down_s.at[slot], down_r.at[slot], slot),
        )
        sides = []
        for pair in range(2):
            sides += unpack(down_r[slot, :, pair], up_r[slot, :, pair])
        sides.append(from_right(sides[0]))
        return mirror(jnp.stack(sides, axis=1))

    def along_z(index, comp, a, first=0):
        return mix(
            DERIV[a, first:], [fields[index, comp, k] for k in range(first, 5)]
        )

    def strain_at(index, a):
        u = [fields[index, comp, a] for comp in range(3)]
        gz = [along_z(index, comp, a) for comp in range(3)]
        return (
            along_x(u[0]),
            along_y(u[1]),
            gz[2],
            along_y(u[0]) + along_x(u[1]),
            gz[0] + along_x(u[2]),
            gz[1] + along_y(u[2]),
        )

    def set_ghost():
        u = [delta[comp] for comp in range(3)]
        gz = [-EDGE * value for value in u]
        lam_g, mu_g = ghost_mat[0], ghost_mat[1]
        xx = along_x(u[0])
        yy = along_y(u[1])
        zz = gz[2]
        side = lam_g * (xx + yy + zz)
        mu_two = mu_g + mu_g
        xx = side + mu_two * xx
        yy = side + mu_two * yy
        zz = side + mu_two * zz
        xy = mu_g * (along_y(u[0]) + along_x(u[1]))
        xz = mu_g * (gz[0] + along_x(u[2]))
        yz = mu_g * (gz[1] + along_y(u[2]))
        work[0] = xy
        work[1] = yy
        work[2] = yz
        values = (
            along_x(xx, True)
            + along_y(work[0], True)
            - EDGE * xz
            + ghost_mat[2] * u[0],
            along_x(xy, True)
            + along_y(work[1], True)
            - EDGE * yz
            + ghost_mat[2] * u[1],
            along_x(xz, True)
            + along_y(work[2], True)
            - EDGE * zz
            + ghost_mat[3] * u[2],
        )
        ghost[...] = assemble_xy(jnp.stack(values, axis=0))

    def put_stress(target, a, strain, add):
        lam_div = clam[a] * (strain[0] + strain[1] + strain[2])
        mu_a = cmu[a]
        mu_two = mu_a + mu_a
        for i in range(3):
            value = lam_div + mu_two * strain[i]
            target[i, a] = target[i, a] + value if add else value
            value = mu_a * strain[3 + i]
            target[3 + i, a] = target[3 + i, a] + value if add else value

    def make_stress(index, target, keep_strain):
        for a in range(5):
            strain = strain_at(index, a)
            put_stress(target, a, strain, False)
            if keep_strain is not None:
                for i in range(6):
                    keep_strain[a, i] = strain[i]

    def face_strain():
        u = [delta[comp] for comp in range(3)]
        return (
            along_x(u[0]),
            along_y(u[1]),
            EDGE * u[2],
            along_y(u[0]) + along_x(u[1]),
            EDGE * u[0] + along_x(u[2]),
            EDGE * u[1] + along_y(u[2]),
        )

    def add_face(target, keep_strain):
        strain = face_strain()
        put_stress(target, 0, strain, True)
        if keep_strain is not None:
            for i in range(6):
                keep_strain[0, i] = keep_strain[0, i] + strain[i]
        for q in range(1, 5):
            gz = [float(DERIV[q, 0]) * delta[comp] for comp in range(3)]
            mu_q = cmu[q]
            side = clam[q] * gz[2]
            target[0, q] = target[0, q] + side
            target[1, q] = target[1, q] + side
            target[2, q] = target[2, q] + (side + (mu_q + mu_q) * gz[2])
            target[4, q] = target[4, q] + mu_q * gz[0]
            target[5, q] = target[5, q] + mu_q * gz[1]
            if keep_strain is not None:
                keep_strain[q, 2] = keep_strain[q, 2] + gz[2]
                keep_strain[q, 4] = keep_strain[q, 4] + gz[0]
                keep_strain[q, 5] = keep_strain[q, 5] + gz[1]

    pairs_of = ((0, 3, 4), (3, 1, 5), (4, 5, 2))

    def both_layers(value):
        return value + mirror(swap_half(value))

    def plane_force(source, a):
        values = []
        for comp in range(3):
            ix, iy, iz = pairs_of[comp]
            total = along_x(source[ix, a], True) + along_y(source[iy, a], True)
            values.append(total + mix(DERIV[:, a], [source[iz, q] for q in range(5)]))
        value = assemble_xy(jnp.stack(values, axis=0))
        return both_layers(value) if a == 4 else value

    def advance(index, older, a, value, load):
        if load is not None:
            value = value - load(a)
        fields[older, :, a] = (
            2.0 * fields[index, :, a] - fields[older, :, a]
        ) - minv[a] * value

    def inside_planes(index, older, source, load):
        for a in range(1, 5):
            advance(index, older, a, plane_force(source, a), load)

    def close_step(index, older, source, slot, load):
        inside_planes(index, older, source, load)
        close_outer(index, older, source, slot, load)

    def close_outer(index, older, source, slot, load):
        value = plane_force(source, 0) + ghost[...]
        advance(index, older, 0, value + receive(slot), load)

    def open_step(index, older, slot, load):
        held[...] = plane_force(stress, 0)
        send(slot, held[...])
        inside_planes(index, older, stress, load)
        advance(index, older, 0, held[...], load)

    def close_face(older, slot, keep_strain):
        delta[...] = -minv[0] * receive(slot)
        fields[older, :, 0] = fields[older, :, 0] + delta[...]
        add_face(stress, keep_strain)

    bring_in(0)
    make_stress(0, stress, None)
    send(0, plane_force(stress, 0))
    bring_in(2)
    make_stress(2, stress_a, astrains.at[2])
    send(1, plane_force(stress_a, 0))
    bring_in(1)
    bring_in(3)

    for place in range(11, 14):
        loads[place].wait()
    nrec = rec_elem_ref.shape[1]
    local = rec_elem_ref[...] - LANES * me
    depth = rec_off_ref[0]
    in_slab = (local >= 0) & (local < LANES)
    over = (local >= -HALF) & (local < 0) & (depth == 4)
    under = (local >= LANES) & (local < LANES + HALF) & (depth == 0)
    rec_at = jnp.where(
        in_slab,
        local,
        jnp.where(over, local + HALF, jnp.where(under, local - HALF, -1)),
    )
    depth = jnp.where(
        in_slab, jnp.where(local < HALF, depth, 4 - depth), jnp.zeros_like(depth)
    )
    lane_t = lax.broadcasted_iota(jnp.int32, (LANES, nrec), 0) == rec_at
    lane_t = jnp.where(lane_t, 1.0, 0.0).astype(jnp.bfloat16)
    eye = jnp.where(
        lax.broadcasted_iota(jnp.int32, (nrec, nrec), 0)
        == lax.broadcasted_iota(jnp.int32, (nrec, nrec), 1),
        1.0,
        0.0,
    ).astype(jnp.bfloat16)
    turned = (((1,), (1,)), ((), ()))

    def turn(part):
        return lax.dot_general(eye, part, turned, preferred_element_type=jnp.float32)

    rec_lane = turn(lane_t)
    rec_lanes = (rec_lane, rec_lane, pick(low_lanes(2), rec_lane, -rec_lane))
    row = depth * 40 + rec_off_ref[2] * 8 + rec_off_ref[1]
    rows_lanes = lax.broadcasted_iota(jnp.int32, (200, nrec), 0) == row
    rows_lanes = jnp.where(rows_lanes, 1.0, 0.0).astype(jnp.bfloat16)
    observed = jnp.concatenate(
        [data_ref[n, comp] for n in range(steps) for comp in range(3)], axis=0
    )
    observed = sum(turn(part) for part in split3(observed))

    for place in range(15, 17):
        loads[place].wait()
    src_local = elem_ref[0] - LANES * me
    src_depth = off_ref[0, 0]
    src_in = (src_local >= 0) & (src_local < LANES)
    src_over = (src_local >= -HALF) & (src_local < 0) & (src_depth == 4)
    src_under = (src_local >= LANES) & (src_local < LANES + HALF) & (src_depth == 0)
    src_lane = jnp.where(
        src_in,
        src_local,
        jnp.where(
            src_over, src_local + HALF, jnp.where(src_under, src_local - HALF, -1)
        ),
    )
    src_depth = jnp.where(
        src_in, jnp.where(src_local < HALF, src_depth, 4 - src_depth), 0
    )
    src_row = src_depth * 40 + off_ref[0, 2] * 8 + off_ref[0, 1]

    shape = (5, 8, LANES)
    src_lanes = lax.broadcasted_iota(jnp.int32, shape, 2) == src_lane
    src_rows = lax.broadcasted_iota(jnp.int32, shape, 0) * 8 + lax.broadcasted_iota(
        jnp.int32, shape, 1
    )
    scaled = adjoint_gain * observed
    columns = jnp.concatenate(
        [
            scaled[:, 3 * moment + comp : 3 * moment + comp + 1] * rec_lanes[comp]
            for moment in range(steps)
            for comp in range(3)
        ],
        axis=1,
    )
    at_points = sum(dot(rows_lanes, part) for part in split3(columns))
    counts = adjoint_gain * dot(rows_lanes, rec_lane.astype(jnp.bfloat16))
    for a in range(5):
        source_at = jnp.where(src_lanes & (src_rows + 40 * a == src_row), 1.0, 0.0)
        count_at = counts[40 * a : 40 * a + 40].reshape(shape)
        data_at = [
            at_points[40 * a : 40 * a + 40, LANES * i : LANES * (i + 1)].reshape(shape)
            for i in range(3 * steps)
        ]
        value = assemble_xy(jnp.stack([source_at, count_at] + data_at, axis=0))
        if a == 4:
            other = swap_half(value)
            value = value + jnp.stack(
                [
                    -other[i] if i >= 2 and (i - 2) % 3 == 2 else other[i]
                    for i in range(2 + 3 * steps)
                ],
                axis=0,
            )
        source_map[a] = value[0]
        count_map[a] = value[1]
        for moment in range(steps):
            data_map[moment, :, a] = value[2 + 3 * moment : 5 + 3 * moment]

    def source_load(moment):
        forces = [force_ref[moment, 0, comp] for comp in range(3)]
        lane = lax.broadcasted_iota(jnp.int32, (8, LANES), 1)
        forces[2] = jnp.where(lane < HALF, forces[2], -forces[2])
        return lambda a: jnp.stack(
            [source_map[a] * forces[comp] for comp in range(3)], axis=0
        )

    def receiver_load(index, moment):
        return (
            lambda a: count_map[a][None] * fields[index, :, a] - data_map[moment, :, a]
        )

    bring_halos()
    delta[...] = halo_e[0]
    add_face(stress, None)
    inside_planes(0, 1, stress, source_load(0))

    wait_both(up_copy(mat_us, mat_ur, mat_slot), down_copy(mat_ds, mat_dr, mat_slot))
    listed = []
    for pair in range(12):
        listed += unpack(mat_dr[pair], mat_ur[pair])
    for which in range(4):
        for c in range(5):
            ghost_mat[which, c] = listed[4 + 5 * which + c]
    face_mass = listed[0:4]
    set_minv(0, mass[0] + jnp.stack(face_mass + [from_right(face_mass[0])], axis=0))

    def ghost_of_start(index):
        top = fields[index, :, 0]
        delta[...] = pick(low4, top, jnp.zeros_like(top))
        set_ghost()

    ghost_of_start(0)
    close_outer(0, 1, stress, 0, source_load(0))

    make_stress(1, stress, strains.at[0])
    open_step(1, 0, 2, source_load(1))
    make_stress(0, stress, strains.at[1])
    send(3, plane_force(stress, 0))

    delta[...] = halo_e[2]
    add_face(stress_a, astrains.at[2])
    ghost_of_start(2)
    close_step(2, 3, stress_a, 1, None)
    load = receiver_load(1, 0)
    for a in range(5):
        first_load[:, a] = load(a)
        fields[3, :, a] = fields[3, :, a] - minv[a] * data_map[2, :, a]
    delta[...] = -minv[0] * held[...]
    set_ghost()

    close_face(0, 2, strains.at[1])
    close_step(0, 1, stress, 3, source_load(2))

    for a in range(5):
        fields[3, :, a] = fields[3, :, a] + minv[a] * (
            count_map[a][None] * fields[1, :, a]
        )
    make_stress(3, stress, astrains.at[1])
    open_step(3, 2, 4, receiver_load(0, 1))
    make_stress(2, stress, astrains.at[0])
    send(5, plane_force(stress, 0))

    def put_out(index, ref):
        sides = []
        for c in range(4):
            upper = fields[index, :, 0:4, c]
            lower = mirror(
                jnp.stack([fields[index, :, 4 - i, c] for i in range(4)], axis=1)
            )
            sides.append(pick(low4, upper, lower).reshape(96, LANES))
        moved = move_right(jnp.concatenate(sides, axis=1), gather_ref[...])
        for ez in range(2):
            first = moved[:, 2 * ez * LANES : (2 * ez + 1) * LANES]
            second = moved[:, (2 * ez + 1) * LANES : (2 * ez + 2) * LANES]
            first = first.reshape(3, 4, 8, LANES)
            second = roll_sub(second.reshape(3, 4, 8, LANES))
            ref[0, :, 4 * ez : 4 * ez + 4] = pick(sub_iota(4) < 4, first, second)

    def add_kernels(adjoint, other_at, first):
        for a in range(5):
            strain = [adjoint[a, i] for i in range(6)]
            other = other_at(a)
            div_a = strain[0] + strain[1] + strain[2]
            div_f = other[0] + other[1] + other[2]
            diag = strain[0] * other[0] + strain[1] * other[1] + strain[2] * other[2]
            shear = strain[3] * other[3] + strain[4] * other[4] + strain[5] * other[5]
            lam_part = div_a * div_f
            mu_part = diag + 0.5 * shear
            if not first:
                lam_part = ksum[0, a] + lam_part
                mu_part = ksum[1, a] + mu_part
            ksum[0, a] = lam_part
            ksum[1, a] = mu_part

    def kept(which):
        return lambda a: [strains[which, a, i] for i in range(6)]

    delta[...] = -minv[0] * held[...]
    set_ghost()
    add_kernels(astrains.at[2], lambda a: strain_at(1, a), True)
    add_kernels(astrains.at[1], kept(1), False)
    loads[14].wait()
    put_out(1, final_f_ref)

    close_face(2, 4, astrains.at[0])

    width = LANES // n_event

    def event_copy(hop):
        target = lax.rem(event + hop, n_event)
        return pltpu.make_async_remote_copy(
            src_ref=ev_s.at[:, pl.ds(pl.multiple_of(width * target, width), width)],
            dst_ref=ev_r.at[hop - 1],
            send_sem=s_ev.at[hop - 1],
            recv_sem=r_ev.at[hop - 1],
            device_id={"event": target},
        )

    def send_kernels():
        scales = (-time_step, -2.0 * time_step)
        for which, modulus_ref in enumerate((lam_ref, mu_ref)):
            value = ksum[which]
            turned_back = jnp.stack([value[4 - a] for a in range(5)], axis=0)
            value = pick(low4, value, turned_back).reshape(200, LANES)
            natural = move_left_t(rows_ref[...], value)
            ev_s[which] = jnp.transpose(natural * (scales[which] * modulus_ref[...]))
        for hop in range(1, n_event):
            event_copy(hop).start()

    add_kernels(astrains.at[0], kept(0), False)
    send_kernels()
    close_step(2, 3, stress, 5, lambda a: first_load[:, a])
    put_out(3, final_a_ref)

    mine = pl.ds(pl.multiple_of(width * event, width), width)
    total = ev_s[:, mine]
    for hop in range(1, n_event):
        event_copy(hop).wait_recv()
        total = total + ev_r[hop - 1]
    out_ref[...] = total

    @pl.when(has_up)
    def _():
        for index in range(4):
            halo_copy(index).wait_send()
        up_copy(mat_us, mat_ur, mat_slot).wait_send()
        for slot in range(n_face):
            up_copy(up_s.at[slot], up_r.at[slot], slot).wait_send()

    @pl.when(has_down)
    def _():
        down_copy(mat_ds, mat_dr, mat_slot).wait_send()
        for slot in range(n_face):
            down_copy(down_s.at[slot], down_r.at[slot], slot).wait_send()

    for hop in range(1, n_event):
        event_copy(hop).wait_send()


def write_out(first, second, third, first_out, second_out, third_out, sems):
    copies = [
        pltpu.make_async_copy(source, target, sems.at[place])
        for place, (source, target) in enumerate(
            ((first, first_out), (second, second_out), (third, third_out))
        )
    ]
    for copy in copies:
        copy.start()
    for copy in copies:
        copy.wait()


def on_device(
    n_mesh,
    n_event,
    forward_before,
    forward_now,
    adjoint_after,
    adjoint_now,
    mass_density,
    lame_lambda,
    lame_mu,
    source_element,
    source_offset,
    source_force,
    receiver_element,
    receiver_offset,
    receiver_data,
):
    assert forward_now.shape[1:] == (3, 8, 8, 128)
    assert lame_mu.shape == (125, 128)
    steps = source_force.shape[1]
    assert steps == 3
    field = forward_now.shape
    vmem = pl.BlockSpec(memory_space=pltpu.VMEM)
    hbm = pl.BlockSpec(memory_space=pltpu.HBM)
    f32 = jnp.float32
    elem = (5, 5, 8, LANES)
    faces = (6, 3, 2, 8, LANES)
    copied = (
        forward_now,
        forward_before,
        adjoint_now,
        adjoint_after,
        mass_density,
        lame_lambda,
        lame_mu,
        receiver_element,
        receiver_offset.transpose(2, 0, 1),
        receiver_data.transpose(1, 3, 0, 2),
    ) + constants()
    small = (source_offset, source_force.transpose(1, 0, 2))
    results = pl.pallas_call(
        functools.partial(kernel, n_mesh, n_event, steps),
        out_shape=(
            pltpu.VMEM(field, f32),
            pltpu.VMEM(field, f32),
            pltpu.VMEM((2, LANES // n_event, 125), f32),
        ),
        in_specs=[hbm] * 17 + [pl.BlockSpec(memory_space=pltpu.SMEM)],
        out_specs=(vmem, vmem, vmem),
        scratch_shapes=[pltpu.VMEM(value.shape, value.dtype) for value in copied]
        + [pltpu.SMEM(value.shape, value.dtype) for value in small]
        + [
            pltpu.SemaphoreType.DMA((len(copied) + len(small),)),
            pltpu.VMEM((4, 3) + elem, f32),
            pltpu.VMEM((6,) + elem, f32),
            pltpu.VMEM((6,) + elem, f32),
            pltpu.VMEM((3,) + elem[1:], f32),
            pltpu.VMEM((3,) + elem[1:], f32),
            pltpu.VMEM((3,) + elem[1:], f32),
            pltpu.VMEM(elem, f32),
            pltpu.VMEM((steps, 3) + elem, f32),
            pltpu.VMEM(elem, f32),
            pltpu.VMEM((3,) + elem, f32),
            pltpu.VMEM((2, 5, 6, 5, 8, LANES), f32),
            pltpu.VMEM((3, 5, 6, 5, 8, LANES), f32),
            pltpu.VMEM((2,) + elem, f32),
            pltpu.VMEM(elem, f32),
            pltpu.VMEM(elem, f32),
            pltpu.VMEM(elem, f32),
            pltpu.VMEM((4,) + elem[1:], f32),
            pltpu.VMEM((3,) + elem[1:], f32),
            pltpu.VMEM((4, 3, 8, LANES), f32),
            pltpu.VMEM((4, 3) + elem[1:], f32),
            pltpu.VMEM((12, 8, LANES), f32),
            pltpu.VMEM((12, 8, LANES), f32),
            pltpu.VMEM((12, 8, LANES), f32),
            pltpu.VMEM((12, 8, LANES), f32),
            pltpu.VMEM(faces, f32),
            pltpu.VMEM(faces, f32),
            pltpu.VMEM(faces, f32),
            pltpu.VMEM(faces, f32),
            pltpu.VMEM((2, LANES, 125), f32),
            pltpu.VMEM((max(1, n_event - 1), 2, LANES // n_event, 125), f32),
            pltpu.SemaphoreType.DMA((11,)),
            pltpu.SemaphoreType.DMA((11,)),
            pltpu.SemaphoreType.DMA((7,)),
            pltpu.SemaphoreType.DMA((7,)),
            pltpu.SemaphoreType.DMA((max(1, n_event - 1),)),
            pltpu.SemaphoreType.DMA((max(1, n_event - 1),)),
        ],
        compiler_params=pltpu.CompilerParams(
            collective_id=0, has_side_effects=True, vmem_limit_bytes=32 * 1024 * 1024
        ),
    )(
        *(
            pltpu.with_memory_space_constraint(value, pltpu.HBM)
            for value in copied + small
        ),
        source_element,
    )
    final_f, final_a, kernels = pl.pallas_call(
        write_out,
        out_shape=tuple(
            jax.ShapeDtypeStruct(value.shape, value.dtype) for value in results
        ),
        in_specs=[vmem] * 3,
        out_specs=(hbm, hbm, hbm),
        scratch_shapes=[pltpu.SemaphoreType.DMA((3,))],
    )(*(pltpu.with_memory_space_constraint(value, pltpu.VMEM) for value in results))
    return (final_f, final_a, kernels.transpose(0, 2, 1))


def solution(mesh):
    return jax.shard_map(
        functools.partial(on_device, mesh.shape["mesh"], mesh.shape["event"]),
        mesh=mesh,
        in_specs=(
            P("event", None, "mesh", None, None),
            P("event", None, "mesh", None, None),
            P("event", None, "mesh", None, None),
            P("event", None, "mesh", None, None),
            P(None, "mesh"),
            P(None, "mesh"),
            P(None, "mesh"),
            P("event"),
            P("event", None),
            P("event", None, None),
            P("event", None),
            P("event", None, None),
            P("event", None, None, None),
        ),
        out_specs=(
            P("event", None, "mesh", None, None),
            P("event", None, "mesh", None, None),
            P(None, None, ("mesh", "event")),
        ),
        check_vma=False,
    )
```

```python
import functools
import math

import jax
import jax.numpy as jnp
import numpy as np
from jax import lax
from jax.experimental import pallas as pl
from jax.experimental.pallas import tpu as pltpu
from jax.sharding import PartitionSpec as P

time_step = 0.04
adjoint_gain = 25.0
LANES = 128


def numpy_tables():
    gll_points = np.array([-1.0, -math.sqrt(3.0 / 7.0), 0.0, math.sqrt(3.0 / 7.0), 1.0])
    legendre = (35.0 * gll_points**4 - 30.0 * gll_points**2 + 3.0) / 8.0
    deriv_table = np.zeros((5, 5))
    for row_q in range(5):
        for col_k in range(5):
            if row_q != col_k:
                deriv_table[row_q, col_k] = legendre[row_q] / (
                    legendre[col_k] * (gll_points[row_q] - gll_points[col_k])
                )
    deriv_table[0, 0] = -5.0
    deriv_table[4, 4] = 5.0
    gll_weights = np.array([0.1, 49.0 / 90.0, 32.0 / 45.0, 49.0 / 90.0, 0.1])
    return (deriv_table, gll_weights)


DERIV, WEIGHTS = numpy_tables()


def constants():
    spread = np.zeros((4, LANES, 4, 4, 32), np.float32)
    for j in range(4):
        for ex in range(32):
            for c in range(4):
                spread[j, 4 * ex + c, c, j, ex] = 1.0
    spread = spread.reshape(512, 512)
    rows = np.zeros((5, 5, 8, 125), np.float32)
    cube = np.zeros((5, 5, 8, LANES), np.float32)
    for a in range(5):
        for b in range(5):
            for c in range(5):
                rows[a, c, b, (a * 5 + b) * 5 + c] = 1.0
                cube[a, c, b, :] = WEIGHTS[a] * WEIGHTS[b] * WEIGHTS[c]
    rows = rows.reshape(200, 125)
    dy = np.zeros((2, 5, 8, LANES), np.float32)
    for k in range(5):
        for b in range(5):
            dy[0, k, b, :] = DERIV[b, k]
            dy[1, k, b, :] = DERIV[k, b]
    bf = jnp.bfloat16
    return (
        jnp.asarray(spread, bf),
        jnp.asarray(np.ascontiguousarray(spread.T), bf),
        jnp.asarray(rows, bf),
        jnp.asarray(cube),
        jnp.asarray(dy),
    )


def split3(value):
    high = value.astype(jnp.bfloat16)
    rest = value - high.astype(jnp.float32)
    middle = rest.astype(jnp.bfloat16)
    low = (rest - middle.astype(jnp.float32)).astype(jnp.bfloat16)
    return (high, middle, low)


def dot(left, right):
    return jnp.dot(left, right, preferred_element_type=jnp.float32)


def move_right(values, table):
    parts = split3(values)
    count = values.shape[0]
    stacked = jnp.concatenate(parts, axis=0)
    moved = dot(stacked, table)
    return moved[0:count] + moved[count : 2 * count] + moved[2 * count : 3 * count]


def move_left(table, values):
    high, middle, low = split3(values)
    return dot(table, high) + dot(table, middle) + dot(table, low)


def move_left_t(table, values):
    contract = (((0,), (0,)), ((), ()))
    return sum(
        lax.dot_general(table, part, contract, preferred_element_type=jnp.float32)
        for part in split3(values)
    )


def roll_lane(value, shift):
    return pltpu.roll(value, shift % LANES, value.ndim - 1)


def lane_iota(ndim):
    return lax.broadcasted_iota(jnp.int32, (1,) * (ndim - 1) + (LANES,), ndim - 1)


def sub_iota(ndim):
    return lax.broadcasted_iota(jnp.int32, (1,) * (ndim - 2) + (8, LANES), ndim - 2)


def pick(mask, first, second):
    return jnp.where(jnp.broadcast_to(mask, first.shape), first, second)


def from_left(value):
    at_edge = lane_iota(value.ndim) % 32 == 0
    return pick(at_edge, roll_lane(value, -31), roll_lane(value, 1))


def from_right(value):
    at_edge = lane_iota(value.ndim) % 32 == 31
    return pick(at_edge, roll_lane(value, 31), roll_lane(value, -1))


def roll_sub(value):
    return pltpu.roll(value, 4, value.ndim - 2)


def assemble_xy(value):
    first = value[:, 0:1] + from_left(value[:, 4:5])
    value = jnp.concatenate([first, value[:, 1:4], from_right(first)], axis=1)
    swapped = roll_sub(value)
    other = pick(
        lane_iota(4) % 64 < 32, roll_lane(swapped, -32), roll_lane(swapped, 32)
    )
    return value + pick(sub_iota(4) % 4 == 0, other, jnp.zeros_like(other))


EDGE = float(DERIV[0, 0])
HALF = 64


def mix(coefs, planes):
    total = None
    for coef, plane in zip(coefs, planes):
        if coef != 0.0:
            term = float(coef) * plane
            total = term if total is None else total + term
    return total


def along_x(value, flipped=False):
    table = DERIV.T if flipped else DERIV
    rows = [value[k] for k in range(5)]
    return jnp.stack([mix(table[c], rows) for c in range(5)], axis=0)


def mirror(value):
    return jnp.concatenate([value[0:2], -value[2:3]], axis=0)


def low_lanes(ndim):
    return lane_iota(ndim) < HALF


def swap_half(value):
    return roll_lane(value, HALF)


def unpack(from_above, from_below):
    low = low_lanes(from_above.ndim)
    return (
        pick(low, from_above, swap_half(from_below)),
        pick(low, swap_half(from_above), from_below),
    )


def pack(first, second):
    low = low_lanes(first.ndim)
    return (
        pick(low, first, swap_half(second)),
        pick(low, swap_half(first), second),
    )


def kernel(
    n_mesh,
    n_event,
    steps,
    now_hbm,
    before_hbm,
    adj_hbm,
    after_hbm,
    rho_hbm,
    lam_hbm,
    mu_hbm,
    rec_elem_hbm,
    rec_off_hbm,
    data_hbm,
    spread_hbm,
    gather_hbm,
    rows_hbm,
    cube_hbm,
    dy_hbm,
    off_hbm,
    force_hbm,
    elem_ref,
    final_f_ref,
    final_a_ref,
    out_ref,
    now_ref,
    before_ref,
    adj_ref,
    after_ref,
    rho_ref,
    lam_ref,
    mu_ref,
    rec_elem_ref,
    rec_off_ref,
    data_ref,
    spread_ref,
    gather_ref,
    rows_ref,
    cube_ref,
    dy_ref,
    off_ref,
    force_ref,
    s_in,
    fields,
    stress,
    stress_a,
    held,
    ghost,
    delta,
    count_map,
    data_map,
    source_map,
    first_load,
    strains,
    astrains,
    ksum,
    clam,
    cmu,
    minv,
    ghost_mat,
    work,
    halo_r,
    halo_e,
    mat_us,
    mat_ur,
    mat_ds,
    mat_dr,
    up_s,
    up_r,
    down_s,
    down_r,
    ev_s,
    ev_r,
    ev_t,
    side_s,
    side_r,
    first_s,
    first_r,
    first_own,
    s_up,
    r_up,
    s_down,
    r_down,
    s_ev,
    r_ev,
    s_pair,
    r_pair,
):
    me = lax.axis_index("mesh")
    event = lax.axis_index("event")
    has_up = me > 0
    has_down = me < n_mesh - 1

    barrier = pltpu.get_barrier_semaphore()

    @pl.when(has_up)
    def _():
        pl.semaphore_signal(barrier, inc=1, device_id={"mesh": me - 1})

    @pl.when(has_down)
    def _():
        pl.semaphore_signal(barrier, inc=1, device_id={"mesh": me + 1})

    for hop in range(1, n_event):
        pl.semaphore_signal(
            barrier, inc=1, device_id={"event": lax.rem(event + hop, n_event)}
        )

    paired = n_event == 2
    has_side = jnp.where(event == 0, me, n_mesh - 1 - me) > 0
    side_device = {"event": 1 - event, "mesh": me - 1 + 2 * event}
    if paired:

        @pl.when(has_side)
        def _():
            pl.semaphore_signal(barrier, inc=1, device_id=side_device)

    loads = []
    pairs = (
        (rows_hbm, rows_ref),
        (lam_hbm, lam_ref),
        (mu_hbm, mu_ref),
        (rho_hbm, rho_ref),
        (cube_hbm, cube_ref),
        (now_hbm, now_ref),
        (before_hbm, before_ref),
        (adj_hbm, adj_ref),
        (after_hbm, after_ref),
        (spread_hbm, spread_ref),
        (dy_hbm, dy_ref),
        (rec_elem_hbm, rec_elem_ref),
        (rec_off_hbm, rec_off_ref),
        (data_hbm, data_ref),
        (gather_hbm, gather_ref),
        (off_hbm, off_ref),
        (force_hbm, force_ref),
    )
    for place, (source, target) in enumerate(pairs):
        load_copy = pltpu.make_async_copy(source, target, s_in.at[place])
        load_copy.start()
        loads.append(load_copy)

    def up_copy(source, target, slot):
        return pltpu.make_async_remote_copy(
            src_ref=source, dst_ref=target, send_sem=s_up.at[slot],
            recv_sem=r_up.at[slot], device_id={"mesh": me - 1},
        )

    def down_copy(source, target, slot):
        return pltpu.make_async_remote_copy(
            src_ref=source, dst_ref=target, send_sem=s_down.at[slot],
            recv_sem=r_down.at[slot], device_id={"mesh": me + 1},
        )

    n_face = 6
    mat_slot = n_face
    halo_slot = n_face + 1

    def start_both(up, down):
        @pl.when(has_up)
        def _():
            up.start()

        @pl.when(has_down)
        def _():
            down.start()

    def wait_both(up, down):
        @pl.when(has_down)
        def _():
            up.wait_recv()

        @pl.when(has_up)
        def _():
            down.wait_recv()

    @pl.when(jnp.logical_not(has_down))
    def _():
        halo_r[...] = jnp.zeros_like(halo_r)
        up_r[...] = jnp.zeros_like(up_r)
        mat_ur[...] = jnp.zeros_like(mat_ur)

    if paired:

        @pl.when(jnp.logical_not(has_side))
        def _():
            side_r[...] = jnp.zeros_like(side_r)

    @pl.when(jnp.logical_not(has_up))
    def _():
        down_r[...] = jnp.zeros_like(down_r)
        mat_dr[...] = jnp.zeros_like(mat_dr)

    pl.semaphore_wait(
        barrier,
        jnp.where(has_up, 1, 0)
        + jnp.where(has_down, 1, 0)
        + (n_event - 1)
        + (jnp.where(has_side, 1, 0) if paired else 0),
    )
    tops = (now_hbm, before_hbm, adj_hbm, after_hbm)

    def halo_copy(index):
        return up_copy(
            tops[index].at[0, :, 0], halo_r.at[index], halo_slot + index
        )

    @pl.when(has_up)
    def _():
        for index in range(4):
            halo_copy(index).start()

    low4 = low_lanes(4)

    for place in range(5):
        loads[place].wait()
    materials = jnp.concatenate([lam_ref[...], mu_ref[...], rho_ref[...]], axis=1)
    moved = move_left(rows_ref[...], materials)
    cube = cube_ref[...]

    def modulus(which):
        value = moved[:, which * LANES : (which + 1) * LANES].reshape(5, 5, 8, LANES)
        turned = jnp.stack([value[4 - a] for a in range(5)], axis=0)
        return pick(low4, value, turned) * cube

    lam_value = modulus(0)
    mu_value = modulus(1)
    clam[...] = lam_value
    cmu[...] = mu_value
    mass = modulus(2)
    mass = [assemble_xy(mass[a : a + 1])[0] for a in range(5)]
    mass[4] = mass[4] + swap_half(mass[4])

    def set_minv(a, value):
        keep = sub_iota(3) < 5
        if a == 0:
            keep = keep & (low_lanes(3) | has_down)
        keep = jnp.broadcast_to(keep, value.shape)
        safe = jnp.where(keep, value, 1.0)
        minv[a] = jnp.where(keep, time_step**2 / safe, 0.0)

    for a in range(1, 5):
        set_minv(a, mass[a])

    squares = [float(DERIV[q, 0]) ** 2 for q in range(5)]
    diag_mu = mix(squares[1:], [mu_value[q] for q in range(1, 5)])
    diag_lam = mix(squares[1:], [lam_value[q] for q in range(1, 5)])
    diag_lam = diag_lam + (diag_mu + diag_mu)
    listed = [mass[0][c] for c in range(4)]
    for value in (lam_value[0], mu_value[0], diag_mu, diag_lam):
        listed += [value[c] for c in range(5)]
    for pair in range(12):
        up, down = pack(listed[2 * pair], listed[2 * pair + 1])
        mat_us[pair] = up
        mat_ds[pair] = down

    start_both(up_copy(mat_us, mat_ur, mat_slot), down_copy(mat_ds, mat_dr, mat_slot))

    for place in range(5, 11):
        loads[place].wait()
    inputs = (now_ref, before_ref, adj_ref, after_ref)

    def bring_in(index):
        ref = inputs[index]
        upper = ref[0, :, 0:5]
        lower = mirror(
            jnp.stack(
                [jnp.zeros((3, 8, LANES), jnp.float32)]
                + [ref[0, :, 8 - a] for a in range(1, 5)],
                axis=1,
            )
        )
        parts = []
        for layer in (upper, lower):
            for shifted in (layer, roll_sub(layer)):
                parts.append(shifted.reshape(120, LANES))
        moved = move_right(jnp.concatenate(parts, axis=1), spread_ref[...])
        for c in range(4):
            fields[index, :, :, c] = moved[:, c * LANES : (c + 1) * LANES].reshape(
                3, 5, 8, LANES
            )
        fields[index, :, :, 4] = from_right(
            moved[:, 0:LANES].reshape(3, 5, 8, LANES)
        )

    def bring_halos():
        @pl.when(has_down)
        def _():
            for index in range(4):
                halo_copy(index).wait_recv()

        planes = jnp.stack([halo_r[:, 0], halo_r[:, 1], -halo_r[:, 2]], axis=1)
        parts = [
            planes.reshape(96, LANES),
            roll_sub(planes).reshape(96, LANES),
        ]
        moved = move_right(
            jnp.concatenate(parts, axis=1), spread_ref[2 * LANES : 4 * LANES]
        )
        for c in range(5):
            part = moved[:, (c % 4) * LANES : (c % 4 + 1) * LANES]
            part = part.reshape(4, 3, 8, LANES)
            if c == 4:
                part = from_right(part)
            halo_e[:, :, c] = part
            fields[0:3, :, 0, c] = fields[0:3, :, 0, c] + part[0:3]

    def owned(ndim):
        return jnp.where(lane_iota(ndim) < HALF, 0, 1) == event

    def side_copy():
        return pltpu.make_async_remote_copy(
            src_ref=side_s, dst_ref=side_r, send_sem=s_pair.at[0],
            recv_sem=r_pair.at[0], device_id=side_device,
        )

    def first_copy():
        return pltpu.make_async_remote_copy(
            src_ref=first_s, dst_ref=first_r, send_sem=s_pair.at[1],
            recv_sem=r_pair.at[1], device_id={"event": 1 - event},
        )

    def send_first():
        if not paired:
            return
        mine = owned(3)
        for a in range(5):
            first_own[:, a] = fields[1, :, a]
            for pair in range(2):
                first = fields[1, :, a, 2 * pair]
                second = fields[1, :, a, 2 * pair + 1]
                first_s[:, a, pair] = pick(mine, swap_half(second), first)
        first_copy().start()

    def take_first():
        first_copy().wait_recv()
        mine = owned(3)
        for a in range(5):
            for pair in range(2):
                packed = first_r[:, a, pair]
                for c, other in ((2 * pair, swap_half(packed)), (2 * pair + 1, packed)):
                    value = pick(mine, first_own[:, a, c], other)
                    fields[4, :, a, c] = value
                    if c == 0:
                        fields[4, :, a, 4] = from_right(value)
        for a in range(5):
            strain = strain_at(4, a)
            for i in range(6):
                strains[2, a, i] = strain[i]

    def send_side(slot):
        if not paired:
            return
        side_s[...] = jnp.where(event == 0, up_s[slot], down_s[slot])

        @pl.when(has_side)
        def _():
            side_copy().start()

    def paired_delta(own):
        @pl.when(has_side)
        def _():
            side_copy().wait_recv()

        sides = []
        for pair in range(2):
            packed = side_r[:, pair]
            turned = swap_half(packed)
            sides += [
                jnp.where(event == 0, turned, packed),
                jnp.where(event == 0, packed, turned),
            ]
        sides.append(from_right(sides[0]))
        other = mirror(jnp.stack(sides, axis=1))
        mine = owned(3)
        scale = pick(mine, minv[0], swap_half(minv[0]))
        return pick(owned(4), own, -scale * other)

    def along_y(value, flipped=False):
        total = None
        for k in range(5):
            row = jnp.broadcast_to(value[..., k : k + 1, :], value.shape)
            term = dy_ref[1 if flipped else 0, k] * row
            total = term if total is None else total + term
        return total

    def send(slot, value):
        for pair in range(2):
            up, down = pack(value[:, 2 * pair], value[:, 2 * pair + 1])
            up_s[slot, :, pair] = up
            down_s[slot, :, pair] = down
        start_both(
            up_copy(up_s.at[slot], up_r.at[slot], slot),
            down_copy(down_s.at[slot], down_r.at[slot], slot),
        )

    def receive(slot):
        wait_both(
            up_copy(up_s.at[slot], up_r.at[slot], slot),
            down_copy(down_s.at[slot], down_r.at[slot], slot),
        )
        sides = []
        for pair in range(2):
            sides += unpack(down_r[slot, :, pair], up_r[slot, :, pair])
        sides.append(from_right(sides[0]))
        return mirror(jnp.stack(sides, axis=1))

    def along_z(index, comp, a, first=0):
        return mix(
            DERIV[a, first:], [fields[index, comp, k] for k in range(first, 5)]
        )

    def strain_at(index, a):
        u = [fields[index, comp, a] for comp in range(3)]
        gz = [along_z(index, comp, a) for comp in range(3)]
        return (
            along_x(u[0]),
            along_y(u[1]),
            gz[2],
            along_y(u[0]) + along_x(u[1]),
            gz[0] + along_x(u[2]),
            gz[1] + along_y(u[2]),
        )

    def set_ghost():
        u = [delta[comp] for comp in range(3)]
        gz = [-EDGE * value for value in u]
        lam_g, mu_g = ghost_mat[0], ghost_mat[1]
        xx = along_x(u[0])
        yy = along_y(u[1])
        zz = gz[2]
        side = lam_g * (xx + yy + zz)
        mu_two = mu_g + mu_g
        xx = side + mu_two * xx
        yy = side + mu_two * yy
        zz = side + mu_two * zz
        xy = mu_g * (along_y(u[0]) + along_x(u[1]))
        xz = mu_g * (gz[0] + along_x(u[2]))
        yz = mu_g * (gz[1] + along_y(u[2]))
        work[0] = xy
        work[1] = yy
        work[2] = yz
        values = (
            along_x(xx, True)
            + along_y(work[0], True)
            - EDGE * xz
            + ghost_mat[2] * u[0],
            along_x(xy, True)
            + along_y(work[1], True)
            - EDGE * yz
            + ghost_mat[2] * u[1],
            along_x(xz, True)
            + along_y(work[2], True)
            - EDGE * zz
            + ghost_mat[3] * u[2],
        )
        ghost[...] = assemble_xy(jnp.stack(values, axis=0))

    def put_stress(target, a, strain, add):
        lam_div = clam[a] * (strain[0] + strain[1] + strain[2])
        mu_a = cmu[a]
        mu_two = mu_a + mu_a
        for i in range(3):
            value = lam_div + mu_two * strain[i]
            target[i, a] = target[i, a] + value if add else value
            value = mu_a * strain[3 + i]
            target[3 + i, a] = target[3 + i, a] + value if add else value

    def make_stress(index, target, keep_strain):
        for a in range(5):
            strain = strain_at(index, a)
            put_stress(target, a, strain, False)
            if keep_strain is not None:
                for i in range(6):
                    keep_strain[a, i] = strain[i]

    def face_strain():
        u = [delta[comp] for comp in range(3)]
        return (
            along_x(u[0]),
            along_y(u[1]),
            EDGE * u[2],
            along_y(u[0]) + along_x(u[1]),
            EDGE * u[0] + along_x(u[2]),
            EDGE * u[1] + along_y(u[2]),
        )

    def add_face(target, keep_strain):
        strain = face_strain()
        put_stress(target, 0, strain, True)
        if keep_strain is not None:
            for i in range(6):
                keep_strain[0, i] = keep_strain[0, i] + strain[i]
        for q in range(1, 5):
            gz = [float(DERIV[q, 0]) * delta[comp] for comp in range(3)]
            mu_q = cmu[q]
            side = clam[q] * gz[2]
            target[0, q] = target[0, q] + side
            target[1, q] = target[1, q] + side
            target[2, q] = target[2, q] + (side + (mu_q + mu_q) * gz[2])
            target[4, q] = target[4, q] + mu_q * gz[0]
            target[5, q] = target[5, q] + mu_q * gz[1]
            if keep_strain is not None:
                keep_strain[q, 2] = keep_strain[q, 2] + gz[2]
                keep_strain[q, 4] = keep_strain[q, 4] + gz[0]
                keep_strain[q, 5] = keep_strain[q, 5] + gz[1]

    pairs_of = ((0, 3, 4), (3, 1, 5), (4, 5, 2))

    def both_layers(value):
        return value + mirror(swap_half(value))

    def plane_force(source, a):
        values = []
        for comp in range(3):
            ix, iy, iz = pairs_of[comp]
            total = along_x(source[ix, a], True) + along_y(source[iy, a], True)
            values.append(total + mix(DERIV[:, a], [source[iz, q] for q in range(5)]))
        value = assemble_xy(jnp.stack(values, axis=0))
        return both_layers(value) if a == 4 else value

    def advance(index, older, a, value, load):
        if load is not None:
            value = value - load(a)
        fields[older, :, a] = (
            2.0 * fields[index, :, a] - fields[older, :, a]
        ) - minv[a] * value

    def inside_planes(index, older, source, load):
        for a in range(1, 5):
            advance(index, older, a, plane_force(source, a), load)

    def close_step(index, older, source, slot, load):
        inside_planes(index, older, source, load)
        close_outer(index, older, source, slot, load)

    def close_outer(index, older, source, slot, load):
        value = plane_force(source, 0) + ghost[...]
        advance(index, older, 0, value + receive(slot), load)

    def open_step(index, older, slot, load):
        held[...] = plane_force(stress, 0)
        send(slot, held[...])
        if slot == 4:
            send_side(slot)
        inside_planes(index, older, stress, load)
        advance(index, older, 0, held[...], load)

    def add_correction(which):
        strain = face_strain()
        for a in range(5):
            other = [strains[which, a, i] for i in range(6)]
            div_f = other[0] + other[1] + other[2]
            if a == 0:
                lam_part = (strain[0] + strain[1] + strain[2]) * div_f
                mu_part = (
                    strain[0] * other[0] + strain[1] * other[1] + strain[2] * other[2]
                ) + 0.5 * (
                    strain[3] * other[3] + strain[4] * other[4] + strain[5] * other[5]
                )
            else:
                gz = [float(DERIV[a, 0]) * delta[comp] for comp in range(3)]
                lam_part = gz[2] * div_f
                mu_part = gz[2] * other[2] + 0.5 * (gz[0] * other[4] + gz[1] * other[5])
            if which == 2:
                lam_part = lam_part + swap_half(lam_part)
                mu_part = mu_part + swap_half(mu_part)
            ksum[0, a] = ksum[0, a] + lam_part
            ksum[1, a] = ksum[1, a] + mu_part

    def close_face(older, slot, keep_strain):
        delta[...] = -minv[0] * receive(slot)
        fields[older, :, 0] = fields[older, :, 0] + delta[...]
        add_face(stress, keep_strain)

    bring_in(0)
    make_stress(0, stress, None)
    send(0, plane_force(stress, 0))
    bring_in(2)
    make_stress(2, stress_a, astrains.at[2])
    send(1, plane_force(stress_a, 0))
    bring_in(1)
    for place in range(15, 17):
        loads[place].wait()
    src_local = elem_ref[0] - LANES * me
    src_depth = off_ref[0, 0]
    src_in = (src_local >= 0) & (src_local < LANES)
    src_over = (src_local >= -HALF) & (src_local < 0) & (src_depth == 4)
    src_under = (src_local >= LANES) & (src_local < LANES + HALF) & (src_depth == 0)
    src_lane = jnp.where(
        src_in,
        src_local,
        jnp.where(
            src_over, src_local + HALF, jnp.where(src_under, src_local - HALF, -1)
        ),
    )
    src_depth = jnp.where(
        src_in, jnp.where(src_local < HALF, src_depth, 4 - src_depth), 0
    )
    src_row = src_depth * 40 + off_ref[0, 2] * 8 + off_ref[0, 1]

    shape = (5, 8, LANES)
    src_lanes = lax.broadcasted_iota(jnp.int32, shape, 2) == src_lane
    src_rows = lax.broadcasted_iota(jnp.int32, shape, 0) * 8 + lax.broadcasted_iota(
        jnp.int32, shape, 1
    )
    for a in range(5):
        source_at = jnp.where(src_lanes & (src_rows + 40 * a == src_row), 1.0, 0.0)
        value = assemble_xy(source_at[None])[0]
        source_map[a] = value + swap_half(value) if a == 4 else value

    def make_maps():
        for place in range(11, 14):
            loads[place].wait()
        nrec = rec_elem_ref.shape[1]
        local = rec_elem_ref[...] - LANES * me
        depth = rec_off_ref[0]
        in_slab = (local >= 0) & (local < LANES)
        over = (local >= -HALF) & (local < 0) & (depth == 4)
        under = (local >= LANES) & (local < LANES + HALF) & (depth == 0)
        rec_at = jnp.where(
            in_slab,
            local,
            jnp.where(over, local + HALF, jnp.where(under, local - HALF, -1)),
        )
        depth = jnp.where(
            in_slab, jnp.where(local < HALF, depth, 4 - depth), jnp.zeros_like(depth)
        )
        lane_t = lax.broadcasted_iota(jnp.int32, (LANES, nrec), 0) == rec_at
        lane_t = jnp.where(lane_t, 1.0, 0.0).astype(jnp.bfloat16)
        eye = jnp.where(
            lax.broadcasted_iota(jnp.int32, (nrec, nrec), 0)
            == lax.broadcasted_iota(jnp.int32, (nrec, nrec), 1),
            1.0,
            0.0,
        ).astype(jnp.bfloat16)
        turned = (((1,), (1,)), ((), ()))

        def turn(part):
            return lax.dot_general(eye, part, turned, preferred_element_type=jnp.float32)

        rec_lane = turn(lane_t)
        rec_lanes = (rec_lane, rec_lane, pick(low_lanes(2), rec_lane, -rec_lane))
        row = depth * 40 + rec_off_ref[2] * 8 + rec_off_ref[1]
        rows_lanes = lax.broadcasted_iota(jnp.int32, (200, nrec), 0) == row
        rows_lanes = jnp.where(rows_lanes, 1.0, 0.0).astype(jnp.bfloat16)
        observed = jnp.concatenate(
            [data_ref[n, comp] for n in range(steps) for comp in range(3)], axis=0
        )
        observed = sum(turn(part) for part in split3(observed))

        scaled = adjoint_gain * observed
        columns = jnp.concatenate(
            [
                scaled[:, 3 * moment + comp : 3 * moment + comp + 1] * rec_lanes[comp]
                for moment in range(steps)
                for comp in range(3)
            ],
            axis=1,
        )
        at_points = sum(dot(rows_lanes, part) for part in split3(columns))
        counts = adjoint_gain * dot(rows_lanes, rec_lane.astype(jnp.bfloat16))
        for a in range(5):
            count_at = counts[40 * a : 40 * a + 40].reshape(shape)
            data_at = [
                at_points[40 * a : 40 * a + 40, LANES * i : LANES * (i + 1)].reshape(shape)
                for i in range(3 * steps)
            ]
            value = assemble_xy(jnp.stack([count_at] + data_at, axis=0))
            if a == 4:
                other = swap_half(value)
                value = value + jnp.stack(
                    [
                        -other[i] if i > 0 and i % 3 == 0 else other[i]
                        for i in range(1 + 3 * steps)
                    ],
                    axis=0,
                )
            count_map[a] = value[0]
            for moment in range(steps):
                data_map[moment, :, a] = value[1 + 3 * moment : 4 + 3 * moment]

    def source_load(moment):
        forces = [force_ref[moment, 0, comp] for comp in range(3)]
        lane = lax.broadcasted_iota(jnp.int32, (8, LANES), 1)
        forces[2] = jnp.where(lane < HALF, forces[2], -forces[2])
        return lambda a: jnp.stack(
            [source_map[a] * forces[comp] for comp in range(3)], axis=0
        )

    def receiver_load(index, moment):
        return (
            lambda a: count_map[a][None] * fields[index, :, a] - data_map[moment, :, a]
        )

    bring_halos()
    delta[...] = halo_e[0]
    add_face(stress, None)
    inside_planes(0, 1, stress, source_load(0))

    wait_both(up_copy(mat_us, mat_ur, mat_slot), down_copy(mat_ds, mat_dr, mat_slot))
    listed = []
    for pair in range(12):
        listed += unpack(mat_dr[pair], mat_ur[pair])
    for which in range(4):
        for c in range(5):
            ghost_mat[which, c] = listed[4 + 5 * which + c]
    face_mass = listed[0:4]
    set_minv(0, mass[0] + jnp.stack(face_mass + [from_right(face_mass[0])], axis=0))

    def ghost_of_start(index):
        top = fields[index, :, 0]
        delta[...] = pick(low4, top, jnp.zeros_like(top))
        set_ghost()

    ghost_of_start(0)
    close_outer(0, 1, stress, 0, source_load(0))

    make_stress(1, stress, strains.at[0])
    open_step(1, 0, 2, source_load(1))
    make_stress(0, stress, strains.at[1])
    send(3, plane_force(stress, 0))

    send_first()
    make_maps()
    bring_in(3)
    fields[3, :, 0] = fields[3, :, 0] + halo_e[3]
    delta[...] = halo_e[2]
    add_face(stress_a, astrains.at[2])
    ghost_of_start(2)
    close_step(2, 3, stress_a, 1, None)
    load = receiver_load(1, 0)
    for a in range(5):
        first_load[:, a] = load(a)
        fields[3, :, a] = fields[3, :, a] - minv[a] * data_map[2, :, a]
    delta[...] = -minv[0] * held[...]
    set_ghost()

    close_face(0, 2, strains.at[1])
    close_step(0, 1, stress, 3, source_load(2))

    for a in range(5):
        fields[3, :, a] = fields[3, :, a] + minv[a] * (
            count_map[a][None] * fields[1, :, a]
        )
    make_stress(3, stress, astrains.at[1])
    open_step(3, 2, 4, receiver_load(0, 1))
    make_stress(2, stress, astrains.at[0])

    def put_out(index, ref):
        sides = []
        for c in range(4):
            upper = fields[index, :, 0:4, c]
            lower = mirror(
                jnp.stack([fields[index, :, 4 - i, c] for i in range(4)], axis=1)
            )
            sides.append(pick(low4, upper, lower).reshape(96, LANES))
        moved = move_right(jnp.concatenate(sides, axis=1), gather_ref[...])
        for ez in range(2):
            first = moved[:, 2 * ez * LANES : (2 * ez + 1) * LANES]
            second = moved[:, (2 * ez + 1) * LANES : (2 * ez + 2) * LANES]
            first = first.reshape(3, 4, 8, LANES)
            second = roll_sub(second.reshape(3, 4, 8, LANES))
            ref[0, :, 4 * ez : 4 * ez + 4] = pick(sub_iota(4) < 4, first, second)

    def add_kernels(adjoint, other_at, first):
        for a in range(5):
            strain = [adjoint[a, i] for i in range(6)]
            other = other_at(a)
            div_a = strain[0] + strain[1] + strain[2]
            div_f = other[0] + other[1] + other[2]
            diag = strain[0] * other[0] + strain[1] * other[1] + strain[2] * other[2]
            shear = strain[3] * other[3] + strain[4] * other[4] + strain[5] * other[5]
            lam_part = div_a * div_f
            mu_part = diag + 0.5 * shear
            if not first:
                lam_part = ksum[0, a] + lam_part
                mu_part = ksum[1, a] + mu_part
            ksum[0, a] = lam_part
            ksum[1, a] = mu_part

    def kept(which):
        return lambda a: [strains[which, a, i] for i in range(6)]

    width = LANES // n_event

    def event_copy(hop):
        target = lax.rem(event + hop, n_event)
        return pltpu.make_async_remote_copy(
            src_ref=ev_s.at[:, pl.ds(pl.multiple_of(width * target, width), width)],
            dst_ref=ev_r.at[hop - 1],
            send_sem=s_ev.at[hop - 1],
            recv_sem=r_ev.at[hop - 1],
            device_id={"event": target},
        )

    def natural_kernels(target):
        scales = (-time_step, -2.0 * time_step)
        for which, modulus_ref in enumerate((lam_ref, mu_ref)):
            value = ksum[which]
            turned_back = jnp.stack([value[4 - a] for a in range(5)], axis=0)
            value = pick(low4, value, turned_back).reshape(200, LANES)
            natural = move_left_t(rows_ref[...], value)
            target[which] = jnp.transpose(natural * (scales[which] * modulus_ref[...]))

    def send_kernels():
        natural_kernels(ev_s)
        for hop in range(1, n_event):
            event_copy(hop).start()

    add_kernels(astrains.at[2], lambda a: strain_at(1, a), True)
    add_kernels(astrains.at[1], kept(1), False)
    add_kernels(astrains.at[0], kept(0), False)
    if paired:
        send_kernels()
    send(5, plane_force(stress, 0))

    delta[...] = -minv[0] * held[...]
    set_ghost()
    if paired:
        take_first()
    loads[14].wait()
    put_out(1, final_f_ref)

    close_face(2, 4, None)
    if paired:
        delta[...] = paired_delta(delta[...])
        add_correction(2)
        natural_kernels(ev_t)
    else:
        add_correction(0)
        send_kernels()
    close_step(2, 3, stress, 5, lambda a: first_load[:, a])
    put_out(3, final_a_ref)

    mine = pl.ds(pl.multiple_of(width * event, width), width)
    total = ev_t[:, mine] if paired else ev_s[:, mine]
    for hop in range(1, n_event):
        event_copy(hop).wait_recv()
        total = total + ev_r[hop - 1]
    out_ref[...] = total

    @pl.when(has_up)
    def _():
        for index in range(4):
            halo_copy(index).wait_send()
        up_copy(mat_us, mat_ur, mat_slot).wait_send()
        for slot in range(n_face):
            up_copy(up_s.at[slot], up_r.at[slot], slot).wait_send()

    @pl.when(has_down)
    def _():
        down_copy(mat_ds, mat_dr, mat_slot).wait_send()
        for slot in range(n_face):
            down_copy(down_s.at[slot], down_r.at[slot], slot).wait_send()

    for hop in range(1, n_event):
        event_copy(hop).wait_send()

    if paired:
        first_copy().wait_send()

        @pl.when(has_side)
        def _():
            side_copy().wait_send()


def write_out(first, second, third, first_out, second_out, third_out, sems):
    copies = [
        pltpu.make_async_copy(source, target, sems.at[place])
        for place, (source, target) in enumerate(
            ((first, first_out), (second, second_out), (third, third_out))
        )
    ]
    for copy in copies:
        copy.start()
    for copy in copies:
        copy.wait()


def on_device(
    n_mesh,
    n_event,
    forward_before,
    forward_now,
    adjoint_after,
    adjoint_now,
    mass_density,
    lame_lambda,
    lame_mu,
    source_element,
    source_offset,
    source_force,
    receiver_element,
    receiver_offset,
    receiver_data,
):
    assert forward_now.shape[1:] == (3, 8, 8, 128)
    assert lame_mu.shape == (125, 128)
    steps = source_force.shape[1]
    assert steps == 3
    field = forward_now.shape
    vmem = pl.BlockSpec(memory_space=pltpu.VMEM)
    hbm = pl.BlockSpec(memory_space=pltpu.HBM)
    f32 = jnp.float32
    elem = (5, 5, 8, LANES)
    faces = (6, 3, 2, 8, LANES)
    copied = (
        forward_now,
        forward_before,
        adjoint_now,
        adjoint_after,
        mass_density,
        lame_lambda,
        lame_mu,
        receiver_element,
        receiver_offset.transpose(2, 0, 1),
        receiver_data.transpose(1, 3, 0, 2),
    ) + constants()
    small = (source_offset, source_force.transpose(1, 0, 2))
    results = pl.pallas_call(
        functools.partial(kernel, n_mesh, n_event, steps),
        out_shape=(
            pltpu.VMEM(field, f32),
            pltpu.VMEM(field, f32),
            pltpu.VMEM((2, LANES // n_event, 125), f32),
        ),
        in_specs=[hbm] * 17 + [pl.BlockSpec(memory_space=pltpu.SMEM)],
        out_specs=(vmem, vmem, vmem),
        scratch_shapes=[pltpu.VMEM(value.shape, value.dtype) for value in copied]
        + [pltpu.SMEM(value.shape, value.dtype) for value in small]
        + [
            pltpu.SemaphoreType.DMA((len(copied) + len(small),)),
            pltpu.VMEM((5, 3) + elem, f32),
            pltpu.VMEM((6,) + elem, f32),
            pltpu.VMEM((6,) + elem, f32),
            pltpu.VMEM((3,) + elem[1:], f32),
            pltpu.VMEM((3,) + elem[1:], f32),
            pltpu.VMEM((3,) + elem[1:], f32),
            pltpu.VMEM(elem, f32),
            pltpu.VMEM((steps, 3) + elem, f32),
            pltpu.VMEM(elem, f32),
            pltpu.VMEM((3,) + elem, f32),
            pltpu.VMEM((3, 5, 6, 5, 8, LANES), f32),
            pltpu.VMEM((3, 5, 6, 5, 8, LANES), f32),
            pltpu.VMEM((2,) + elem, f32),
            pltpu.VMEM(elem, f32),
            pltpu.VMEM(elem, f32),
            pltpu.VMEM(elem, f32),
            pltpu.VMEM((4,) + elem[1:], f32),
            pltpu.VMEM((3,) + elem[1:], f32),
            pltpu.VMEM((4, 3, 8, LANES), f32),
            pltpu.VMEM((4, 3) + elem[1:], f32),
            pltpu.VMEM((12, 8, LANES), f32),
            pltpu.VMEM((12, 8, LANES), f32),
            pltpu.VMEM((12, 8, LANES), f32),
            pltpu.VMEM((12, 8, LANES), f32),
            pltpu.VMEM(faces, f32),
            pltpu.VMEM(faces, f32),
            pltpu.VMEM(faces, f32),
            pltpu.VMEM(faces, f32),
            pltpu.VMEM((2, LANES, 125), f32),
            pltpu.VMEM((max(1, n_event - 1), 2, LANES // n_event, 125), f32),
            pltpu.VMEM((2, LANES, 125), f32),
            pltpu.VMEM((3, 2, 8, LANES), f32),
            pltpu.VMEM((3, 2, 8, LANES), f32),
            pltpu.VMEM((3, 5, 2, 8, LANES), f32),
            pltpu.VMEM((3, 5, 2, 8, LANES), f32),
            pltpu.VMEM((3,) + elem, f32),
            pltpu.SemaphoreType.DMA((11,)),
            pltpu.SemaphoreType.DMA((11,)),
            pltpu.SemaphoreType.DMA((7,)),
            pltpu.SemaphoreType.DMA((7,)),
            pltpu.SemaphoreType.DMA((max(1, n_event - 1),)),
            pltpu.SemaphoreType.DMA((max(1, n_event - 1),)),
            pltpu.SemaphoreType.DMA((2,)),
            pltpu.SemaphoreType.DMA((2,)),
        ],
        compiler_params=pltpu.CompilerParams(
            collective_id=0, has_side_effects=True, vmem_limit_bytes=32 * 1024 * 1024
        ),
    )(
        *(
            pltpu.with_memory_space_constraint(value, pltpu.HBM)
            for value in copied + small
        ),
        source_element,
    )
    final_f, final_a, kernels = pl.pallas_call(
        write_out,
        out_shape=tuple(
            jax.ShapeDtypeStruct(value.shape, value.dtype) for value in results
        ),
        in_specs=[vmem] * 3,
        out_specs=(hbm, hbm, hbm),
        scratch_shapes=[pltpu.SemaphoreType.DMA((3,))],
    )(*(pltpu.with_memory_space_constraint(value, pltpu.VMEM) for value in results))
    return (final_f, final_a, kernels.transpose(0, 2, 1))


def solution(mesh):
    return jax.shard_map(
        functools.partial(on_device, mesh.shape["mesh"], mesh.shape["event"]),
        mesh=mesh,
        in_specs=(
            P("event", None, "mesh", None, None),
            P("event", None, "mesh", None, None),
            P("event", None, "mesh", None, None),
            P("event", None, "mesh", None, None),
            P(None, "mesh"),
            P(None, "mesh"),
            P(None, "mesh"),
            P("event"),
            P("event", None),
            P("event", None, None),
            P("event", None),
            P("event", None, None),
            P("event", None, None, None),
        ),
        out_specs=(
            P("event", None, "mesh", None, None),
            P("event", None, "mesh", None, None),
            P(None, None, ("mesh", "event")),
        ),
        check_vma=False,
    )
```

```python
import functools
import math

import jax
import jax.numpy as jnp
import numpy as np
from jax import lax
from jax.experimental import pallas as pl
from jax.experimental.pallas import tpu as pltpu
from jax.sharding import PartitionSpec as P

time_step = 0.04
adjoint_gain = 25.0
LANES = 128


def numpy_tables():
    gll_points = np.array([-1.0, -math.sqrt(3.0 / 7.0), 0.0, math.sqrt(3.0 / 7.0), 1.0])
    legendre = (35.0 * gll_points**4 - 30.0 * gll_points**2 + 3.0) / 8.0
    deriv_table = np.zeros((5, 5))
    for row_q in range(5):
        for col_k in range(5):
            if row_q != col_k:
                deriv_table[row_q, col_k] = legendre[row_q] / (
                    legendre[col_k] * (gll_points[row_q] - gll_points[col_k])
                )
    deriv_table[0, 0] = -5.0
    deriv_table[4, 4] = 5.0
    gll_weights = np.array([0.1, 49.0 / 90.0, 32.0 / 45.0, 49.0 / 90.0, 0.1])
    return (deriv_table, gll_weights)


DERIV, WEIGHTS = numpy_tables()


def constants():
    spread = np.zeros((4, LANES, 4, 4, 32), np.float32)
    for j in range(4):
        for ex in range(32):
            for c in range(4):
                spread[j, 4 * ex + c, c, j, ex] = 1.0
    spread = spread.reshape(512, 512)
    rows = np.zeros((5, 5, 8, 125), np.float32)
    cube = np.zeros((5, 5, 8, LANES), np.float32)
    for a in range(5):
        for b in range(5):
            for c in range(5):
                rows[a, c, b, (a * 5 + b) * 5 + c] = 1.0
                cube[a, c, b, :] = WEIGHTS[a] * WEIGHTS[b] * WEIGHTS[c]
    rows = rows.reshape(200, 125)
    dy = np.zeros((2, 5, 8, LANES), np.float32)
    for k in range(5):
        for b in range(5):
            dy[0, k, b, :] = DERIV[b, k]
            dy[1, k, b, :] = DERIV[k, b]
    bf = jnp.bfloat16
    return (
        jnp.asarray(spread, bf),
        jnp.asarray(np.ascontiguousarray(spread.T), bf),
        jnp.asarray(rows, bf),
        jnp.asarray(cube),
        jnp.asarray(dy),
    )


def split2(value):
    high = value.astype(jnp.bfloat16)
    return (high, (value - high.astype(jnp.float32)).astype(jnp.bfloat16))


def dot(left, right):
    return jnp.dot(left, right, preferred_element_type=jnp.float32)


def move_right(values, table):
    parts = split2(values)
    count = values.shape[0]
    stacked = jnp.concatenate(parts, axis=0)
    moved = dot(stacked, table)
    return moved[0:count] + moved[count : 2 * count]


def move_left(table, values):
    return sum(dot(table, part) for part in split2(values))


def move_left_t(table, values):
    contract = (((0,), (0,)), ((), ()))
    return sum(
        lax.dot_general(table, part, contract, preferred_element_type=jnp.float32)
        for part in split2(values)
    )


def roll_lane(value, shift):
    return pltpu.roll(value, shift % LANES, value.ndim - 1)


def lane_iota(ndim):
    return lax.broadcasted_iota(jnp.int32, (1,) * (ndim - 1) + (LANES,), ndim - 1)


def sub_iota(ndim):
    return lax.broadcasted_iota(jnp.int32, (1,) * (ndim - 2) + (8, LANES), ndim - 2)


def pick(mask, first, second):
    return jnp.where(jnp.broadcast_to(mask, first.shape), first, second)


def from_left(value):
    at_edge = lane_iota(value.ndim) % 32 == 0
    return pick(at_edge, roll_lane(value, -31), roll_lane(value, 1))


def from_right(value):
    at_edge = lane_iota(value.ndim) % 32 == 31
    return pick(at_edge, roll_lane(value, 31), roll_lane(value, -1))


def roll_sub(value):
    return pltpu.roll(value, 4, value.ndim - 2)


def assemble_xy(value):
    first = value[:, 0:1] + from_left(value[:, 4:5])
    value = jnp.concatenate([first, value[:, 1:4], from_right(first)], axis=1)
    swapped = roll_sub(value)
    other = pick(
        lane_iota(4) % 64 < 32, roll_lane(swapped, -32), roll_lane(swapped, 32)
    )
    return value + pick(sub_iota(4) % 4 == 0, other, jnp.zeros_like(other))


EDGE = float(DERIV[0, 0])
HALF = 64


def mix(coefs, planes):
    total = None
    for coef, plane in zip(coefs, planes):
        if coef != 0.0:
            term = float(coef) * plane
            total = term if total is None else total + term
    return total


def along_x(value, flipped=False):
    table = DERIV.T if flipped else DERIV
    even = [value[k] + value[4 - k] for k in range(2)] + [value[2]]
    odd = [value[k] - value[4 - k] for k in range(2)]
    sums = []
    diffs = []
    for c in range(2):
        sums.append(mix([0.5 * (table[c, k] - table[c, 4 - k]) for k in range(2)], odd))
        diffs.append(
            mix(
                [0.5 * (table[c, k] + table[c, 4 - k]) for k in range(2)]
                + [table[c, 2]],
                even,
            )
        )
    rows = [sums[c] + diffs[c] for c in range(2)]
    rows.append(mix(table[2, 0:2], odd))
    rows += [sums[c] - diffs[c] for c in (1, 0)]
    return jnp.stack(rows, axis=0)


def mirror(value):
    return jnp.concatenate([value[0:2], -value[2:3]], axis=0)


def low_lanes(ndim):
    return lane_iota(ndim) < HALF


def swap_half(value):
    return roll_lane(value, HALF)


def unpack(from_above, from_below):
    low = low_lanes(from_above.ndim)
    return (
        pick(low, from_above, swap_half(from_below)),
        pick(low, swap_half(from_above), from_below),
    )


def pack(first, second):
    low = low_lanes(first.ndim)
    return (
        pick(low, first, swap_half(second)),
        pick(low, swap_half(first), second),
    )


def kernel(
    n_mesh,
    n_event,
    steps,
    now_hbm,
    before_hbm,
    adj_hbm,
    after_hbm,
    rho_hbm,
    lam_hbm,
    mu_hbm,
    rec_elem_hbm,
    rec_off_hbm,
    data_hbm,
    spread_hbm,
    gather_hbm,
    rows_hbm,
    cube_hbm,
    dy_hbm,
    off_hbm,
    force_hbm,
    elem_ref,
    final_f_ref,
    final_a_ref,
    out_ref,
    now_ref,
    before_ref,
    adj_ref,
    after_ref,
    rho_ref,
    lam_ref,
    mu_ref,
    rec_elem_ref,
    rec_off_ref,
    data_ref,
    spread_ref,
    gather_ref,
    rows_ref,
    cube_ref,
    dy_ref,
    off_ref,
    force_ref,
    s_in,
    fields,
    stress,
    stress_a,
    held,
    ghost,
    delta,
    count_map,
    data_map,
    source_map,
    first_load,
    strains,
    astrains,
    ksum,
    clam,
    cmu,
    minv,
    ghost_mat,
    work,
    halo_r,
    halo_e,
    mat_us,
    mat_ur,
    mat_ds,
    mat_dr,
    up_s,
    up_r,
    down_s,
    down_r,
    ev_s,
    ev_r,
    ev_t,
    side_s,
    side_r,
    first_s,
    first_r,
    first_own,
    s_up,
    r_up,
    s_down,
    r_down,
    s_ev,
    r_ev,
    s_pair,
    r_pair,
):
    me = lax.axis_index("mesh")
    event = lax.axis_index("event")
    has_up = me > 0
    has_down = me < n_mesh - 1

    barrier = pltpu.get_barrier_semaphore()

    @pl.when(has_up)
    def _():
        pl.semaphore_signal(barrier, inc=1, device_id={"mesh": me - 1})

    @pl.when(has_down)
    def _():
        pl.semaphore_signal(barrier, inc=1, device_id={"mesh": me + 1})

    for hop in range(1, n_event):
        pl.semaphore_signal(
            barrier, inc=1, device_id={"event": lax.rem(event + hop, n_event)}
        )

    paired = n_event == 2
    has_side = jnp.where(event == 0, me, n_mesh - 1 - me) > 0
    side_device = {"event": 1 - event, "mesh": me - 1 + 2 * event}
    if paired:

        @pl.when(has_side)
        def _():
            pl.semaphore_signal(barrier, inc=1, device_id=side_device)

    loads = []
    pairs = (
        (rows_hbm, rows_ref),
        (lam_hbm, lam_ref),
        (mu_hbm, mu_ref),
        (rho_hbm, rho_ref),
        (cube_hbm, cube_ref),
        (now_hbm, now_ref),
        (before_hbm, before_ref),
        (adj_hbm, adj_ref),
        (after_hbm, after_ref),
        (spread_hbm, spread_ref),
        (dy_hbm, dy_ref),
        (rec_elem_hbm, rec_elem_ref),
        (rec_off_hbm, rec_off_ref),
        (data_hbm, data_ref),
        (gather_hbm, gather_ref),
        (off_hbm, off_ref),
        (force_hbm, force_ref),
    )
    for place, (source, target) in enumerate(pairs):
        load_copy = pltpu.make_async_copy(source, target, s_in.at[place])
        load_copy.start()
        loads.append(load_copy)

    def up_copy(source, target, slot):
        return pltpu.make_async_remote_copy(
            src_ref=source, dst_ref=target, send_sem=s_up.at[slot],
            recv_sem=r_up.at[slot], device_id={"mesh": me - 1},
        )

    def down_copy(source, target, slot):
        return pltpu.make_async_remote_copy(
            src_ref=source, dst_ref=target, send_sem=s_down.at[slot],
            recv_sem=r_down.at[slot], device_id={"mesh": me + 1},
        )

    n_face = 6
    mat_slot = n_face
    halo_slot = n_face + 1

    def start_both(up, down):
        @pl.when(has_up)
        def _():
            up.start()

        @pl.when(has_down)
        def _():
            down.start()

    def wait_both(up, down):
        @pl.when(has_down)
        def _():
            up.wait_recv()

        @pl.when(has_up)
        def _():
            down.wait_recv()

    @pl.when(jnp.logical_not(has_down))
    def _():
        halo_r[...] = jnp.zeros_like(halo_r)
        up_r[...] = jnp.zeros_like(up_r)
        mat_ur[...] = jnp.zeros_like(mat_ur)

    if paired:

        @pl.when(jnp.logical_not(has_side))
        def _():
            side_r[...] = jnp.zeros_like(side_r)

    @pl.when(jnp.logical_not(has_up))
    def _():
        down_r[...] = jnp.zeros_like(down_r)
        mat_dr[...] = jnp.zeros_like(mat_dr)

    pl.semaphore_wait(
        barrier,
        jnp.where(has_up, 1, 0)
        + jnp.where(has_down, 1, 0)
        + (n_event - 1)
        + (jnp.where(has_side, 1, 0) if paired else 0),
    )
    tops = (now_hbm, before_hbm, adj_hbm, after_hbm)

    def halo_copy(index):
        return up_copy(
            tops[index].at[0, :, 0], halo_r.at[index], halo_slot + index
        )

    @pl.when(has_up)
    def _():
        for index in range(4):
            halo_copy(index).start()

    low4 = low_lanes(4)

    for place in range(5):
        loads[place].wait()
    materials = jnp.concatenate([lam_ref[...], mu_ref[...], rho_ref[...]], axis=1)
    moved = move_left(rows_ref[...], materials)
    cube = cube_ref[...]

    def modulus(which):
        value = moved[:, which * LANES : (which + 1) * LANES].reshape(5, 5, 8, LANES)
        turned = jnp.stack([value[4 - a] for a in range(5)], axis=0)
        return pick(low4, value, turned) * cube

    lam_value = modulus(0)
    mu_value = modulus(1)
    clam[...] = lam_value
    cmu[...] = mu_value
    mass = modulus(2)
    mass = [assemble_xy(mass[a : a + 1])[0] for a in range(5)]
    mass[4] = mass[4] + swap_half(mass[4])

    def set_minv(a, value):
        keep = sub_iota(3) < 5
        if a == 0:
            keep = keep & (low_lanes(3) | has_down)
        keep = jnp.broadcast_to(keep, value.shape)
        safe = jnp.where(keep, value, 1.0)
        minv[a] = jnp.where(keep, time_step**2 / safe, 0.0)

    for a in range(1, 5):
        set_minv(a, mass[a])

    squares = [float(DERIV[q, 0]) ** 2 for q in range(5)]
    diag_mu = mix(squares[1:], [mu_value[q] for q in range(1, 5)])
    diag_lam = mix(squares[1:], [lam_value[q] for q in range(1, 5)])
    diag_lam = diag_lam + (diag_mu + diag_mu)
    listed = [mass[0][c] for c in range(4)]
    for value in (lam_value[0], mu_value[0], diag_mu, diag_lam):
        listed += [value[c] for c in range(5)]
    for pair in range(12):
        up, down = pack(listed[2 * pair], listed[2 * pair + 1])
        mat_us[pair] = up
        mat_ds[pair] = down

    start_both(up_copy(mat_us, mat_ur, mat_slot), down_copy(mat_ds, mat_dr, mat_slot))

    for place in range(5, 11):
        loads[place].wait()
    inputs = (now_ref, before_ref, adj_ref, after_ref)

    def bring_in(index):
        ref = inputs[index]
        upper = ref[0, :, 0:5]
        lower = mirror(
            jnp.stack(
                [jnp.zeros((3, 8, LANES), jnp.float32)]
                + [ref[0, :, 8 - a] for a in range(1, 5)],
                axis=1,
            )
        )
        parts = []
        for layer in (upper, lower):
            for shifted in (layer, roll_sub(layer)):
                parts.append(shifted.reshape(120, LANES))
        moved = move_right(jnp.concatenate(parts, axis=1), spread_ref[...])
        for c in range(4):
            fields[index, :, :, c] = moved[:, c * LANES : (c + 1) * LANES].reshape(
                3, 5, 8, LANES
            )
        fields[index, :, :, 4] = from_right(
            moved[:, 0:LANES].reshape(3, 5, 8, LANES)
        )

    def bring_halos():
        @pl.when(has_down)
        def _():
            for index in range(4):
                halo_copy(index).wait_recv()

        planes = jnp.stack([halo_r[:, 0], halo_r[:, 1], -halo_r[:, 2]], axis=1)
        parts = [
            planes.reshape(96, LANES),
            roll_sub(planes).reshape(96, LANES),
        ]
        moved = move_right(
            jnp.concatenate(parts, axis=1), spread_ref[2 * LANES : 4 * LANES]
        )
        for c in range(5):
            part = moved[:, (c % 4) * LANES : (c % 4 + 1) * LANES]
            part = part.reshape(4, 3, 8, LANES)
            if c == 4:
                part = from_right(part)
            halo_e[:, :, c] = part
            fields[0:3, :, 0, c] = fields[0:3, :, 0, c] + part[0:3]

    def owned(ndim):
        return jnp.where(lane_iota(ndim) < HALF, 0, 1) == event

    def side_copy():
        return pltpu.make_async_remote_copy(
            src_ref=side_s, dst_ref=side_r, send_sem=s_pair.at[0],
            recv_sem=r_pair.at[0], device_id=side_device,
        )

    def first_copy():
        return pltpu.make_async_remote_copy(
            src_ref=first_s, dst_ref=first_r, send_sem=s_pair.at[1],
            recv_sem=r_pair.at[1], device_id={"event": 1 - event},
        )

    def send_first():
        if not paired:
            return
        mine = owned(3)
        for a in range(5):
            first_own[:, a] = fields[1, :, a]
            for pair in range(2):
                first = fields[1, :, a, 2 * pair]
                second = fields[1, :, a, 2 * pair + 1]
                first_s[:, a, pair] = pick(mine, swap_half(second), first)
        first_copy().start()

    def take_first():
        first_copy().wait_recv()
        mine = owned(3)
        for a in range(5):
            for pair in range(2):
                packed = first_r[:, a, pair]
                for c, other in ((2 * pair, swap_half(packed)), (2 * pair + 1, packed)):
                    value = pick(mine, first_own[:, a, c], other)
                    fields[4, :, a, c] = value
                    if c == 0:
                        fields[4, :, a, 4] = from_right(value)
        for a in range(5):
            strain = strain_at(4, a)
            for i in range(6):
                strains[2, a, i] = strain[i]

    def send_side(slot):
        if not paired:
            return
        side_s[...] = jnp.where(event == 0, up_s[slot], down_s[slot])

        @pl.when(has_side)
        def _():
            side_copy().start()

    def paired_delta(own):
        @pl.when(has_side)
        def _():
            side_copy().wait_recv()

        sides = []
        for pair in range(2):
            packed = side_r[:, pair]
            turned = swap_half(packed)
            sides += [
                jnp.where(event == 0, turned, packed),
                jnp.where(event == 0, packed, turned),
            ]
        sides.append(from_right(sides[0]))
        other = mirror(jnp.stack(sides, axis=1))
        mine = owned(3)
        scale = pick(mine, minv[0], swap_half(minv[0]))
        return pick(owned(4), own, -scale * other)

    def along_y(value, flipped=False):
        total = None
        for k in range(5):
            row = jnp.broadcast_to(value[..., k : k + 1, :], value.shape)
            term = dy_ref[1 if flipped else 0, k] * row
            total = term if total is None else total + term
        return total

    def send(slot, value):
        for pair in range(2):
            up, down = pack(value[:, 2 * pair], value[:, 2 * pair + 1])
            up_s[slot, :, pair] = up
            down_s[slot, :, pair] = down
        start_both(
            up_copy(up_s.at[slot], up_r.at[slot], slot),
            down_copy(down_s.at[slot], down_r.at[slot], slot),
        )

    def receive(slot):
        wait_both(
            up_copy(up_s.at[slot], up_r.at[slot], slot),
            down_copy(down_s.at[slot], down_r.at[slot], slot),
        )
        sides = []
        for pair in range(2):
            sides += unpack(down_r[slot, :, pair], up_r[slot, :, pair])
        sides.append(from_right(sides[0]))
        return mirror(jnp.stack(sides, axis=1))

    def along_z(index, comp, a, first=0):
        return mix(
            DERIV[a, first:], [fields[index, comp, k] for k in range(first, 5)]
        )

    def strain_at(index, a):
        u = [fields[index, comp, a] for comp in range(3)]
        gz = [along_z(index, comp, a) for comp in range(3)]
        return (
            along_x(u[0]),
            along_y(u[1]),
            gz[2],
            along_y(u[0]) + along_x(u[1]),
            gz[0] + along_x(u[2]),
            gz[1] + along_y(u[2]),
        )

    def set_ghost():
        u = [delta[comp] for comp in range(3)]
        gz = [-EDGE * value for value in u]
        lam_g, mu_g = ghost_mat[0], ghost_mat[1]
        xx = along_x(u[0])
        yy = along_y(u[1])
        zz = gz[2]
        side = lam_g * (xx + yy + zz)
        mu_two = mu_g + mu_g
        xx = side + mu_two * xx
        yy = side + mu_two * yy
        zz = side + mu_two * zz
        xy = mu_g * (along_y(u[0]) + along_x(u[1]))
        xz = mu_g * (gz[0] + along_x(u[2]))
        yz = mu_g * (gz[1] + along_y(u[2]))
        work[0] = xy
        work[1] = yy
        work[2] = yz
        values = (
            along_x(xx, True)
            + along_y(work[0], True)
            - EDGE * xz
            + ghost_mat[2] * u[0],
            along_x(xy, True)
            + along_y(work[1], True)
            - EDGE * yz
            + ghost_mat[2] * u[1],
            along_x(xz, True)
            + along_y(work[2], True)
            - EDGE * zz
            + ghost_mat[3] * u[2],
        )
        ghost[...] = assemble_xy(jnp.stack(values, axis=0))

    def put_stress(target, a, strain, add):
        lam_div = clam[a] * (strain[0] + strain[1] + strain[2])
        mu_a = cmu[a]
        mu_two = mu_a + mu_a
        for i in range(3):
            value = lam_div + mu_two * strain[i]
            target[i, a] = target[i, a] + value if add else value
            value = mu_a * strain[3 + i]
            target[3 + i, a] = target[3 + i, a] + value if add else value

    def make_stress(index, target, keep_strain):
        for a in range(5):
            strain = strain_at(index, a)
            put_stress(target, a, strain, False)
            if keep_strain is not None:
                for i in range(6):
                    keep_strain[a, i] = strain[i]

    def face_strain():
        u = [delta[comp] for comp in range(3)]
        return (
            along_x(u[0]),
            along_y(u[1]),
            EDGE * u[2],
            along_y(u[0]) + along_x(u[1]),
            EDGE * u[0] + along_x(u[2]),
            EDGE * u[1] + along_y(u[2]),
        )

    def add_face(target, keep_strain):
        strain = face_strain()
        put_stress(target, 0, strain, True)
        if keep_strain is not None:
            for i in range(6):
                keep_strain[0, i] = keep_strain[0, i] + strain[i]
        for q in range(1, 5):
            gz = [float(DERIV[q, 0]) * delta[comp] for comp in range(3)]
            mu_q = cmu[q]
            side = clam[q] * gz[2]
            target[0, q] = target[0, q] + side
            target[1, q] = target[1, q] + side
            target[2, q] = target[2, q] + (side + (mu_q + mu_q) * gz[2])
            target[4, q] = target[4, q] + mu_q * gz[0]
            target[5, q] = target[5, q] + mu_q * gz[1]
            if keep_strain is not None:
                keep_strain[q, 2] = keep_strain[q, 2] + gz[2]
                keep_strain[q, 4] = keep_strain[q, 4] + gz[0]
                keep_strain[q, 5] = keep_strain[q, 5] + gz[1]

    pairs_of = ((0, 3, 4), (3, 1, 5), (4, 5, 2))

    def both_layers(value):
        return value + mirror(swap_half(value))

    def plane_force(source, a):
        values = []
        for comp in range(3):
            ix, iy, iz = pairs_of[comp]
            total = along_x(source[ix, a], True) + along_y(source[iy, a], True)
            values.append(total + mix(DERIV[:, a], [source[iz, q] for q in range(5)]))
        value = assemble_xy(jnp.stack(values, axis=0))
        return both_layers(value) if a == 4 else value

    def advance(index, older, a, value, load):
        if load is not None:
            value = value - load(a)
        fields[older, :, a] = (
            2.0 * fields[index, :, a] - fields[older, :, a]
        ) - minv[a] * value

    def inside_planes(index, older, source, load):
        for a in range(1, 5):
            advance(index, older, a, plane_force(source, a), load)

    def close_step(index, older, source, slot, load):
        inside_planes(index, older, source, load)
        close_outer(index, older, source, slot, load)

    def close_outer(index, older, source, slot, load):
        value = plane_force(source, 0) + ghost[...]
        advance(index, older, 0, value + receive(slot), load)

    def open_step(index, older, slot, load):
        held[...] = plane_force(stress, 0)
        send(slot, held[...])
        if slot == 4:
            send_side(slot)
        inside_planes(index, older, stress, load)
        advance(index, older, 0, held[...], load)

    def add_correction(which):
        strain = face_strain()
        for a in range(5):
            other = [strains[which, a, i] for i in range(6)]
            div_f = other[0] + other[1] + other[2]
            if a == 0:
                lam_part = (strain[0] + strain[1] + strain[2]) * div_f
                mu_part = (
                    strain[0] * other[0] + strain[1] * other[1] + strain[2] * other[2]
                ) + 0.5 * (
                    strain[3] * other[3] + strain[4] * other[4] + strain[5] * other[5]
                )
            else:
                gz = [float(DERIV[a, 0]) * delta[comp] for comp in range(3)]
                lam_part = gz[2] * div_f
                mu_part = gz[2] * other[2] + 0.5 * (gz[0] * other[4] + gz[1] * other[5])
            if which == 2:
                lam_part = lam_part + swap_half(lam_part)
                mu_part = mu_part + swap_half(mu_part)
            ksum[0, a] = ksum[0, a] + lam_part
            ksum[1, a] = ksum[1, a] + mu_part

    def close_face(older, slot, keep_strain):
        delta[...] = -minv[0] * receive(slot)
        fields[older, :, 0] = fields[older, :, 0] + delta[...]
        add_face(stress, keep_strain)

    bring_in(0)
    make_stress(0, stress, None)
    send(0, plane_force(stress, 0))
    bring_in(2)
    make_stress(2, stress_a, astrains.at[2])
    send(1, plane_force(stress_a, 0))
    bring_in(1)
    for place in range(15, 17):
        loads[place].wait()
    src_local = elem_ref[0] - LANES * me
    src_depth = off_ref[0, 0]
    src_in = (src_local >= 0) & (src_local < LANES)
    src_over = (src_local >= -HALF) & (src_local < 0) & (src_depth == 4)
    src_under = (src_local >= LANES) & (src_local < LANES + HALF) & (src_depth == 0)
    src_lane = jnp.where(
        src_in,
        src_local,
        jnp.where(
            src_over, src_local + HALF, jnp.where(src_under, src_local - HALF, -1)
        ),
    )
    src_depth = jnp.where(
        src_in, jnp.where(src_local < HALF, src_depth, 4 - src_depth), 0
    )
    src_row = src_depth * 40 + off_ref[0, 2] * 8 + off_ref[0, 1]

    shape = (5, 8, LANES)
    src_lanes = lax.broadcasted_iota(jnp.int32, shape, 2) == src_lane
    src_rows = lax.broadcasted_iota(jnp.int32, shape, 0) * 8 + lax.broadcasted_iota(
        jnp.int32, shape, 1
    )
    for a in range(5):
        source_at = jnp.where(src_lanes & (src_rows + 40 * a == src_row), 1.0, 0.0)
        value = assemble_xy(source_at[None])[0]
        source_map[a] = value + swap_half(value) if a == 4 else value

    def make_maps():
        for place in range(11, 14):
            loads[place].wait()
        nrec = rec_elem_ref.shape[1]
        local = rec_elem_ref[...] - LANES * me
        depth = rec_off_ref[0]
        in_slab = (local >= 0) & (local < LANES)
        over = (local >= -HALF) & (local < 0) & (depth == 4)
        under = (local >= LANES) & (local < LANES + HALF) & (depth == 0)
        rec_at = jnp.where(
            in_slab,
            local,
            jnp.where(over, local + HALF, jnp.where(under, local - HALF, -1)),
        )
        depth = jnp.where(
            in_slab, jnp.where(local < HALF, depth, 4 - depth), jnp.zeros_like(depth)
        )
        lane_t = lax.broadcasted_iota(jnp.int32, (LANES, nrec), 0) == rec_at
        lane_t = jnp.where(lane_t, 1.0, 0.0).astype(jnp.bfloat16)
        eye = jnp.where(
            lax.broadcasted_iota(jnp.int32, (nrec, nrec), 0)
            == lax.broadcasted_iota(jnp.int32, (nrec, nrec), 1),
            1.0,
            0.0,
        ).astype(jnp.bfloat16)
        turned = (((1,), (1,)), ((), ()))

        def turn(part):
            return lax.dot_general(eye, part, turned, preferred_element_type=jnp.float32)

        rec_lane = turn(lane_t)
        rec_lanes = (rec_lane, rec_lane, pick(low_lanes(2), rec_lane, -rec_lane))
        row = depth * 40 + rec_off_ref[2] * 8 + rec_off_ref[1]
        rows_lanes = lax.broadcasted_iota(jnp.int32, (200, nrec), 0) == row
        rows_lanes = jnp.where(rows_lanes, 1.0, 0.0).astype(jnp.bfloat16)
        observed = jnp.concatenate(
            [data_ref[n, comp] for n in range(steps) for comp in range(3)], axis=0
        )
        observed = sum(turn(part) for part in split2(observed))

        scaled = adjoint_gain * observed
        columns = jnp.concatenate(
            [
                scaled[:, 3 * moment + comp : 3 * moment + comp + 1] * rec_lanes[comp]
                for moment in range(steps)
                for comp in range(3)
            ],
            axis=1,
        )
        at_points = sum(dot(rows_lanes, part) for part in split2(columns))
        counts = adjoint_gain * dot(rows_lanes, rec_lane.astype(jnp.bfloat16))
        for a in range(5):
            count_at = counts[40 * a : 40 * a + 40].reshape(shape)
            data_at = [
                at_points[40 * a : 40 * a + 40, LANES * i : LANES * (i + 1)].reshape(shape)
                for i in range(3 * steps)
            ]
            value = assemble_xy(jnp.stack([count_at] + data_at, axis=0))
            if a == 4:
                other = swap_half(value)
                value = value + jnp.stack(
                    [
                        -other[i] if i > 0 and i % 3 == 0 else other[i]
                        for i in range(1 + 3 * steps)
                    ],
                    axis=0,
                )
            count_map[a] = value[0]
            for moment in range(steps):
                data_map[moment, :, a] = value[1 + 3 * moment : 4 + 3 * moment]

    def source_load(moment):
        forces = [force_ref[moment, 0, comp] for comp in range(3)]
        lane = lax.broadcasted_iota(jnp.int32, (8, LANES), 1)
        forces[2] = jnp.where(lane < HALF, forces[2], -forces[2])
        return lambda a: jnp.stack(
            [source_map[a] * forces[comp] for comp in range(3)], axis=0
        )

    def receiver_load(index, moment):
        return (
            lambda a: count_map[a][None] * fields[index, :, a] - data_map[moment, :, a]
        )

    bring_halos()
    delta[...] = halo_e[0]
    add_face(stress, None)
    inside_planes(0, 1, stress, source_load(0))

    wait_both(up_copy(mat_us, mat_ur, mat_slot), down_copy(mat_ds, mat_dr, mat_slot))
    listed = []
    for pair in range(12):
        listed += unpack(mat_dr[pair], mat_ur[pair])
    for which in range(4):
        for c in range(5):
            ghost_mat[which, c] = listed[4 + 5 * which + c]
    face_mass = listed[0:4]
    set_minv(0, mass[0] + jnp.stack(face_mass + [from_right(face_mass[0])], axis=0))

    def ghost_of_start(index):
        top = fields[index, :, 0]
        delta[...] = pick(low4, top, jnp.zeros_like(top))
        set_ghost()

    ghost_of_start(0)
    close_outer(0, 1, stress, 0, source_load(0))

    make_stress(1, stress, strains.at[0])
    open_step(1, 0, 2, source_load(1))
    make_stress(0, stress, strains.at[1])
    send(3, plane_force(stress, 0))

    send_first()
    make_maps()
    bring_in(3)
    fields[3, :, 0] = fields[3, :, 0] + halo_e[3]
    delta[...] = halo_e[2]
    add_face(stress_a, astrains.at[2])
    ghost_of_start(2)
    close_step(2, 3, stress_a, 1, None)
    load = receiver_load(1, 0)
    for a in range(5):
        first_load[:, a] = load(a)
        fields[3, :, a] = fields[3, :, a] - minv[a] * data_map[2, :, a]
    delta[...] = -minv[0] * held[...]
    set_ghost()

    close_face(0, 2, strains.at[1])
    close_step(0, 1, stress, 3, source_load(2))

    for a in range(5):
        fields[3, :, a] = fields[3, :, a] + minv[a] * (
            count_map[a][None] * fields[1, :, a]
        )
    make_stress(3, stress, astrains.at[1])
    open_step(3, 2, 4, receiver_load(0, 1))
    make_stress(2, stress, astrains.at[0])

    def put_out(index, ref):
        sides = []
        for c in range(4):
            upper = fields[index, :, 0:4, c]
            lower = mirror(
                jnp.stack([fields[index, :, 4 - i, c] for i in range(4)], axis=1)
            )
            sides.append(pick(low4, upper, lower).reshape(96, LANES))
        moved = move_right(jnp.concatenate(sides, axis=1), gather_ref[...])
        for ez in range(2):
            first = moved[:, 2 * ez * LANES : (2 * ez + 1) * LANES]
            second = moved[:, (2 * ez + 1) * LANES : (2 * ez + 2) * LANES]
            first = first.reshape(3, 4, 8, LANES)
            second = roll_sub(second.reshape(3, 4, 8, LANES))
            ref[0, :, 4 * ez : 4 * ez + 4] = pick(sub_iota(4) < 4, first, second)

    def add_kernels(adjoint, other_at, first):
        for a in range(5):
            strain = [adjoint[a, i] for i in range(6)]
            other = other_at(a)
            div_a = strain[0] + strain[1] + strain[2]
            div_f = other[0] + other[1] + other[2]
            diag = strain[0] * other[0] + strain[1] * other[1] + strain[2] * other[2]
            shear = strain[3] * other[3] + strain[4] * other[4] + strain[5] * other[5]
            lam_part = div_a * div_f
            mu_part = diag + 0.5 * shear
            if not first:
                lam_part = ksum[0, a] + lam_part
                mu_part = ksum[1, a] + mu_part
            ksum[0, a] = lam_part
            ksum[1, a] = mu_part

    def kept(which):
        return lambda a: [strains[which, a, i] for i in range(6)]

    width = LANES // n_event

    def event_copy(hop, which):
        target = lax.rem(event + hop, n_event)
        return pltpu.make_async_remote_copy(
            src_ref=ev_s.at[which, pl.ds(pl.multiple_of(width * target, width), width)],
            dst_ref=ev_r.at[hop - 1, which],
            send_sem=s_ev.at[2 * hop - 2 + which],
            recv_sem=r_ev.at[2 * hop - 2 + which],
            device_id={"event": target},
        )

    def natural_kernel(which, target):
        scale, modulus_ref = ((-time_step, lam_ref), (-2.0 * time_step, mu_ref))[which]
        value = ksum[which]
        turned_back = jnp.stack([value[4 - a] for a in range(5)], axis=0)
        value = pick(low4, value, turned_back).reshape(200, LANES)
        natural = move_left_t(rows_ref[...], value)
        target[which] = jnp.transpose(natural * (scale * modulus_ref[...]))

    def send_kernels():
        for which in range(2):
            natural_kernel(which, ev_s)
            for hop in range(1, n_event):
                event_copy(hop, which).start()

    send(5, plane_force(stress, 0))

    add_kernels(astrains.at[2], lambda a: strain_at(1, a), True)
    add_kernels(astrains.at[1], kept(1), False)
    add_kernels(astrains.at[0], kept(0), False)
    if paired:
        send_kernels()

    delta[...] = -minv[0] * held[...]
    set_ghost()
    if paired:
        take_first()
    loads[14].wait()
    put_out(1, final_f_ref)

    close_face(2, 4, None)
    if paired:
        delta[...] = paired_delta(delta[...])
        add_correction(2)
        for which in range(2):
            natural_kernel(which, ev_t)
    else:
        add_correction(0)
        send_kernels()
    close_step(2, 3, stress, 5, lambda a: first_load[:, a])
    put_out(3, final_a_ref)

    mine = pl.ds(pl.multiple_of(width * event, width), width)
    total = ev_t[:, mine] if paired else ev_s[:, mine]
    for hop in range(1, n_event):
        for which in range(2):
            event_copy(hop, which).wait_recv()
        total = total + ev_r[hop - 1]
    out_ref[...] = total

    @pl.when(has_up)
    def _():
        for index in range(4):
            halo_copy(index).wait_send()
        up_copy(mat_us, mat_ur, mat_slot).wait_send()
        for slot in range(n_face):
            up_copy(up_s.at[slot], up_r.at[slot], slot).wait_send()

    @pl.when(has_down)
    def _():
        down_copy(mat_ds, mat_dr, mat_slot).wait_send()
        for slot in range(n_face):
            down_copy(down_s.at[slot], down_r.at[slot], slot).wait_send()

    for hop in range(1, n_event):
        for which in range(2):
            event_copy(hop, which).wait_send()

    if paired:
        first_copy().wait_send()

        @pl.when(has_side)
        def _():
            side_copy().wait_send()


def write_out(first, second, third, first_out, second_out, third_out, sems):
    copies = [
        pltpu.make_async_copy(source, target, sems.at[place])
        for place, (source, target) in enumerate(
            ((first, first_out), (second, second_out), (third, third_out))
        )
    ]
    for copy in copies:
        copy.start()
    for copy in copies:
        copy.wait()


def on_device(
    n_mesh,
    n_event,
    forward_before,
    forward_now,
    adjoint_after,
    adjoint_now,
    mass_density,
    lame_lambda,
    lame_mu,
    source_element,
    source_offset,
    source_force,
    receiver_element,
    receiver_offset,
    receiver_data,
):
    assert forward_now.shape[1:] == (3, 8, 8, 128)
    assert lame_mu.shape == (125, 128)
    steps = source_force.shape[1]
    assert steps == 3
    field = forward_now.shape
    vmem = pl.BlockSpec(memory_space=pltpu.VMEM)
    hbm = pl.BlockSpec(memory_space=pltpu.HBM)
    f32 = jnp.float32
    elem = (5, 5, 8, LANES)
    faces = (6, 3, 2, 8, LANES)
    copied = (
        forward_now,
        forward_before,
        adjoint_now,
        adjoint_after,
        mass_density,
        lame_lambda,
        lame_mu,
        receiver_element,
        receiver_offset.transpose(2, 0, 1),
        receiver_data.transpose(1, 3, 0, 2),
    ) + constants()
    small = (source_offset, source_force.transpose(1, 0, 2))
    results = pl.pallas_call(
        functools.partial(kernel, n_mesh, n_event, steps),
        out_shape=(
            pltpu.VMEM(field, f32),
            pltpu.VMEM(field, f32),
            pltpu.VMEM((2, LANES // n_event, 125), f32),
        ),
        in_specs=[hbm] * 17 + [pl.BlockSpec(memory_space=pltpu.SMEM)],
        out_specs=(vmem, vmem, vmem),
        scratch_shapes=[pltpu.VMEM(value.shape, value.dtype) for value in copied]
        + [pltpu.SMEM(value.shape, value.dtype) for value in small]
        + [
            pltpu.SemaphoreType.DMA((len(copied) + len(small),)),
            pltpu.VMEM((5, 3) + elem, f32),
            pltpu.VMEM((6,) + elem, f32),
            pltpu.VMEM((6,) + elem, f32),
            pltpu.VMEM((3,) + elem[1:], f32),
            pltpu.VMEM((3,) + elem[1:], f32),
            pltpu.VMEM((3,) + elem[1:], f32),
            pltpu.VMEM(elem, f32),
            pltpu.VMEM((steps, 3) + elem, f32),
            pltpu.VMEM(elem, f32),
            pltpu.VMEM((3,) + elem, f32),
            pltpu.VMEM((3, 5, 6, 5, 8, LANES), f32),
            pltpu.VMEM((3, 5, 6, 5, 8, LANES), f32),
            pltpu.VMEM((2,) + elem, f32),
            pltpu.VMEM(elem, f32),
            pltpu.VMEM(elem, f32),
            pltpu.VMEM(elem, f32),
            pltpu.VMEM((4,) + elem[1:], f32),
            pltpu.VMEM((3,) + elem[1:], f32),
            pltpu.VMEM((4, 3, 8, LANES), f32),
            pltpu.VMEM((4, 3) + elem[1:], f32),
            pltpu.VMEM((12, 8, LANES), f32),
            pltpu.VMEM((12, 8, LANES), f32),
            pltpu.VMEM((12, 8, LANES), f32),
            pltpu.VMEM((12, 8, LANES), f32),
            pltpu.VMEM(faces, f32),
            pltpu.VMEM(faces, f32),
            pltpu.VMEM(faces, f32),
            pltpu.VMEM(faces, f32),
            pltpu.VMEM((2, LANES, 125), f32),
            pltpu.VMEM((max(1, n_event - 1), 2, LANES // n_event, 125), f32),
            pltpu.VMEM((2, LANES, 125), f32),
            pltpu.VMEM((3, 2, 8, LANES), f32),
            pltpu.VMEM((3, 2, 8, LANES), f32),
            pltpu.VMEM((3, 5, 2, 8, LANES), f32),
            pltpu.VMEM((3, 5, 2, 8, LANES), f32),
            pltpu.VMEM((3,) + elem, f32),
            pltpu.SemaphoreType.DMA((11,)),
            pltpu.SemaphoreType.DMA((11,)),
            pltpu.SemaphoreType.DMA((7,)),
            pltpu.SemaphoreType.DMA((7,)),
            pltpu.SemaphoreType.DMA((max(2, 2 * n_event - 2),)),
            pltpu.SemaphoreType.DMA((max(2, 2 * n_event - 2),)),
            pltpu.SemaphoreType.DMA((2,)),
            pltpu.SemaphoreType.DMA((2,)),
        ],
        compiler_params=pltpu.CompilerParams(
            collective_id=0, has_side_effects=True, vmem_limit_bytes=32 * 1024 * 1024
        ),
    )(
        *(
            pltpu.with_memory_space_constraint(value, pltpu.HBM)
            for value in copied + small
        ),
        source_element,
    )
    final_f, final_a, kernels = pl.pallas_call(
        write_out,
        out_shape=tuple(
            jax.ShapeDtypeStruct(value.shape, value.dtype) for value in results
        ),
        in_specs=[vmem] * 3,
        out_specs=(hbm, hbm, hbm),
        scratch_shapes=[pltpu.SemaphoreType.DMA((3,))],
    )(*(pltpu.with_memory_space_constraint(value, pltpu.VMEM) for value in results))
    return (final_f, final_a, kernels.transpose(0, 2, 1))


def solution(mesh):
    return jax.shard_map(
        functools.partial(on_device, mesh.shape["mesh"], mesh.shape["event"]),
        mesh=mesh,
        in_specs=(
            P("event", None, "mesh", None, None),
            P("event", None, "mesh", None, None),
            P("event", None, "mesh", None, None),
            P("event", None, "mesh", None, None),
            P(None, "mesh"),
            P(None, "mesh"),
            P(None, "mesh"),
            P("event"),
            P("event", None),
            P("event", None, None),
            P("event", None),
            P("event", None, None),
            P("event", None, None, None),
        ),
        out_specs=(
            P("event", None, "mesh", None, None),
            P("event", None, "mesh", None, None),
            P(None, None, ("mesh", "event")),
        ),
        check_vma=False,
    )
```

```python
import functools
import math

import jax
import jax.numpy as jnp
import numpy as np
from jax import lax
from jax.experimental import pallas as pl
from jax.experimental.pallas import tpu as pltpu
from jax.sharding import PartitionSpec as P

time_step = 0.04
adjoint_gain = 25.0
LANES = 128


def numpy_tables():
    gll_points = np.array([-1.0, -math.sqrt(3.0 / 7.0), 0.0, math.sqrt(3.0 / 7.0), 1.0])
    legendre = (35.0 * gll_points**4 - 30.0 * gll_points**2 + 3.0) / 8.0
    deriv_table = np.zeros((5, 5))
    for row_q in range(5):
        for col_k in range(5):
            if row_q != col_k:
                deriv_table[row_q, col_k] = legendre[row_q] / (
                    legendre[col_k] * (gll_points[row_q] - gll_points[col_k])
                )
    deriv_table[0, 0] = -5.0
    deriv_table[4, 4] = 5.0
    gll_weights = np.array([0.1, 49.0 / 90.0, 32.0 / 45.0, 49.0 / 90.0, 0.1])
    return (deriv_table, gll_weights)


DERIV, WEIGHTS = numpy_tables()


def constants():
    spread = np.zeros((4, LANES, 4, 4, 32), np.float32)
    for j in range(4):
        for ex in range(32):
            for c in range(4):
                spread[j, 4 * ex + c, c, j, ex] = 1.0
    spread = spread.reshape(512, 512)
    rows = np.zeros((5, 5, 8, 125), np.float32)
    cube = np.zeros((5, 5, 8, LANES), np.float32)
    for a in range(5):
        for b in range(5):
            for c in range(5):
                rows[a, c, b, (a * 5 + b) * 5 + c] = 1.0
                cube[a, c, b, :] = WEIGHTS[a] * WEIGHTS[b] * WEIGHTS[c]
    rows = rows.reshape(200, 125)
    dy = np.zeros((2, 5, 8, LANES), np.float32)
    for k in range(5):
        for b in range(5):
            dy[0, k, b, :] = DERIV[b, k]
            dy[1, k, b, :] = DERIV[k, b]
    bf = jnp.bfloat16
    return (
        jnp.asarray(spread, bf),
        jnp.asarray(np.ascontiguousarray(spread.T), bf),
        jnp.asarray(rows, bf),
        jnp.asarray(cube),
        jnp.asarray(dy),
    )


def split2(value):
    high = value.astype(jnp.bfloat16)
    return (high, (value - high.astype(jnp.float32)).astype(jnp.bfloat16))


def dot(left, right):
    return jnp.dot(left, right, preferred_element_type=jnp.float32)


def move_right(values, table):
    parts = split2(values)
    count = values.shape[0]
    stacked = jnp.concatenate(parts, axis=0)
    moved = dot(stacked, table)
    return moved[0:count] + moved[count : 2 * count]


def move_left(table, values):
    return sum(dot(table, part) for part in split2(values))


def move_left_t(table, values):
    contract = (((0,), (0,)), ((), ()))
    return sum(
        lax.dot_general(table, part, contract, preferred_element_type=jnp.float32)
        for part in split2(values)
    )


def roll_lane(value, shift):
    return pltpu.roll(value, shift % LANES, value.ndim - 1)


def lane_iota(ndim):
    return lax.broadcasted_iota(jnp.int32, (1,) * (ndim - 1) + (LANES,), ndim - 1)


def sub_iota(ndim):
    return lax.broadcasted_iota(jnp.int32, (1,) * (ndim - 2) + (8, LANES), ndim - 2)


def pick(mask, first, second):
    return jnp.where(jnp.broadcast_to(mask, first.shape), first, second)


def from_left(value):
    at_edge = lane_iota(value.ndim) % 32 == 0
    return pick(at_edge, roll_lane(value, -31), roll_lane(value, 1))


def from_right(value):
    at_edge = lane_iota(value.ndim) % 32 == 31
    return pick(at_edge, roll_lane(value, 31), roll_lane(value, -1))


def roll_sub(value):
    return pltpu.roll(value, 4, value.ndim - 2)


def assemble_xy(value):
    first = value[:, 0:1] + from_left(value[:, 4:5])
    value = jnp.concatenate([first, value[:, 1:4], from_right(first)], axis=1)
    swapped = roll_sub(value)
    other = pick(
        lane_iota(4) % 64 < 32, roll_lane(swapped, -32), roll_lane(swapped, 32)
    )
    return value + pick(sub_iota(4) % 4 == 0, other, jnp.zeros_like(other))


EDGE = float(DERIV[0, 0])
HALF = 64


def mix(coefs, planes):
    total = None
    for coef, plane in zip(coefs, planes):
        if coef != 0.0:
            term = float(coef) * plane
            total = term if total is None else total + term
    return total


def along_x(value, flipped=False):
    table = DERIV.T if flipped else DERIV
    even = [value[k] + value[4 - k] for k in range(2)] + [value[2]]
    odd = [value[k] - value[4 - k] for k in range(2)]
    sums = []
    diffs = []
    for c in range(2):
        sums.append(mix([0.5 * (table[c, k] - table[c, 4 - k]) for k in range(2)], odd))
        diffs.append(
            mix(
                [0.5 * (table[c, k] + table[c, 4 - k]) for k in range(2)]
                + [table[c, 2]],
                even,
            )
        )
    rows = [sums[c] + diffs[c] for c in range(2)]
    rows.append(mix(table[2, 0:2], odd))
    rows += [sums[c] - diffs[c] for c in (1, 0)]
    return jnp.stack(rows, axis=0)


def mirror(value):
    return jnp.concatenate([value[0:2], -value[2:3]], axis=0)


def low_lanes(ndim):
    return lane_iota(ndim) < HALF


def swap_half(value):
    return roll_lane(value, HALF)


def unpack(from_above, from_below):
    low = low_lanes(from_above.ndim)
    return (
        pick(low, from_above, swap_half(from_below)),
        pick(low, swap_half(from_above), from_below),
    )


def pack(first, second):
    low = low_lanes(first.ndim)
    return (
        pick(low, first, swap_half(second)),
        pick(low, swap_half(first), second),
    )


def kernel(
    n_mesh,
    n_event,
    steps,
    now_hbm,
    before_hbm,
    adj_hbm,
    after_hbm,
    rho_hbm,
    lam_hbm,
    mu_hbm,
    rec_elem_hbm,
    rec_off_hbm,
    data_hbm,
    spread_hbm,
    gather_hbm,
    rows_hbm,
    cube_hbm,
    dy_hbm,
    off_hbm,
    force_hbm,
    elem_ref,
    final_f_ref,
    final_a_ref,
    out_ref,
    now_ref,
    before_ref,
    adj_ref,
    after_ref,
    rho_ref,
    lam_ref,
    mu_ref,
    rec_elem_ref,
    rec_off_ref,
    data_ref,
    spread_ref,
    gather_ref,
    rows_ref,
    cube_ref,
    dy_ref,
    off_ref,
    force_ref,
    s_in,
    fields,
    stress,
    stress_a,
    held,
    ghost,
    delta,
    count_map,
    data_map,
    source_map,
    first_load,
    strains,
    astrains,
    ksum,
    clam,
    cmu,
    minv,
    ghost_mat,
    work,
    halo_r,
    halo_e,
    mat_us,
    mat_ur,
    mat_ds,
    mat_dr,
    up_s,
    up_r,
    down_s,
    down_r,
    ev_s,
    ev_r,
    ev_t,
    side_s,
    side_r,
    first_s,
    first_r,
    first_own,
    s_up,
    r_up,
    s_down,
    r_down,
    s_ev,
    r_ev,
    s_pair,
    r_pair,
):
    me = lax.axis_index("mesh")
    event = lax.axis_index("event")
    has_up = me > 0
    has_down = me < n_mesh - 1

    barrier = pltpu.get_barrier_semaphore()

    @pl.when(has_up)
    def _():
        pl.semaphore_signal(barrier, inc=1, device_id={"mesh": me - 1})

    @pl.when(has_down)
    def _():
        pl.semaphore_signal(barrier, inc=1, device_id={"mesh": me + 1})

    for hop in range(1, n_event):
        pl.semaphore_signal(
            barrier, inc=1, device_id={"event": lax.rem(event + hop, n_event)}
        )

    paired = n_event == 2
    has_side = jnp.where(event == 0, me, n_mesh - 1 - me) > 0
    side_device = {"event": 1 - event, "mesh": me - 1 + 2 * event}
    if paired:

        @pl.when(has_side)
        def _():
            pl.semaphore_signal(barrier, inc=1, device_id=side_device)

    loads = []
    pairs = (
        (rows_hbm, rows_ref),
        (lam_hbm, lam_ref),
        (mu_hbm, mu_ref),
        (rho_hbm, rho_ref),
        (cube_hbm, cube_ref),
        (now_hbm, now_ref),
        (before_hbm, before_ref),
        (adj_hbm, adj_ref),
        (after_hbm, after_ref),
        (spread_hbm, spread_ref),
        (dy_hbm, dy_ref),
        (rec_elem_hbm, rec_elem_ref),
        (rec_off_hbm, rec_off_ref),
        (data_hbm, data_ref),
        (gather_hbm, gather_ref),
        (off_hbm, off_ref),
        (force_hbm, force_ref),
    )
    for place, (source, target) in enumerate(pairs):
        load_copy = pltpu.make_async_copy(source, target, s_in.at[place])
        load_copy.start()
        loads.append(load_copy)

    def up_copy(source, target, slot):
        return pltpu.make_async_remote_copy(
            src_ref=source, dst_ref=target, send_sem=s_up.at[slot],
            recv_sem=r_up.at[slot], device_id={"mesh": me - 1},
        )

    def down_copy(source, target, slot):
        return pltpu.make_async_remote_copy(
            src_ref=source, dst_ref=target, send_sem=s_down.at[slot],
            recv_sem=r_down.at[slot], device_id={"mesh": me + 1},
        )

    n_face = 6
    mat_slot = n_face
    halo_slot = n_face + 1

    def start_both(up, down):
        @pl.when(has_up)
        def _():
            up.start()

        @pl.when(has_down)
        def _():
            down.start()

    def wait_both(up, down):
        @pl.when(has_down)
        def _():
            up.wait_recv()

        @pl.when(has_up)
        def _():
            down.wait_recv()

    @pl.when(jnp.logical_not(has_down))
    def _():
        halo_r[...] = jnp.zeros_like(halo_r)
        up_r[...] = jnp.zeros_like(up_r)
        mat_ur[...] = jnp.zeros_like(mat_ur)

    if paired:

        @pl.when(jnp.logical_not(has_side))
        def _():
            side_r[...] = jnp.zeros_like(side_r)

    @pl.when(jnp.logical_not(has_up))
    def _():
        down_r[...] = jnp.zeros_like(down_r)
        mat_dr[...] = jnp.zeros_like(mat_dr)

    pl.semaphore_wait(
        barrier,
        jnp.where(has_up, 1, 0)
        + jnp.where(has_down, 1, 0)
        + (n_event - 1)
        + (jnp.where(has_side, 1, 0) if paired else 0),
    )
    tops = (now_hbm, before_hbm, adj_hbm, after_hbm)

    def halo_copy(index):
        return up_copy(
            tops[index].at[0, :, 0], halo_r.at[index], halo_slot + index
        )

    @pl.when(has_up)
    def _():
        for index in range(4):
            halo_copy(index).start()

    low4 = low_lanes(4)

    for place in range(5):
        loads[place].wait()
    materials = jnp.concatenate([lam_ref[...], mu_ref[...], rho_ref[...]], axis=1)
    moved = move_left(rows_ref[...], materials)
    cube = cube_ref[...]

    def modulus(which):
        value = moved[:, which * LANES : (which + 1) * LANES].reshape(5, 5, 8, LANES)
        turned = jnp.stack([value[4 - a] for a in range(5)], axis=0)
        return pick(low4, value, turned) * cube

    lam_value = modulus(0)
    mu_value = modulus(1)
    clam[...] = lam_value
    cmu[...] = mu_value
    mass = modulus(2)
    mass = [assemble_xy(mass[a : a + 1])[0] for a in range(5)]
    mass[4] = mass[4] + swap_half(mass[4])

    def set_minv(a, value):
        keep = sub_iota(3) < 5
        if a == 0:
            keep = keep & (low_lanes(3) | has_down)
        keep = jnp.broadcast_to(keep, value.shape)
        safe = jnp.where(keep, value, 1.0)
        minv[a] = jnp.where(keep, time_step**2 / safe, 0.0)

    for a in range(1, 5):
        set_minv(a, mass[a])

    squares = [float(DERIV[q, 0]) ** 2 for q in range(5)]
    diag_mu = mix(squares[1:], [mu_value[q] for q in range(1, 5)])
    diag_lam = mix(squares[1:], [lam_value[q] for q in range(1, 5)])
    diag_lam = diag_lam + (diag_mu + diag_mu)
    listed = [mass[0][c] for c in range(4)]
    for value in (lam_value[0], mu_value[0], diag_mu, diag_lam):
        listed += [value[c] for c in range(5)]
    for pair in range(12):
        up, down = pack(listed[2 * pair], listed[2 * pair + 1])
        mat_us[pair] = up
        mat_ds[pair] = down

    start_both(up_copy(mat_us, mat_ur, mat_slot), down_copy(mat_ds, mat_dr, mat_slot))

    for place in range(5, 11):
        loads[place].wait()
    inputs = (now_ref, before_ref, adj_ref, after_ref)

    def bring_in(index):
        ref = inputs[index]
        upper = ref[0, :, 0:5]
        lower = mirror(
            jnp.stack(
                [jnp.zeros((3, 8, LANES), jnp.float32)]
                + [ref[0, :, 8 - a] for a in range(1, 5)],
                axis=1,
            )
        )
        parts = []
        for layer in (upper, lower):
            for shifted in (layer, roll_sub(layer)):
                parts.append(shifted.reshape(120, LANES))
        moved = move_right(jnp.concatenate(parts, axis=1), spread_ref[...])
        for c in range(4):
            fields[index, :, :, c] = moved[:, c * LANES : (c + 1) * LANES].reshape(
                3, 5, 8, LANES
            )
        fields[index, :, :, 4] = from_right(
            moved[:, 0:LANES].reshape(3, 5, 8, LANES)
        )

    def bring_halos():
        @pl.when(has_down)
        def _():
            for index in range(4):
                halo_copy(index).wait_recv()

        planes = jnp.stack([halo_r[:, 0], halo_r[:, 1], -halo_r[:, 2]], axis=1)
        parts = [
            planes.reshape(96, LANES),
            roll_sub(planes).reshape(96, LANES),
        ]
        moved = move_right(
            jnp.concatenate(parts, axis=1), spread_ref[2 * LANES : 4 * LANES]
        )
        for c in range(5):
            part = moved[:, (c % 4) * LANES : (c % 4 + 1) * LANES]
            part = part.reshape(4, 3, 8, LANES)
            if c == 4:
                part = from_right(part)
            halo_e[:, :, c] = part
            fields[0:3, :, 0, c] = fields[0:3, :, 0, c] + part[0:3]

    def owned(ndim):
        return jnp.where(lane_iota(ndim) < HALF, 0, 1) == event

    def side_copy():
        return pltpu.make_async_remote_copy(
            src_ref=side_s, dst_ref=side_r, send_sem=s_pair.at[0],
            recv_sem=r_pair.at[0], device_id=side_device,
        )

    def first_copy():
        return pltpu.make_async_remote_copy(
            src_ref=first_s, dst_ref=first_r, send_sem=s_pair.at[1],
            recv_sem=r_pair.at[1], device_id={"event": 1 - event},
        )

    def send_first():
        if not paired:
            return
        mine = owned(3)
        for a in range(5):
            first_own[:, a] = fields[1, :, a]
            for pair in range(2):
                first = fields[1, :, a, 2 * pair]
                second = fields[1, :, a, 2 * pair + 1]
                first_s[:, a, pair] = pick(mine, swap_half(second), first)
        first_copy().start()

    def take_first():
        first_copy().wait_recv()
        mine = owned(3)
        for a in range(5):
            for pair in range(2):
                packed = first_r[:, a, pair]
                for c, other in ((2 * pair, swap_half(packed)), (2 * pair + 1, packed)):
                    value = pick(mine, first_own[:, a, c], other)
                    fields[4, :, a, c] = value
                    if c == 0:
                        fields[4, :, a, 4] = from_right(value)
        for a in range(5):
            strain = strain_at(4, a)
            for i in range(6):
                strains[2, a, i] = strain[i]

    def send_side(slot):
        if not paired:
            return
        side_s[...] = jnp.where(event == 0, up_s[slot], down_s[slot])

        @pl.when(has_side)
        def _():
            side_copy().start()

    def paired_delta(own):
        @pl.when(has_side)
        def _():
            side_copy().wait_recv()

        sides = []
        for pair in range(2):
            packed = side_r[:, pair]
            turned = swap_half(packed)
            sides += [
                jnp.where(event == 0, turned, packed),
                jnp.where(event == 0, packed, turned),
            ]
        sides.append(from_right(sides[0]))
        other = mirror(jnp.stack(sides, axis=1))
        mine = owned(3)
        scale = pick(mine, minv[0], swap_half(minv[0]))
        return pick(owned(4), own, -scale * other)

    def along_y(value, flipped=False):
        total = None
        for k in range(5):
            row = jnp.broadcast_to(value[..., k : k + 1, :], value.shape)
            term = dy_ref[1 if flipped else 0, k] * row
            total = term if total is None else total + term
        return total

    def send(slot, value):
        for pair in range(2):
            up, down = pack(value[:, 2 * pair], value[:, 2 * pair + 1])
            up_s[slot, :, pair] = up
            down_s[slot, :, pair] = down
        start_both(
            up_copy(up_s.at[slot], up_r.at[slot], slot),
            down_copy(down_s.at[slot], down_r.at[slot], slot),
        )

    def receive(slot):
        wait_both(
            up_copy(up_s.at[slot], up_r.at[slot], slot),
            down_copy(down_s.at[slot], down_r.at[slot], slot),
        )
        sides = []
        for pair in range(2):
            sides += unpack(down_r[slot, :, pair], up_r[slot, :, pair])
        sides.append(from_right(sides[0]))
        return mirror(jnp.stack(sides, axis=1))

    def along_z(index, comp, a, first=0):
        return mix(
            DERIV[a, first:], [fields[index, comp, k] for k in range(first, 5)]
        )

    def strain_at(index, a):
        u = [fields[index, comp, a] for comp in range(3)]
        gz = [along_z(index, comp, a) for comp in range(3)]
        return (
            along_x(u[0]),
            along_y(u[1]),
            gz[2],
            along_y(u[0]) + along_x(u[1]),
            gz[0] + along_x(u[2]),
            gz[1] + along_y(u[2]),
        )

    def set_ghost():
        u = [delta[comp] for comp in range(3)]
        gz = [-EDGE * value for value in u]
        lam_g, mu_g = ghost_mat[0], ghost_mat[1]
        xx = along_x(u[0])
        yy = along_y(u[1])
        zz = gz[2]
        side = lam_g * (xx + yy + zz)
        mu_two = mu_g + mu_g
        xx = side + mu_two * xx
        yy = side + mu_two * yy
        zz = side + mu_two * zz
        xy = mu_g * (along_y(u[0]) + along_x(u[1]))
        xz = mu_g * (gz[0] + along_x(u[2]))
        yz = mu_g * (gz[1] + along_y(u[2]))
        work[0] = xy
        work[1] = yy
        work[2] = yz
        values = (
            along_x(xx, True)
            + along_y(work[0], True)
            - EDGE * xz
            + ghost_mat[2] * u[0],
            along_x(xy, True)
            + along_y(work[1], True)
            - EDGE * yz
            + ghost_mat[2] * u[1],
            along_x(xz, True)
            + along_y(work[2], True)
            - EDGE * zz
            + ghost_mat[3] * u[2],
        )
        ghost[...] = assemble_xy(jnp.stack(values, axis=0))

    def put_stress(target, a, strain, add):
        lam_div = clam[a] * (strain[0] + strain[1] + strain[2])
        mu_a = cmu[a]
        mu_two = mu_a + mu_a
        for i in range(3):
            value = lam_div + mu_two * strain[i]
            target[i, a] = target[i, a] + value if add else value
            value = mu_a * strain[3 + i]
            target[3 + i, a] = target[3 + i, a] + value if add else value

    def make_stress(index, target, keep_strain):
        for a in range(5):
            strain = strain_at(index, a)
            put_stress(target, a, strain, False)
            if keep_strain is not None:
                for i in range(6):
                    keep_strain[a, i] = strain[i]

    def face_strain():
        u = [delta[comp] for comp in range(3)]
        return (
            along_x(u[0]),
            along_y(u[1]),
            EDGE * u[2],
            along_y(u[0]) + along_x(u[1]),
            EDGE * u[0] + along_x(u[2]),
            EDGE * u[1] + along_y(u[2]),
        )

    def add_face(target, keep_strain):
        strain = face_strain()
        put_stress(target, 0, strain, True)
        if keep_strain is not None:
            for i in range(6):
                keep_strain[0, i] = keep_strain[0, i] + strain[i]
        for q in range(1, 5):
            gz = [float(DERIV[q, 0]) * delta[comp] for comp in range(3)]
            mu_q = cmu[q]
            side = clam[q] * gz[2]
            target[0, q] = target[0, q] + side
            target[1, q] = target[1, q] + side
            target[2, q] = target[2, q] + (side + (mu_q + mu_q) * gz[2])
            target[4, q] = target[4, q] + mu_q * gz[0]
            target[5, q] = target[5, q] + mu_q * gz[1]
            if keep_strain is not None:
                keep_strain[q, 2] = keep_strain[q, 2] + gz[2]
                keep_strain[q, 4] = keep_strain[q, 4] + gz[0]
                keep_strain[q, 5] = keep_strain[q, 5] + gz[1]

    pairs_of = ((0, 3, 4), (3, 1, 5), (4, 5, 2))

    def both_layers(value):
        return value + mirror(swap_half(value))

    def plane_force(source, a):
        values = []
        for comp in range(3):
            ix, iy, iz = pairs_of[comp]
            total = along_x(source[ix, a], True) + along_y(source[iy, a], True)
            values.append(total + mix(DERIV[:, a], [source[iz, q] for q in range(5)]))
        value = assemble_xy(jnp.stack(values, axis=0))
        return both_layers(value) if a == 4 else value

    def advance(index, older, a, value, load):
        if load is not None:
            value = value - load(a)
        fields[older, :, a] = (
            2.0 * fields[index, :, a] - fields[older, :, a]
        ) - minv[a] * value

    def inside_planes(index, older, source, load):
        for a in range(1, 5):
            advance(index, older, a, plane_force(source, a), load)

    def close_step(index, older, source, slot, load):
        inside_planes(index, older, source, load)
        close_outer(index, older, source, slot, load)

    def close_outer(index, older, source, slot, load):
        value = plane_force(source, 0) + ghost[...]
        advance(index, older, 0, value + receive(slot), load)

    def open_step(index, older, slot, load):
        held[...] = plane_force(stress, 0)
        send(slot, held[...])
        if slot == 4:
            send_side(slot)
        inside_planes(index, older, stress, load)
        advance(index, older, 0, held[...], load)

    def add_correction(which):
        strain = face_strain()
        for a in range(5):
            other = [strains[which, a, i] for i in range(6)]
            div_f = other[0] + other[1] + other[2]
            if a == 0:
                lam_part = (strain[0] + strain[1] + strain[2]) * div_f
                mu_part = (
                    strain[0] * other[0] + strain[1] * other[1] + strain[2] * other[2]
                ) + 0.5 * (
                    strain[3] * other[3] + strain[4] * other[4] + strain[5] * other[5]
                )
            else:
                gz = [float(DERIV[a, 0]) * delta[comp] for comp in range(3)]
                lam_part = gz[2] * div_f
                mu_part = gz[2] * other[2] + 0.5 * (gz[0] * other[4] + gz[1] * other[5])
            if which == 2:
                lam_part = lam_part + swap_half(lam_part)
                mu_part = mu_part + swap_half(mu_part)
            ksum[0, a] = ksum[0, a] + lam_part
            ksum[1, a] = ksum[1, a] + mu_part

    def close_face(older, slot, keep_strain):
        delta[...] = -minv[0] * receive(slot)
        fields[older, :, 0] = fields[older, :, 0] + delta[...]
        add_face(stress, keep_strain)

    bring_in(0)
    make_stress(0, stress, None)
    send(0, plane_force(stress, 0))
    bring_in(2)
    make_stress(2, stress_a, astrains.at[2])
    send(1, plane_force(stress_a, 0))
    bring_in(1)
    for place in range(15, 17):
        loads[place].wait()
    src_local = elem_ref[0] - LANES * me
    src_depth = off_ref[0, 0]
    src_in = (src_local >= 0) & (src_local < LANES)
    src_over = (src_local >= -HALF) & (src_local < 0) & (src_depth == 4)
    src_under = (src_local >= LANES) & (src_local < LANES + HALF) & (src_depth == 0)
    src_lane = jnp.where(
        src_in,
        src_local,
        jnp.where(
            src_over, src_local + HALF, jnp.where(src_under, src_local - HALF, -1)
        ),
    )
    src_depth = jnp.where(
        src_in, jnp.where(src_local < HALF, src_depth, 4 - src_depth), 0
    )
    src_row = src_depth * 40 + off_ref[0, 2] * 8 + off_ref[0, 1]

    shape = (5, 8, LANES)
    src_lanes = lax.broadcasted_iota(jnp.int32, shape, 2) == src_lane
    src_rows = lax.broadcasted_iota(jnp.int32, shape, 0) * 8 + lax.broadcasted_iota(
        jnp.int32, shape, 1
    )
    for a in range(5):
        source_at = jnp.where(src_lanes & (src_rows + 40 * a == src_row), 1.0, 0.0)
        value = assemble_xy(source_at[None])[0]
        source_map[a] = value + swap_half(value) if a == 4 else value

    def make_maps():
        for place in range(11, 14):
            loads[place].wait()
        nrec = rec_elem_ref.shape[1]
        local = rec_elem_ref[...] - LANES * me
        depth = rec_off_ref[0]
        in_slab = (local >= 0) & (local < LANES)
        over = (local >= -HALF) & (local < 0) & (depth == 4)
        under = (local >= LANES) & (local < LANES + HALF) & (depth == 0)
        rec_at = jnp.where(
            in_slab,
            local,
            jnp.where(over, local + HALF, jnp.where(under, local - HALF, -1)),
        )
        depth = jnp.where(
            in_slab, jnp.where(local < HALF, depth, 4 - depth), jnp.zeros_like(depth)
        )
        across, along = rec_off_ref[1], rec_off_ref[2]
        lane_list, row_list, sign_list = [], [], []
        for move in range(8):
            present, at, y_row, x_row = rec_at >= 0, rec_at, across, along
            if move & 1:
                present = present & ((along == 0) | (along == 4))
                near = at & 31
                at = at - near + (jnp.where(along == 0, near + 31, near + 1) & 31)
                x_row = 4 - along
            if move & 2:
                present = present & ((across == 0) | (across == 4))
                at = at ^ 32
                y_row = 4 - across
            if move & 4:
                present = present & (depth == 4)
                at = at ^ HALF
            lane_list.append(jnp.where(present, at, -1))
            row_list.append(depth * 40 + x_row * 8 + y_row)
            sign_list.append(jnp.where(at < HALF, 1.0, -1.0))
        copies = 8 * nrec
        lane_at = jnp.concatenate(lane_list, axis=1)
        row_at = jnp.concatenate(row_list, axis=1)
        sign_at = jnp.concatenate(sign_list, axis=1)
        rows_hot = lax.broadcasted_iota(jnp.int32, (200, copies), 0) == row_at
        rows_hot = jnp.where(rows_hot, 1.0, 0.0).astype(jnp.bfloat16)
        lanes_hot = lax.broadcasted_iota(jnp.int32, (LANES, copies), 0) == lane_at
        lanes_hot = jnp.where(lanes_hot, 1.0, 0.0).astype(jnp.bfloat16)

        def spread_out(operand):
            return lax.dot_general(
                rows_hot,
                operand,
                (((1,), (1,)), ((), ())),
                preferred_element_type=jnp.float32,
            )

        counts = spread_out(lanes_hot)
        for a in range(5):
            count_map[a] = adjoint_gain * counts[40 * a : 40 * a + 40].reshape(shape)
        for moment in range(steps):
            for comp in range(3):
                seen = jnp.concatenate([data_ref[moment, comp]] * 8, axis=1)
                seen = adjoint_gain * seen
                if comp == 2:
                    seen = seen * sign_at
                found = sum(
                    spread_out(
                        lanes_hot * jnp.broadcast_to(part, (LANES, copies))
                    )
                    for part in split2(seen)
                )
                for a in range(5):
                    data_map[moment, comp, a] = found[40 * a : 40 * a + 40].reshape(
                        shape
                    )

    def source_load(moment):
        forces = [force_ref[moment, 0, comp] for comp in range(3)]
        lane = lax.broadcasted_iota(jnp.int32, (8, LANES), 1)
        forces[2] = jnp.where(lane < HALF, forces[2], -forces[2])
        return lambda a: jnp.stack(
            [source_map[a] * forces[comp] for comp in range(3)], axis=0
        )

    def receiver_load(index, moment):
        return (
            lambda a: count_map[a][None] * fields[index, :, a] - data_map[moment, :, a]
        )

    bring_halos()
    delta[...] = halo_e[0]
    add_face(stress, None)
    inside_planes(0, 1, stress, source_load(0))

    wait_both(up_copy(mat_us, mat_ur, mat_slot), down_copy(mat_ds, mat_dr, mat_slot))
    listed = []
    for pair in range(12):
        listed += unpack(mat_dr[pair], mat_ur[pair])
    for which in range(4):
        for c in range(5):
            ghost_mat[which, c] = listed[4 + 5 * which + c]
    face_mass = listed[0:4]
    set_minv(0, mass[0] + jnp.stack(face_mass + [from_right(face_mass[0])], axis=0))

    def ghost_of_start(index):
        top = fields[index, :, 0]
        delta[...] = pick(low4, top, jnp.zeros_like(top))
        set_ghost()

    ghost_of_start(0)
    close_outer(0, 1, stress, 0, source_load(0))

    make_stress(1, stress, strains.at[0])
    open_step(1, 0, 2, source_load(1))
    make_stress(0, stress, strains.at[1])
    send(3, plane_force(stress, 0))

    send_first()
    make_maps()
    bring_in(3)
    fields[3, :, 0] = fields[3, :, 0] + halo_e[3]
    delta[...] = halo_e[2]
    add_face(stress_a, astrains.at[2])
    ghost_of_start(2)
    close_step(2, 3, stress_a, 1, None)
    load = receiver_load(1, 0)
    for a in range(5):
        first_load[:, a] = load(a)
        fields[3, :, a] = fields[3, :, a] - minv[a] * data_map[2, :, a]
    delta[...] = -minv[0] * held[...]
    set_ghost()

    close_face(0, 2, strains.at[1])
    close_step(0, 1, stress, 3, source_load(2))

    for a in range(5):
        fields[3, :, a] = fields[3, :, a] + minv[a] * (
            count_map[a][None] * fields[1, :, a]
        )
    make_stress(3, stress, astrains.at[1])
    open_step(3, 2, 4, receiver_load(0, 1))
    make_stress(2, stress, astrains.at[0])

    def put_out(index, ref):
        sides = []
        for c in range(4):
            upper = fields[index, :, 0:4, c]
            lower = mirror(
                jnp.stack([fields[index, :, 4 - i, c] for i in range(4)], axis=1)
            )
            sides.append(pick(low4, upper, lower).reshape(96, LANES))
        moved = move_right(jnp.concatenate(sides, axis=1), gather_ref[...])
        for ez in range(2):
            first = moved[:, 2 * ez * LANES : (2 * ez + 1) * LANES]
            second = moved[:, (2 * ez + 1) * LANES : (2 * ez + 2) * LANES]
            first = first.reshape(3, 4, 8, LANES)
            second = roll_sub(second.reshape(3, 4, 8, LANES))
            ref[0, :, 4 * ez : 4 * ez + 4] = pick(sub_iota(4) < 4, first, second)

    def add_kernels(adjoint, other_at, first):
        for a in range(5):
            strain = [adjoint[a, i] for i in range(6)]
            other = other_at(a)
            div_a = strain[0] + strain[1] + strain[2]
            div_f = other[0] + other[1] + other[2]
            diag = strain[0] * other[0] + strain[1] * other[1] + strain[2] * other[2]
            shear = strain[3] * other[3] + strain[4] * other[4] + strain[5] * other[5]
            lam_part = div_a * div_f
            mu_part = diag + 0.5 * shear
            if not first:
                lam_part = ksum[0, a] + lam_part
                mu_part = ksum[1, a] + mu_part
            ksum[0, a] = lam_part
            ksum[1, a] = mu_part

    def kept(which):
        return lambda a: [strains[which, a, i] for i in range(6)]

    width = LANES // n_event

    def event_copy(hop, which):
        target = lax.rem(event + hop, n_event)
        return pltpu.make_async_remote_copy(
            src_ref=ev_s.at[which, pl.ds(pl.multiple_of(width * target, width), width)],
            dst_ref=ev_r.at[hop - 1, which],
            send_sem=s_ev.at[2 * hop - 2 + which],
            recv_sem=r_ev.at[2 * hop - 2 + which],
            device_id={"event": target},
        )

    def natural_kernel(which, target):
        scale, modulus_ref = ((-time_step, lam_ref), (-2.0 * time_step, mu_ref))[which]
        value = ksum[which]
        turned_back = jnp.stack([value[4 - a] for a in range(5)], axis=0)
        value = pick(low4, value, turned_back).reshape(200, LANES)
        natural = move_left_t(rows_ref[...], value)
        target[which] = jnp.transpose(natural * (scale * modulus_ref[...]))

    def send_kernels():
        for which in range(2):
            natural_kernel(which, ev_s)
            for hop in range(1, n_event):
                event_copy(hop, which).start()

    send(5, plane_force(stress, 0))

    add_kernels(astrains.at[2], lambda a: strain_at(1, a), True)
    add_kernels(astrains.at[1], kept(1), False)
    add_kernels(astrains.at[0], kept(0), False)
    if paired:
        send_kernels()

    delta[...] = -minv[0] * held[...]
    set_ghost()
    if paired:
        take_first()
    loads[14].wait()
    put_out(1, final_f_ref)

    close_face(2, 4, None)
    if paired:
        delta[...] = paired_delta(delta[...])
        add_correction(2)
        for which in range(2):
            natural_kernel(which, ev_t)
    else:
        add_correction(0)
        send_kernels()
    close_step(2, 3, stress, 5, lambda a: first_load[:, a])
    put_out(3, final_a_ref)

    mine = pl.ds(pl.multiple_of(width * event, width), width)
    total = ev_t[:, mine] if paired else ev_s[:, mine]
    for hop in range(1, n_event):
        for which in range(2):
            event_copy(hop, which).wait_recv()
        total = total + ev_r[hop - 1]
    out_ref[...] = total

    @pl.when(has_up)
    def _():
        for index in range(4):
            halo_copy(index).wait_send()
        up_copy(mat_us, mat_ur, mat_slot).wait_send()
        for slot in range(n_face):
            up_copy(up_s.at[slot], up_r.at[slot], slot).wait_send()

    @pl.when(has_down)
    def _():
        down_copy(mat_ds, mat_dr, mat_slot).wait_send()
        for slot in range(n_face):
            down_copy(down_s.at[slot], down_r.at[slot], slot).wait_send()

    for hop in range(1, n_event):
        for which in range(2):
            event_copy(hop, which).wait_send()

    if paired:
        first_copy().wait_send()

        @pl.when(has_side)
        def _():
            side_copy().wait_send()


def write_out(first, second, third, first_out, second_out, third_out, sems):
    copies = [
        pltpu.make_async_copy(source, target, sems.at[place])
        for place, (source, target) in enumerate(
            ((first, first_out), (second, second_out), (third, third_out))
        )
    ]
    for copy in copies:
        copy.start()
    for copy in copies:
        copy.wait()


def on_device(
    n_mesh,
    n_event,
    forward_before,
    forward_now,
    adjoint_after,
    adjoint_now,
    mass_density,
    lame_lambda,
    lame_mu,
    source_element,
    source_offset,
    source_force,
    receiver_element,
    receiver_offset,
    receiver_data,
):
    assert forward_now.shape[1:] == (3, 8, 8, 128)
    assert lame_mu.shape == (125, 128)
    steps = source_force.shape[1]
    assert steps == 3
    field = forward_now.shape
    vmem = pl.BlockSpec(memory_space=pltpu.VMEM)
    hbm = pl.BlockSpec(memory_space=pltpu.HBM)
    f32 = jnp.float32
    elem = (5, 5, 8, LANES)
    faces = (6, 3, 2, 8, LANES)
    copied = (
        forward_now,
        forward_before,
        adjoint_now,
        adjoint_after,
        mass_density,
        lame_lambda,
        lame_mu,
        receiver_element,
        receiver_offset.transpose(2, 0, 1),
        receiver_data.transpose(1, 3, 0, 2),
    ) + constants()
    small = (source_offset, source_force.transpose(1, 0, 2))
    results = pl.pallas_call(
        functools.partial(kernel, n_mesh, n_event, steps),
        out_shape=(
            pltpu.VMEM(field, f32),
            pltpu.VMEM(field, f32),
            pltpu.VMEM((2, LANES // n_event, 125), f32),
        ),
        in_specs=[hbm] * 17 + [pl.BlockSpec(memory_space=pltpu.SMEM)],
        out_specs=(vmem, vmem, vmem),
        scratch_shapes=[pltpu.VMEM(value.shape, value.dtype) for value in copied]
        + [pltpu.SMEM(value.shape, value.dtype) for value in small]
        + [
            pltpu.SemaphoreType.DMA((len(copied) + len(small),)),
            pltpu.VMEM((5, 3) + elem, f32),
            pltpu.VMEM((6,) + elem, f32),
            pltpu.VMEM((6,) + elem, f32),
            pltpu.VMEM((3,) + elem[1:], f32),
            pltpu.VMEM((3,) + elem[1:], f32),
            pltpu.VMEM((3,) + elem[1:], f32),
            pltpu.VMEM(elem, f32),
            pltpu.VMEM((steps, 3) + elem, f32),
            pltpu.VMEM(elem, f32),
            pltpu.VMEM((3,) + elem, f32),
            pltpu.VMEM((3, 5, 6, 5, 8, LANES), f32),
            pltpu.VMEM((3, 5, 6, 5, 8, LANES), f32),
            pltpu.VMEM((2,) + elem, f32),
            pltpu.VMEM(elem, f32),
            pltpu.VMEM(elem, f32),
            pltpu.VMEM(elem, f32),
            pltpu.VMEM((4,) + elem[1:], f32),
            pltpu.VMEM((3,) + elem[1:], f32),
            pltpu.VMEM((4, 3, 8, LANES), f32),
            pltpu.VMEM((4, 3) + elem[1:], f32),
            pltpu.VMEM((12, 8, LANES), f32),
            pltpu.VMEM((12, 8, LANES), f32),
            pltpu.VMEM((12, 8, LANES), f32),
            pltpu.VMEM((12, 8, LANES), f32),
            pltpu.VMEM(faces, f32),
            pltpu.VMEM(faces, f32),
            pltpu.VMEM(faces, f32),
            pltpu.VMEM(faces, f32),
            pltpu.VMEM((2, LANES, 125), f32),
            pltpu.VMEM((max(1, n_event - 1), 2, LANES // n_event, 125), f32),
            pltpu.VMEM((2, LANES, 125), f32),
            pltpu.VMEM((3, 2, 8, LANES), f32),
            pltpu.VMEM((3, 2, 8, LANES), f32),
            pltpu.VMEM((3, 5, 2, 8, LANES), f32),
            pltpu.VMEM((3, 5, 2, 8, LANES), f32),
            pltpu.VMEM((3,) + elem, f32),
            pltpu.SemaphoreType.DMA((11,)),
            pltpu.SemaphoreType.DMA((11,)),
            pltpu.SemaphoreType.DMA((7,)),
            pltpu.SemaphoreType.DMA((7,)),
            pltpu.SemaphoreType.DMA((max(2, 2 * n_event - 2),)),
            pltpu.SemaphoreType.DMA((max(2, 2 * n_event - 2),)),
            pltpu.SemaphoreType.DMA((2,)),
            pltpu.SemaphoreType.DMA((2,)),
        ],
        compiler_params=pltpu.CompilerParams(
            collective_id=0, has_side_effects=True, vmem_limit_bytes=32 * 1024 * 1024
        ),
    )(
        *(
            pltpu.with_memory_space_constraint(value, pltpu.HBM)
            for value in copied + small
        ),
        source_element,
    )
    final_f, final_a, kernels = pl.pallas_call(
        write_out,
        out_shape=tuple(
            jax.ShapeDtypeStruct(value.shape, value.dtype) for value in results
        ),
        in_specs=[vmem] * 3,
        out_specs=(hbm, hbm, hbm),
        scratch_shapes=[pltpu.SemaphoreType.DMA((3,))],
    )(*(pltpu.with_memory_space_constraint(value, pltpu.VMEM) for value in results))
    return (final_f, final_a, kernels.transpose(0, 2, 1))


def solution(mesh):
    return jax.shard_map(
        functools.partial(on_device, mesh.shape["mesh"], mesh.shape["event"]),
        mesh=mesh,
        in_specs=(
            P("event", None, "mesh", None, None),
            P("event", None, "mesh", None, None),
            P("event", None, "mesh", None, None),
            P("event", None, "mesh", None, None),
            P(None, "mesh"),
            P(None, "mesh"),
            P(None, "mesh"),
            P("event"),
            P("event", None),
            P("event", None, None),
            P("event", None),
            P("event", None, None),
            P("event", None, None, None),
        ),
        out_specs=(
            P("event", None, "mesh", None, None),
            P("event", None, "mesh", None, None),
            P(None, None, ("mesh", "event")),
        ),
        check_vma=False,
    )
```

```python
import functools
import math

import jax
import jax.numpy as jnp
import numpy as np
from jax import lax
from jax.experimental import pallas as pl
from jax.experimental.pallas import tpu as pltpu
from jax.sharding import PartitionSpec as P

time_step = 0.04
adjoint_gain = 25.0
LANES = 128


def numpy_tables():
    gll_points = np.array([-1.0, -math.sqrt(3.0 / 7.0), 0.0, math.sqrt(3.0 / 7.0), 1.0])
    legendre = (35.0 * gll_points**4 - 30.0 * gll_points**2 + 3.0) / 8.0
    deriv_table = np.zeros((5, 5))
    for row_q in range(5):
        for col_k in range(5):
            if row_q != col_k:
                deriv_table[row_q, col_k] = legendre[row_q] / (
                    legendre[col_k] * (gll_points[row_q] - gll_points[col_k])
                )
    deriv_table[0, 0] = -5.0
    deriv_table[4, 4] = 5.0
    gll_weights = np.array([0.1, 49.0 / 90.0, 32.0 / 45.0, 49.0 / 90.0, 0.1])
    return (deriv_table, gll_weights)


DERIV, WEIGHTS = numpy_tables()


def constants():
    spread = np.zeros((4, LANES, 4, 4, 32), np.float32)
    for j in range(4):
        for ex in range(32):
            for c in range(4):
                spread[j, 4 * ex + c, c, j, ex] = 1.0
    spread = spread.reshape(512, 512)
    rows = np.zeros((5, 5, 8, 125), np.float32)
    cube = np.zeros((5, 5, 8, LANES), np.float32)
    for a in range(5):
        for b in range(5):
            for c in range(5):
                rows[a, c, b, (a * 5 + b) * 5 + c] = 1.0
                cube[a, c, b, :] = WEIGHTS[a] * WEIGHTS[b] * WEIGHTS[c]
    rows = rows.reshape(200, 125)
    dy = np.zeros((2, 5, 8, LANES), np.float32)
    for k in range(5):
        for b in range(5):
            dy[0, k, b, :] = DERIV[b, k]
            dy[1, k, b, :] = DERIV[k, b]
    bf = jnp.bfloat16
    return (
        jnp.asarray(spread, bf),
        jnp.asarray(np.ascontiguousarray(spread.T), bf),
        jnp.asarray(rows, bf),
        jnp.asarray(cube),
        jnp.asarray(dy),
    )


def split2(value):
    high = value.astype(jnp.bfloat16)
    return (high, (value - high.astype(jnp.float32)).astype(jnp.bfloat16))


def dot(left, right):
    return jnp.dot(left, right, preferred_element_type=jnp.float32)


def move_right(values, table):
    parts = split2(values)
    count = values.shape[0]
    stacked = jnp.concatenate(parts, axis=0)
    moved = dot(stacked, table)
    return moved[0:count] + moved[count : 2 * count]


def move_left(table, values):
    return sum(dot(table, part) for part in split2(values))


def move_left_t(table, values):
    contract = (((0,), (0,)), ((), ()))
    return sum(
        lax.dot_general(table, part, contract, preferred_element_type=jnp.float32)
        for part in split2(values)
    )


def roll_lane(value, shift):
    return pltpu.roll(value, shift % LANES, value.ndim - 1)


def lane_iota(ndim):
    return lax.broadcasted_iota(jnp.int32, (1,) * (ndim - 1) + (LANES,), ndim - 1)


def sub_iota(ndim):
    return lax.broadcasted_iota(jnp.int32, (1,) * (ndim - 2) + (8, LANES), ndim - 2)


def pick(mask, first, second):
    return jnp.where(jnp.broadcast_to(mask, first.shape), first, second)


def from_left(value):
    at_edge = lane_iota(value.ndim) % 32 == 0
    return pick(at_edge, roll_lane(value, -31), roll_lane(value, 1))


def from_right(value):
    at_edge = lane_iota(value.ndim) % 32 == 31
    return pick(at_edge, roll_lane(value, 31), roll_lane(value, -1))


def roll_sub(value):
    return pltpu.roll(value, 4, value.ndim - 2)


def assemble_xy(value):
    first = value[:, 0:1] + from_left(value[:, 4:5])
    value = jnp.concatenate([first, value[:, 1:4], from_right(first)], axis=1)
    swapped = roll_sub(value)
    other = pick(
        lane_iota(4) % 64 < 32, roll_lane(swapped, -32), roll_lane(swapped, 32)
    )
    return value + pick(sub_iota(4) % 4 == 0, other, jnp.zeros_like(other))


EDGE = float(DERIV[0, 0])
HALF = 64


def mix(coefs, planes):
    total = None
    for coef, plane in zip(coefs, planes):
        if coef != 0.0:
            term = float(coef) * plane
            total = term if total is None else total + term
    return total


def along_x(value, flipped=False):
    table = DERIV.T if flipped else DERIV
    even = [value[k] + value[4 - k] for k in range(2)] + [value[2]]
    odd = [value[k] - value[4 - k] for k in range(2)]
    sums = []
    diffs = []
    for c in range(2):
        sums.append(mix([0.5 * (table[c, k] - table[c, 4 - k]) for k in range(2)], odd))
        diffs.append(
            mix(
                [0.5 * (table[c, k] + table[c, 4 - k]) for k in range(2)]
                + [table[c, 2]],
                even,
            )
        )
    rows = [sums[c] + diffs[c] for c in range(2)]
    rows.append(mix(table[2, 0:2], odd))
    rows += [sums[c] - diffs[c] for c in (1, 0)]
    return jnp.stack(rows, axis=0)


def mirror(value):
    return jnp.concatenate([value[0:2], -value[2:3]], axis=0)


def low_lanes(ndim):
    return lane_iota(ndim) < HALF


def swap_half(value):
    return roll_lane(value, HALF)


def unpack(from_above, from_below):
    low = low_lanes(from_above.ndim)
    return (
        pick(low, from_above, swap_half(from_below)),
        pick(low, swap_half(from_above), from_below),
    )


def pack(first, second):
    low = low_lanes(first.ndim)
    return (
        pick(low, first, swap_half(second)),
        pick(low, swap_half(first), second),
    )


def kernel(
    n_mesh,
    n_event,
    steps,
    now_hbm,
    before_hbm,
    adj_hbm,
    after_hbm,
    rho_hbm,
    lam_hbm,
    mu_hbm,
    rec_elem_hbm,
    rec_off_hbm,
    data_hbm,
    spread_hbm,
    gather_hbm,
    rows_hbm,
    cube_hbm,
    dy_hbm,
    off_hbm,
    force_hbm,
    elem_ref,
    final_f_ref,
    final_a_ref,
    out_ref,
    now_ref,
    before_ref,
    adj_ref,
    after_ref,
    rho_ref,
    lam_ref,
    mu_ref,
    rec_elem_ref,
    rec_off_ref,
    data_ref,
    spread_ref,
    gather_ref,
    rows_ref,
    cube_ref,
    dy_ref,
    off_ref,
    force_ref,
    s_in,
    fields,
    stress,
    stress_a,
    held,
    ghost,
    delta,
    count_map,
    data_map,
    source_map,
    first_load,
    strains,
    astrains,
    ksum,
    clam,
    cmu,
    minv,
    ghost_mat,
    work,
    halo_r,
    halo_e,
    mat_us,
    mat_ur,
    mat_ds,
    mat_dr,
    up_s,
    up_r,
    down_s,
    down_r,
    ev_s,
    ev_r,
    ev_t,
    side_s,
    side_r,
    first_s,
    first_r,
    first_own,
    s_up,
    r_up,
    s_down,
    r_down,
    s_ev,
    r_ev,
    s_pair,
    r_pair,
):
    me = lax.axis_index("mesh")
    event = lax.axis_index("event")
    has_up = me > 0
    has_down = me < n_mesh - 1

    barrier = pltpu.get_barrier_semaphore()

    @pl.when(has_up)
    def _():
        pl.semaphore_signal(barrier, inc=1, device_id={"mesh": me - 1})

    @pl.when(has_down)
    def _():
        pl.semaphore_signal(barrier, inc=1, device_id={"mesh": me + 1})

    for hop in range(1, n_event):
        pl.semaphore_signal(
            barrier, inc=1, device_id={"event": lax.rem(event + hop, n_event)}
        )

    paired = n_event == 2
    has_side = jnp.where(event == 0, me, n_mesh - 1 - me) > 0
    side_device = {"event": 1 - event, "mesh": me - 1 + 2 * event}
    if paired:

        @pl.when(has_side)
        def _():
            pl.semaphore_signal(barrier, inc=1, device_id=side_device)

    loads = []
    pairs = (
        (rows_hbm, rows_ref),
        (lam_hbm, lam_ref),
        (mu_hbm, mu_ref),
        (rho_hbm, rho_ref),
        (cube_hbm, cube_ref),
        (now_hbm, now_ref),
        (before_hbm, before_ref),
        (adj_hbm, adj_ref),
        (after_hbm, after_ref),
        (spread_hbm, spread_ref),
        (dy_hbm, dy_ref),
        (rec_elem_hbm, rec_elem_ref),
        (rec_off_hbm, rec_off_ref),
        (data_hbm, data_ref),
        (gather_hbm, gather_ref),
        (off_hbm, off_ref),
        (force_hbm, force_ref),
    )
    for place, (source, target) in enumerate(pairs):
        load_copy = pltpu.make_async_copy(source, target, s_in.at[place])
        load_copy.start()
        loads.append(load_copy)

    def up_copy(source, target, slot):
        return pltpu.make_async_remote_copy(
            src_ref=source, dst_ref=target, send_sem=s_up.at[slot],
            recv_sem=r_up.at[slot], device_id={"mesh": me - 1},
        )

    def down_copy(source, target, slot):
        return pltpu.make_async_remote_copy(
            src_ref=source, dst_ref=target, send_sem=s_down.at[slot],
            recv_sem=r_down.at[slot], device_id={"mesh": me + 1},
        )

    n_face = 6
    mat_slot = n_face
    halo_slot = n_face + 1

    def start_both(up, down):
        @pl.when(has_up)
        def _():
            up.start()

        @pl.when(has_down)
        def _():
            down.start()

    def wait_both(up, down):
        @pl.when(has_down)
        def _():
            up.wait_recv()

        @pl.when(has_up)
        def _():
            down.wait_recv()

    @pl.when(jnp.logical_not(has_down))
    def _():
        halo_r[...] = jnp.zeros_like(halo_r)
        up_r[...] = jnp.zeros_like(up_r)
        mat_ur[...] = jnp.zeros_like(mat_ur)

    if paired:

        @pl.when(jnp.logical_not(has_side))
        def _():
            side_r[...] = jnp.zeros_like(side_r)

    @pl.when(jnp.logical_not(has_up))
    def _():
        down_r[...] = jnp.zeros_like(down_r)
        mat_dr[...] = jnp.zeros_like(mat_dr)

    pl.semaphore_wait(
        barrier,
        jnp.where(has_up, 1, 0)
        + jnp.where(has_down, 1, 0)
        + (n_event - 1)
        + (jnp.where(has_side, 1, 0) if paired else 0),
    )
    tops = (now_hbm, before_hbm, adj_hbm, after_hbm)

    def halo_copy(index):
        return up_copy(
            tops[index].at[0, :, 0], halo_r.at[index], halo_slot + index
        )

    @pl.when(has_up)
    def _():
        for index in range(4):
            halo_copy(index).start()

    low4 = low_lanes(4)

    for place in range(5):
        loads[place].wait()
    materials = jnp.concatenate([lam_ref[...], mu_ref[...], rho_ref[...]], axis=1)
    moved = move_left(rows_ref[...], materials)
    cube = cube_ref[...]

    def modulus(which):
        value = moved[:, which * LANES : (which + 1) * LANES].reshape(5, 5, 8, LANES)
        turned = jnp.stack([value[4 - a] for a in range(5)], axis=0)
        return pick(low4, value, turned) * cube

    lam_value = modulus(0)
    mu_value = modulus(1)
    clam[...] = lam_value
    cmu[...] = mu_value
    mass = modulus(2)
    mass = [assemble_xy(mass[a : a + 1])[0] for a in range(5)]
    mass[4] = mass[4] + swap_half(mass[4])

    def set_minv(a, value):
        keep = sub_iota(3) < 5
        if a == 0:
            keep = keep & (low_lanes(3) | has_down)
        keep = jnp.broadcast_to(keep, value.shape)
        safe = jnp.where(keep, value, 1.0)
        minv[a] = jnp.where(keep, time_step**2 / safe, 0.0)

    for a in range(1, 5):
        set_minv(a, mass[a])

    squares = [float(DERIV[q, 0]) ** 2 for q in range(5)]
    diag_mu = mix(squares[1:], [mu_value[q] for q in range(1, 5)])
    diag_lam = mix(squares[1:], [lam_value[q] for q in range(1, 5)])
    diag_lam = diag_lam + (diag_mu + diag_mu)
    listed = [mass[0][c] for c in range(4)]
    for value in (lam_value[0], mu_value[0], diag_mu, diag_lam):
        listed += [value[c] for c in range(5)]
    for pair in range(12):
        up, down = pack(listed[2 * pair], listed[2 * pair + 1])
        mat_us[pair] = up
        mat_ds[pair] = down

    start_both(up_copy(mat_us, mat_ur, mat_slot), down_copy(mat_ds, mat_dr, mat_slot))

    for place in (5, 6, 7, 8, 9, 10, 15, 16):
        loads[place].wait()
    inputs = (now_ref, before_ref, adj_ref, after_ref)

    def bring_in(index):
        ref = inputs[index]
        upper = ref[0, :, 0:5]
        lower = mirror(
            jnp.stack(
                [jnp.zeros((3, 8, LANES), jnp.float32)]
                + [ref[0, :, 8 - a] for a in range(1, 5)],
                axis=1,
            )
        )
        parts = []
        for layer in (upper, lower):
            for shifted in (layer, roll_sub(layer)):
                parts.append(shifted.reshape(120, LANES))
        moved = move_right(jnp.concatenate(parts, axis=1), spread_ref[...])
        for c in range(4):
            fields[index, :, :, c] = moved[:, c * LANES : (c + 1) * LANES].reshape(
                3, 5, 8, LANES
            )
        fields[index, :, :, 4] = from_right(
            moved[:, 0:LANES].reshape(3, 5, 8, LANES)
        )

    def bring_halos():
        @pl.when(has_down)
        def _():
            for index in range(4):
                halo_copy(index).wait_recv()

        planes = jnp.stack([halo_r[:, 0], halo_r[:, 1], -halo_r[:, 2]], axis=1)
        parts = [
            planes.reshape(96, LANES),
            roll_sub(planes).reshape(96, LANES),
        ]
        moved = move_right(
            jnp.concatenate(parts, axis=1), spread_ref[2 * LANES : 4 * LANES]
        )
        for c in range(5):
            part = moved[:, (c % 4) * LANES : (c % 4 + 1) * LANES]
            part = part.reshape(4, 3, 8, LANES)
            if c == 4:
                part = from_right(part)
            halo_e[:, :, c] = part
            fields[0:3, :, 0, c] = fields[0:3, :, 0, c] + part[0:3]

    def owned(ndim):
        return jnp.where(lane_iota(ndim) < HALF, 0, 1) == event

    def side_copy():
        return pltpu.make_async_remote_copy(
            src_ref=side_s, dst_ref=side_r, send_sem=s_pair.at[0],
            recv_sem=r_pair.at[0], device_id=side_device,
        )

    def first_copy():
        return pltpu.make_async_remote_copy(
            src_ref=first_s, dst_ref=first_r, send_sem=s_pair.at[1],
            recv_sem=r_pair.at[1], device_id={"event": 1 - event},
        )

    def send_first():
        if not paired:
            return
        mine = owned(3)
        for a in range(5):
            first_own[:, a] = fields[1, :, a]
            for pair in range(2):
                first = fields[1, :, a, 2 * pair]
                second = fields[1, :, a, 2 * pair + 1]
                first_s[:, a, pair] = pick(mine, swap_half(second), first)
        first_copy().start()

    def take_first():
        first_copy().wait_recv()
        mine = owned(3)
        for a in range(5):
            for pair in range(2):
                packed = first_r[:, a, pair]
                for c, other in ((2 * pair, swap_half(packed)), (2 * pair + 1, packed)):
                    value = pick(mine, first_own[:, a, c], other)
                    fields[4, :, a, c] = value
                    if c == 0:
                        fields[4, :, a, 4] = from_right(value)
        for a in range(5):
            strain = strain_at(4, a)
            for i in range(6):
                strains[2, a, i] = strain[i]

    def send_side(slot):
        if not paired:
            return
        side_s[...] = jnp.where(event == 0, up_s[slot], down_s[slot])

        @pl.when(has_side)
        def _():
            side_copy().start()

    def paired_delta(own):
        @pl.when(has_side)
        def _():
            side_copy().wait_recv()

        sides = []
        for pair in range(2):
            packed = side_r[:, pair]
            turned = swap_half(packed)
            sides += [
                jnp.where(event == 0, turned, packed),
                jnp.where(event == 0, packed, turned),
            ]
        sides.append(from_right(sides[0]))
        other = mirror(jnp.stack(sides, axis=1))
        mine = owned(3)
        scale = pick(mine, minv[0], swap_half(minv[0]))
        return pick(owned(4), own, -scale * other)

    def along_y(value, flipped=False):
        total = None
        for k in range(5):
            row = jnp.broadcast_to(value[..., k : k + 1, :], value.shape)
            term = dy_ref[1 if flipped else 0, k] * row
            total = term if total is None else total + term
        return total

    def send(slot, value):
        for pair in range(2):
            up, down = pack(value[:, 2 * pair], value[:, 2 * pair + 1])
            up_s[slot, :, pair] = up
            down_s[slot, :, pair] = down
        start_both(
            up_copy(up_s.at[slot], up_r.at[slot], slot),
            down_copy(down_s.at[slot], down_r.at[slot], slot),
        )

    def receive(slot):
        wait_both(
            up_copy(up_s.at[slot], up_r.at[slot], slot),
            down_copy(down_s.at[slot], down_r.at[slot], slot),
        )
        sides = []
        for pair in range(2):
            sides += unpack(down_r[slot, :, pair], up_r[slot, :, pair])
        sides.append(from_right(sides[0]))
        return mirror(jnp.stack(sides, axis=1))

    def along_z(index, comp, a, first=0):
        return mix(
            DERIV[a, first:], [fields[index, comp, k] for k in range(first, 5)]
        )

    def strain_at(index, a):
        u = [fields[index, comp, a] for comp in range(3)]
        gz = [along_z(index, comp, a) for comp in range(3)]
        return (
            along_x(u[0]),
            along_y(u[1]),
            gz[2],
            along_y(u[0]) + along_x(u[1]),
            gz[0] + along_x(u[2]),
            gz[1] + along_y(u[2]),
        )

    def set_ghost():
        u = [delta[comp] for comp in range(3)]
        gz = [-EDGE * value for value in u]
        lam_g, mu_g = ghost_mat[0], ghost_mat[1]
        xx = along_x(u[0])
        yy = along_y(u[1])
        zz = gz[2]
        side = lam_g * (xx + yy + zz)
        mu_two = mu_g + mu_g
        xx = side + mu_two * xx
        yy = side + mu_two * yy
        zz = side + mu_two * zz
        xy = mu_g * (along_y(u[0]) + along_x(u[1]))
        xz = mu_g * (gz[0] + along_x(u[2]))
        yz = mu_g * (gz[1] + along_y(u[2]))
        work[0] = xy
        work[1] = yy
        work[2] = yz
        values = (
            along_x(xx, True)
            + along_y(work[0], True)
            - EDGE * xz
            + ghost_mat[2] * u[0],
            along_x(xy, True)
            + along_y(work[1], True)
            - EDGE * yz
            + ghost_mat[2] * u[1],
            along_x(xz, True)
            + along_y(work[2], True)
            - EDGE * zz
            + ghost_mat[3] * u[2],
        )
        ghost[...] = assemble_xy(jnp.stack(values, axis=0))

    def put_stress(target, a, strain, add):
        lam_div = clam[a] * (strain[0] + strain[1] + strain[2])
        mu_a = cmu[a]
        mu_two = mu_a + mu_a
        for i in range(3):
            value = lam_div + mu_two * strain[i]
            target[i, a] = target[i, a] + value if add else value
            value = mu_a * strain[3 + i]
            target[3 + i, a] = target[3 + i, a] + value if add else value

    def make_stress(index, target, keep_strain):
        for a in range(5):
            strain = strain_at(index, a)
            put_stress(target, a, strain, False)
            if keep_strain is not None:
                for i in range(6):
                    keep_strain[a, i] = strain[i]

    def face_strain():
        u = [delta[comp] for comp in range(3)]
        return (
            along_x(u[0]),
            along_y(u[1]),
            EDGE * u[2],
            along_y(u[0]) + along_x(u[1]),
            EDGE * u[0] + along_x(u[2]),
            EDGE * u[1] + along_y(u[2]),
        )

    def add_face(target, keep_strain):
        strain = face_strain()
        put_stress(target, 0, strain, True)
        if keep_strain is not None:
            for i in range(6):
                keep_strain[0, i] = keep_strain[0, i] + strain[i]
        for q in range(1, 5):
            gz = [float(DERIV[q, 0]) * delta[comp] for comp in range(3)]
            mu_q = cmu[q]
            side = clam[q] * gz[2]
            target[0, q] = target[0, q] + side
            target[1, q] = target[1, q] + side
            target[2, q] = target[2, q] + (side + (mu_q + mu_q) * gz[2])
            target[4, q] = target[4, q] + mu_q * gz[0]
            target[5, q] = target[5, q] + mu_q * gz[1]
            if keep_strain is not None:
                keep_strain[q, 2] = keep_strain[q, 2] + gz[2]
                keep_strain[q, 4] = keep_strain[q, 4] + gz[0]
                keep_strain[q, 5] = keep_strain[q, 5] + gz[1]

    pairs_of = ((0, 3, 4), (3, 1, 5), (4, 5, 2))

    def both_layers(value):
        return value + mirror(swap_half(value))

    def plane_force(source, a):
        values = []
        for comp in range(3):
            ix, iy, iz = pairs_of[comp]
            total = along_x(source[ix, a], True) + along_y(source[iy, a], True)
            values.append(total + mix(DERIV[:, a], [source[iz, q] for q in range(5)]))
        value = assemble_xy(jnp.stack(values, axis=0))
        return both_layers(value) if a == 4 else value

    def advance(index, older, a, value, load):
        if load is not None:
            value = value - load(a)
        fields[older, :, a] = (
            2.0 * fields[index, :, a] - fields[older, :, a]
        ) - minv[a] * value

    def inside_planes(index, older, source, load):
        for a in range(1, 5):
            advance(index, older, a, plane_force(source, a), load)

    def close_step(index, older, source, slot, load):
        inside_planes(index, older, source, load)
        close_outer(index, older, source, slot, load)

    def close_outer(index, older, source, slot, load):
        value = plane_force(source, 0) + ghost[...]
        advance(index, older, 0, value + receive(slot), load)

    def open_step(index, older, slot, load):
        held[...] = plane_force(stress, 0)
        send(slot, held[...])
        if slot == 4:
            send_side(slot)
        inside_planes(index, older, stress, load)
        advance(index, older, 0, held[...], load)

    def add_correction(which):
        strain = face_strain()
        for a in range(5):
            other = [strains[which, a, i] for i in range(6)]
            div_f = other[0] + other[1] + other[2]
            if a == 0:
                lam_part = (strain[0] + strain[1] + strain[2]) * div_f
                mu_part = (
                    strain[0] * other[0] + strain[1] * other[1] + strain[2] * other[2]
                ) + 0.5 * (
                    strain[3] * other[3] + strain[4] * other[4] + strain[5] * other[5]
                )
            else:
                gz = [float(DERIV[a, 0]) * delta[comp] for comp in range(3)]
                lam_part = gz[2] * div_f
                mu_part = gz[2] * other[2] + 0.5 * (gz[0] * other[4] + gz[1] * other[5])
            if which == 2:
                lam_part = lam_part + swap_half(lam_part)
                mu_part = mu_part + swap_half(mu_part)
            ksum[0, a] = ksum[0, a] + lam_part
            ksum[1, a] = ksum[1, a] + mu_part

    def close_face(older, slot, keep_strain):
        delta[...] = -minv[0] * receive(slot)
        fields[older, :, 0] = fields[older, :, 0] + delta[...]
        add_face(stress, keep_strain)

    bring_in(0)
    make_stress(0, stress, None)
    send(0, plane_force(stress, 0))
    bring_in(2)
    make_stress(2, stress_a, astrains.at[2])
    send(1, plane_force(stress_a, 0))
    bring_in(1)
    src_local = elem_ref[0] - LANES * me
    src_depth = off_ref[0, 0]
    src_in = (src_local >= 0) & (src_local < LANES)
    src_over = (src_local >= -HALF) & (src_local < 0) & (src_depth == 4)
    src_under = (src_local >= LANES) & (src_local < LANES + HALF) & (src_depth == 0)
    src_lane = jnp.where(
        src_in,
        src_local,
        jnp.where(
            src_over, src_local + HALF, jnp.where(src_under, src_local - HALF, -1)
        ),
    )
    src_depth = jnp.where(
        src_in, jnp.where(src_local < HALF, src_depth, 4 - src_depth), 0
    )
    src_row = src_depth * 40 + off_ref[0, 2] * 8 + off_ref[0, 1]

    shape = (5, 8, LANES)
    src_lanes = lax.broadcasted_iota(jnp.int32, shape, 2) == src_lane
    src_rows = lax.broadcasted_iota(jnp.int32, shape, 0) * 8 + lax.broadcasted_iota(
        jnp.int32, shape, 1
    )
    for a in range(5):
        source_at = jnp.where(src_lanes & (src_rows + 40 * a == src_row), 1.0, 0.0)
        value = assemble_xy(source_at[None])[0]
        source_map[a] = value + swap_half(value) if a == 4 else value

    def make_maps():
        nrec = rec_elem_ref.shape[1]
        local = rec_elem_ref[...] - LANES * me
        depth = rec_off_ref[0]
        in_slab = (local >= 0) & (local < LANES)
        over = (local >= -HALF) & (local < 0) & (depth == 4)
        under = (local >= LANES) & (local < LANES + HALF) & (depth == 0)
        rec_at = jnp.where(
            in_slab,
            local,
            jnp.where(over, local + HALF, jnp.where(under, local - HALF, -1)),
        )
        depth = jnp.where(
            in_slab, jnp.where(local < HALF, depth, 4 - depth), jnp.zeros_like(depth)
        )
        across, along = rec_off_ref[1], rec_off_ref[2]
        lane_list, row_list, sign_list = [], [], []
        for move in range(8):
            present, at, y_row, x_row = rec_at >= 0, rec_at, across, along
            if move & 1:
                present = present & ((along == 0) | (along == 4))
                near = at & 31
                at = at - near + (jnp.where(along == 0, near + 31, near + 1) & 31)
                x_row = 4 - along
            if move & 2:
                present = present & ((across == 0) | (across == 4))
                at = at ^ 32
                y_row = 4 - across
            if move & 4:
                present = present & (depth == 4)
                at = at ^ HALF
            lane_list.append(jnp.where(present, at, -1))
            row_list.append(depth * 40 + x_row * 8 + y_row)
            sign_list.append(jnp.where(at < HALF, 1.0, -1.0))
        copies = 8 * nrec
        lane_at = jnp.concatenate(lane_list, axis=1)
        row_at = jnp.concatenate(row_list, axis=1)
        sign_at = jnp.concatenate(sign_list, axis=1)
        rows_hot = lax.broadcasted_iota(jnp.int32, (200, copies), 0) == row_at
        rows_hot = jnp.where(rows_hot, 1.0, 0.0).astype(jnp.bfloat16)
        lanes_hot = lax.broadcasted_iota(jnp.int32, (LANES, copies), 0) == lane_at
        lanes_hot = jnp.where(lanes_hot, 1.0, 0.0).astype(jnp.bfloat16)

        def spread_out(operand):
            return lax.dot_general(
                rows_hot,
                operand,
                (((1,), (1,)), ((), ())),
                preferred_element_type=jnp.float32,
            )

        counts = spread_out(lanes_hot)
        for a in range(5):
            count_map[a] = adjoint_gain * counts[40 * a : 40 * a + 40].reshape(shape)
        for moment in range(steps):
            for comp in range(3):
                seen = jnp.concatenate([data_ref[moment, comp]] * 8, axis=1)
                seen = adjoint_gain * seen
                if comp == 2:
                    seen = seen * sign_at
                found = sum(
                    spread_out(
                        lanes_hot * jnp.broadcast_to(part, (LANES, copies))
                    )
                    for part in split2(seen)
                )
                for a in range(5):
                    data_map[moment, comp, a] = found[40 * a : 40 * a + 40].reshape(
                        shape
                    )

    def source_load(moment):
        forces = [force_ref[moment, 0, comp] for comp in range(3)]
        lane = lax.broadcasted_iota(jnp.int32, (8, LANES), 1)
        forces[2] = jnp.where(lane < HALF, forces[2], -forces[2])
        return lambda a: jnp.stack(
            [source_map[a] * forces[comp] for comp in range(3)], axis=0
        )

    def receiver_load(index, moment):
        return (
            lambda a: count_map[a][None] * fields[index, :, a] - data_map[moment, :, a]
        )

    for place in range(11, 15):
        loads[place].wait()
    bring_halos()
    delta[...] = halo_e[0]
    add_face(stress, None)
    inside_planes(0, 1, stress, source_load(0))

    wait_both(up_copy(mat_us, mat_ur, mat_slot), down_copy(mat_ds, mat_dr, mat_slot))
    listed = []
    for pair in range(12):
        listed += unpack(mat_dr[pair], mat_ur[pair])
    for which in range(4):
        for c in range(5):
            ghost_mat[which, c] = listed[4 + 5 * which + c]
    face_mass = listed[0:4]
    set_minv(0, mass[0] + jnp.stack(face_mass + [from_right(face_mass[0])], axis=0))

    def ghost_of_start(index):
        top = fields[index, :, 0]
        delta[...] = pick(low4, top, jnp.zeros_like(top))
        set_ghost()

    ghost_of_start(0)
    close_outer(0, 1, stress, 0, source_load(0))

    make_stress(1, stress, strains.at[0])
    open_step(1, 0, 2, source_load(1))
    make_stress(0, stress, strains.at[1])
    send(3, plane_force(stress, 0))

    send_first()
    make_maps()
    bring_in(3)
    fields[3, :, 0] = fields[3, :, 0] + halo_e[3]
    delta[...] = halo_e[2]
    add_face(stress_a, astrains.at[2])
    ghost_of_start(2)
    close_step(2, 3, stress_a, 1, None)
    load = receiver_load(1, 0)
    for a in range(5):
        first_load[:, a] = load(a)
        fields[3, :, a] = fields[3, :, a] - minv[a] * data_map[2, :, a]
    delta[...] = -minv[0] * held[...]
    set_ghost()

    close_face(0, 2, strains.at[1])
    close_step(0, 1, stress, 3, source_load(2))

    for a in range(5):
        fields[3, :, a] = fields[3, :, a] + minv[a] * (
            count_map[a][None] * fields[1, :, a]
        )
    make_stress(3, stress, astrains.at[1])
    open_step(3, 2, 4, receiver_load(0, 1))
    make_stress(2, stress, astrains.at[0])

    def put_out(index, ref):
        sides = []
        for c in range(4):
            upper = fields[index, :, 0:4, c]
            lower = mirror(
                jnp.stack([fields[index, :, 4 - i, c] for i in range(4)], axis=1)
            )
            sides.append(pick(low4, upper, lower).reshape(96, LANES))
        moved = move_right(jnp.concatenate(sides, axis=1), gather_ref[...])
        for ez in range(2):
            first = moved[:, 2 * ez * LANES : (2 * ez + 1) * LANES]
            second = moved[:, (2 * ez + 1) * LANES : (2 * ez + 2) * LANES]
            first = first.reshape(3, 4, 8, LANES)
            second = roll_sub(second.reshape(3, 4, 8, LANES))
            ref[0, :, 4 * ez : 4 * ez + 4] = pick(sub_iota(4) < 4, first, second)

    def add_kernels(adjoint, other_at, first):
        for a in range(5):
            strain = [adjoint[a, i] for i in range(6)]
            other = other_at(a)
            div_a = strain[0] + strain[1] + strain[2]
            div_f = other[0] + other[1] + other[2]
            diag = strain[0] * other[0] + strain[1] * other[1] + strain[2] * other[2]
            shear = strain[3] * other[3] + strain[4] * other[4] + strain[5] * other[5]
            lam_part = div_a * div_f
            mu_part = diag + 0.5 * shear
            if not first:
                lam_part = ksum[0, a] + lam_part
                mu_part = ksum[1, a] + mu_part
            ksum[0, a] = lam_part
            ksum[1, a] = mu_part

    def kept(which):
        return lambda a: [strains[which, a, i] for i in range(6)]

    width = LANES // n_event

    def event_copy(hop, which):
        target = lax.rem(event + hop, n_event)
        return pltpu.make_async_remote_copy(
            src_ref=ev_s.at[which, pl.ds(pl.multiple_of(width * target, width), width)],
            dst_ref=ev_r.at[hop - 1, which],
            send_sem=s_ev.at[2 * hop - 2 + which],
            recv_sem=r_ev.at[2 * hop - 2 + which],
            device_id={"event": target},
        )

    def natural_kernel(which, target):
        scale, modulus_ref = ((-time_step, lam_ref), (-2.0 * time_step, mu_ref))[which]
        value = ksum[which]
        turned_back = jnp.stack([value[4 - a] for a in range(5)], axis=0)
        value = pick(low4, value, turned_back).reshape(200, LANES)
        natural = move_left_t(rows_ref[...], value)
        target[which] = jnp.transpose(natural * (scale * modulus_ref[...]))

    def send_kernels():
        for which in range(2):
            natural_kernel(which, ev_s)
            for hop in range(1, n_event):
                event_copy(hop, which).start()

    send(5, plane_force(stress, 0))

    add_kernels(astrains.at[2], lambda a: strain_at(1, a), True)
    add_kernels(astrains.at[1], kept(1), False)
    add_kernels(astrains.at[0], kept(0), False)
    if paired:
        send_kernels()

    delta[...] = -minv[0] * held[...]
    set_ghost()
    if paired:
        take_first()
    put_out(1, final_f_ref)

    close_face(2, 4, None)
    if paired:
        delta[...] = paired_delta(delta[...])
        add_correction(2)
        for which in range(2):
            natural_kernel(which, ev_t)
    else:
        add_correction(0)
        send_kernels()
    close_step(2, 3, stress, 5, lambda a: first_load[:, a])
    put_out(3, final_a_ref)

    mine = pl.ds(pl.multiple_of(width * event, width), width)
    total = ev_t[:, mine] if paired else ev_s[:, mine]
    for hop in range(1, n_event):
        for which in range(2):
            event_copy(hop, which).wait_recv()
        total = total + ev_r[hop - 1]
    out_ref[...] = total

    @pl.when(has_up)
    def _():
        for index in range(4):
            halo_copy(index).wait_send()
        up_copy(mat_us, mat_ur, mat_slot).wait_send()
        for slot in range(n_face):
            up_copy(up_s.at[slot], up_r.at[slot], slot).wait_send()

    @pl.when(has_down)
    def _():
        down_copy(mat_ds, mat_dr, mat_slot).wait_send()
        for slot in range(n_face):
            down_copy(down_s.at[slot], down_r.at[slot], slot).wait_send()

    for hop in range(1, n_event):
        for which in range(2):
            event_copy(hop, which).wait_send()

    if paired:
        first_copy().wait_send()

        @pl.when(has_side)
        def _():
            side_copy().wait_send()


def write_out(first, second, third, first_out, second_out, third_out, sems):
    copies = [
        pltpu.make_async_copy(source, target, sems.at[place])
        for place, (source, target) in enumerate(
            ((first, first_out), (second, second_out), (third, third_out))
        )
    ]
    for copy in copies:
        copy.start()
    for copy in copies:
        copy.wait()


def on_device(
    n_mesh,
    n_event,
    forward_before,
    forward_now,
    adjoint_after,
    adjoint_now,
    mass_density,
    lame_lambda,
    lame_mu,
    source_element,
    source_offset,
    source_force,
    receiver_element,
    receiver_offset,
    receiver_data,
):
    assert forward_now.shape[1:] == (3, 8, 8, 128)
    assert lame_mu.shape == (125, 128)
    steps = source_force.shape[1]
    assert steps == 3
    field = forward_now.shape
    vmem = pl.BlockSpec(memory_space=pltpu.VMEM)
    hbm = pl.BlockSpec(memory_space=pltpu.HBM)
    f32 = jnp.float32
    elem = (5, 5, 8, LANES)
    faces = (6, 3, 2, 8, LANES)
    copied = (
        forward_now,
        forward_before,
        adjoint_now,
        adjoint_after,
        mass_density,
        lame_lambda,
        lame_mu,
        receiver_element,
        receiver_offset.transpose(2, 0, 1),
        receiver_data.transpose(1, 3, 0, 2),
    ) + constants()
    small = (source_offset, source_force.transpose(1, 0, 2))
    results = pl.pallas_call(
        functools.partial(kernel, n_mesh, n_event, steps),
        out_shape=(
            pltpu.VMEM(field, f32),
            pltpu.VMEM(field, f32),
            pltpu.VMEM((2, LANES // n_event, 125), f32),
        ),
        in_specs=[hbm] * 17 + [pl.BlockSpec(memory_space=pltpu.SMEM)],
        out_specs=(vmem, vmem, vmem),
        scratch_shapes=[pltpu.VMEM(value.shape, value.dtype) for value in copied]
        + [pltpu.SMEM(value.shape, value.dtype) for value in small]
        + [
            pltpu.SemaphoreType.DMA((len(copied) + len(small),)),
            pltpu.VMEM((5, 3) + elem, f32),
            pltpu.VMEM((6,) + elem, f32),
            pltpu.VMEM((6,) + elem, f32),
            pltpu.VMEM((3,) + elem[1:], f32),
            pltpu.VMEM((3,) + elem[1:], f32),
            pltpu.VMEM((3,) + elem[1:], f32),
            pltpu.VMEM(elem, f32),
            pltpu.VMEM((steps, 3) + elem, f32),
            pltpu.VMEM(elem, f32),
            pltpu.VMEM((3,) + elem, f32),
            pltpu.VMEM((3, 5, 6, 5, 8, LANES), f32),
            pltpu.VMEM((3, 5, 6, 5, 8, LANES), f32),
            pltpu.VMEM((2,) + elem, f32),
            pltpu.VMEM(elem, f32),
            pltpu.VMEM(elem, f32),
            pltpu.VMEM(elem, f32),
            pltpu.VMEM((4,) + elem[1:], f32),
            pltpu.VMEM((3,) + elem[1:], f32),
            pltpu.VMEM((4, 3, 8, LANES), f32),
            pltpu.VMEM((4, 3) + elem[1:], f32),
            pltpu.VMEM((12, 8, LANES), f32),
            pltpu.VMEM((12, 8, LANES), f32),
            pltpu.VMEM((12, 8, LANES), f32),
            pltpu.VMEM((12, 8, LANES), f32),
            pltpu.VMEM(faces, f32),
            pltpu.VMEM(faces, f32),
            pltpu.VMEM(faces, f32),
            pltpu.VMEM(faces, f32),
            pltpu.VMEM((2, LANES, 125), f32),
            pltpu.VMEM((max(1, n_event - 1), 2, LANES // n_event, 125), f32),
            pltpu.VMEM((2, LANES, 125), f32),
            pltpu.VMEM((3, 2, 8, LANES), f32),
            pltpu.VMEM((3, 2, 8, LANES), f32),
            pltpu.VMEM((3, 5, 2, 8, LANES), f32),
            pltpu.VMEM((3, 5, 2, 8, LANES), f32),
            pltpu.VMEM((3,) + elem, f32),
            pltpu.SemaphoreType.DMA((11,)),
            pltpu.SemaphoreType.DMA((11,)),
            pltpu.SemaphoreType.DMA((7,)),
            pltpu.SemaphoreType.DMA((7,)),
            pltpu.SemaphoreType.DMA((max(2, 2 * n_event - 2),)),
            pltpu.SemaphoreType.DMA((max(2, 2 * n_event - 2),)),
            pltpu.SemaphoreType.DMA((2,)),
            pltpu.SemaphoreType.DMA((2,)),
        ],
        compiler_params=pltpu.CompilerParams(
            collective_id=0, has_side_effects=True, vmem_limit_bytes=32 * 1024 * 1024
        ),
    )(
        *(
            pltpu.with_memory_space_constraint(value, pltpu.HBM)
            for value in copied + small
        ),
        source_element,
    )
    final_f, final_a, kernels = pl.pallas_call(
        write_out,
        out_shape=tuple(
            jax.ShapeDtypeStruct(value.shape, value.dtype) for value in results
        ),
        in_specs=[vmem] * 3,
        out_specs=(hbm, hbm, hbm),
        scratch_shapes=[pltpu.SemaphoreType.DMA((3,))],
    )(*(pltpu.with_memory_space_constraint(value, pltpu.VMEM) for value in results))
    return (final_f, final_a, kernels.transpose(0, 2, 1))


def solution(mesh):
    return jax.shard_map(
        functools.partial(on_device, mesh.shape["mesh"], mesh.shape["event"]),
        mesh=mesh,
        in_specs=(
            P("event", None, "mesh", None, None),
            P("event", None, "mesh", None, None),
            P("event", None, "mesh", None, None),
            P("event", None, "mesh", None, None),
            P(None, "mesh"),
            P(None, "mesh"),
            P(None, "mesh"),
            P("event"),
            P("event", None),
            P("event", None, None),
            P("event", None),
            P("event", None, None),
            P("event", None, None, None),
        ),
        out_specs=(
            P("event", None, "mesh", None, None),
            P("event", None, "mesh", None, None),
            P(None, None, ("mesh", "event")),
        ),
        check_vma=False,
    )
```
